32 devices in a mesh: section: 2 (over core), ctx: 4 (over y, x), dp: 4 (over z).
Axes of the slice: x: 2, y: 2, z: 4, core: 2. Of those that a mesh axis runs over, the one named last changes fastest.
Arguments:
- block_input: float32 [2, 4, 512, 960], P(None, 'dp', 'ctx'), may hold values from -6 to 6
- out_grad: float32 [2, 4, 512, 960], P(None, 'dp', 'ctx'), may hold values from -6 to 6
- w_query: bfloat16 [2, 960, 960], P('section', 'dp'), may hold values from -0.1875 to 0.1875
- w_key: bfloat16 [2, 960, 320], P('section', 'dp'), may hold values from -0.1875 to 0.1875
- w_value: bfloat16 [2, 960, 320], P('section', 'dp'), may hold values from -0.1875 to 0.1875
- w_out: bfloat16 [2, 960, 960], P('section', 'dp'), may hold values from -1.5 to 1.5
- norm_attn: bfloat16 [2, 960], P('section', 'dp'), may hold values from 0.099609375 to 1.8984375
- w_gate: bfloat16 [2, 960, 2560], P('section', None, 'dp'), may hold values from -0.1875 to 0.1875
- w_up: bfloat16 [2, 960, 2560], P('section', None, 'dp'), may hold values from -0.1875 to 0.1875
- w_down: bfloat16 [2, 2560, 960], P('section', 'dp'), may hold values from -0.125 to 0.125
- norm_ffn: bfloat16 [2, 960], P('section', 'dp'), may hold values from 0.099609375 to 1.8984375
Outputs:
- section_out: float32 [2, 2, 4, 512, 960], P('section', None, 'dp', 'ctx')
- section_in_grad: float32 [2, 2, 4, 512, 960], P('section', None, 'dp', 'ctx')
- grad_query: float32 [2, 960, 960], P('section', 'dp')
- grad_key: float32 [2, 960, 320], P('section', 'dp')
- grad_value: float32 [2, 960, 320], P('section', 'dp')
- grad_out: float32 [2, 960, 960], P('section', 'dp')
- grad_norm_attn: float32 [2, 960], P('section', 'dp')
- grad_gate: float32 [2, 960, 2560], P('section', None, 'dp')
- grad_up: float32 [2, 960, 2560], P('section', None, 'dp')
- grad_down: float32 [2, 2560, 960], P('section', 'dp')
- grad_norm_ffn: float32 [2, 960], P('section', 'dp')
The draws below stay inside these ranges and needn't reach their ends.
All inputs are finite; a program needn't handle non-finite values.
Results may differ from the reference program's by a relative error of at most 0.03.
Values may be sent and summed in bfloat16 or wider, within the bound.
No kernel may reach another device: no remote copies, remote signals or barrier semaphores. Data moves between devices by JAX's collectives and lax.ppermute only.
A program may use at most 256 MiB of HBM per device.

```python
import jax
import jax.numpy as jnp
from jax import lax

D = 960
HEADS = 15
KV_HEADS = 5
HEAD_DIM = 64
FF = 2560
MB = 2
QW = 960
KVW = 320
GROUP = 3
SEQ = 512
SEQS = 4
N_SECTION = 2


def shard_levels(stream_key, extent, pieces, smallest, largest):
    def one(axis_at, blocks):
        heights = jax.random.uniform(jax.random.fold_in(jax.random.fold_in(stream_key, 6), axis_at), (blocks,), jnp.float32, smallest / len(pieces), largest / len(pieces))
        return jnp.repeat(jnp.exp(heights), extent[axis_at] // blocks).reshape((-1,) + (1,) * (len(extent) - axis_at - 1))

    level = one(*pieces[0])
    for cut in pieces[1:]:
        level = level * one(*cut)
    return level


def gaussian(own_key, dims, scale, bound, shards=(), kind=jnp.bfloat16):
    level = shard_levels(own_key, dims, shards, -0.22, 0.18) if shards else 1.0
    values = jax.random.normal(own_key, dims, jnp.float32) * scale * level
    return jnp.minimum(jnp.maximum(values, -bound), bound).astype(kind)


def setup_inputs(seed: int = 0) -> dict:
    key_of = jax.random.split(jax.random.key(seed), 12)
    block_input = gaussian(key_of[0], (MB, SEQS, SEQ, D), 1.0, 6.0, ((1, 4), (2, 4)), jnp.float32)
    out_grad = gaussian(key_of[1], (MB, SEQS, SEQ, D), 1.0, 6.0, ((1, 4), (2, 4)), jnp.float32)
    w_query = gaussian(key_of[2], (N_SECTION, D, QW), D ** -0.5, 0.1875, ((0, 2), (1, 4)))
    w_key = gaussian(key_of[3], (N_SECTION, D, KVW), D ** -0.5, 0.1875, ((0, 2), (1, 4)))
    w_value = gaussian(key_of[4], (N_SECTION, D, KVW), D ** -0.5, 0.1875, ((0, 2), (1, 4)))
    w_out = gaussian(key_of[5], (N_SECTION, QW, D), (max(QW // 64, 1)) ** -0.5, 1.5, ((0, 2), (1, 4)))
    norm_attn = jnp.clip(1.0 + 0.18 * jax.random.normal(key_of[6], (N_SECTION, D), jnp.float32), 0.099609375, 1.8984375).astype(jnp.bfloat16)
    w_gate = gaussian(key_of[7], (N_SECTION, D, FF), D ** -0.5, 0.1875, ((0, 2), (2, 4)))
    w_up = gaussian(key_of[8], (N_SECTION, D, FF), D ** -0.5, 0.1875, ((0, 2), (2, 4)))
    w_down = gaussian(key_of[9], (N_SECTION, FF, D), FF ** -0.5, 0.125, ((0, 2), (1, 4)))
    norm_ffn = jnp.clip(1.0 + 0.18 * jax.random.normal(key_of[10], (N_SECTION, D), jnp.float32), 0.099609375, 1.8984375).astype(jnp.bfloat16)
    return {"block_input": block_input, "out_grad": out_grad, "w_query": w_query, "w_key": w_key, "w_value": w_value, "w_out": w_out, "norm_attn": norm_attn, "w_gate": w_gate, "w_up": w_up, "w_down": w_down, "norm_ffn": norm_ffn}


EPSILON = 1e-05
ROPE_BASE = 10000.0

def rope_tables(positions):
    half_dim = HEAD_DIM // 2
    freq_rows = ROPE_BASE ** (-(jnp.arange(half_dim, dtype=jnp.float32) * 2.0 / HEAD_DIM))
    angles = positions.astype(jnp.float32)[:, None] * freq_rows[None, :]
    cosine = jnp.concatenate([jnp.cos(angles), jnp.cos(angles)], axis=1)
    sine_rows = jnp.concatenate([jnp.sin(angles), jnp.sin(angles)], axis=1)
    return (cosine, sine_rows)

def turn_half(new_value):
    half_dim = HEAD_DIM // 2
    return jnp.concatenate([-new_value[..., half_dim:], new_value[..., :half_dim]], axis=-1)

def rotate(new_value, cosine, sine_rows):
    return new_value * cosine[:, None, :] + turn_half(new_value) * sine_rows[:, None, :]

def unrotate(grad_rows, cosine, sine_rows):
    return grad_rows * cosine[:, None, :] - turn_half(grad_rows * sine_rows[:, None, :])

def normalize(new_value, gain_row):
    inverse = lax.rsqrt(lax.optimization_barrier(jnp.mean(new_value * new_value, axis=-1, keepdims=True)) + EPSILON)
    return (new_value * inverse * gain_row.astype(jnp.float32), inverse)

def normalize_back(new_value, inverse, gain_row, grad_rows):
    scaled = grad_rows * gain_row.astype(jnp.float32)
    gain_grad = lax.optimization_barrier(jnp.sum(grad_rows * new_value * inverse, axis=0))
    value_grad = inverse * scaled - new_value * inverse ** 3 * lax.optimization_barrier(jnp.mean(scaled * new_value, axis=-1, keepdims=True))
    return (value_grad, gain_grad)

def project(normed, wq_all, wk_all, wv_all, cosine, sine_rows):
    queries = jnp.dot(normed, wq_all, preferred_element_type=jnp.float32).reshape(SEQ, HEADS, HEAD_DIM)
    queries = rotate(queries, cosine, sine_rows).astype(jnp.bfloat16)
    key_rows = jnp.dot(normed, wk_all, preferred_element_type=jnp.float32).reshape(SEQ, KV_HEADS, HEAD_DIM)
    key_rows = rotate(key_rows, cosine, sine_rows).astype(jnp.bfloat16)
    value_rows = jnp.dot(normed, wv_all, preferred_element_type=jnp.float32).astype(jnp.bfloat16)
    return (queries, key_rows, value_rows.reshape(SEQ, KV_HEADS, HEAD_DIM))

def attention_forward(queries, key_rows, value_rows):
    key_span = min(512, SEQ)
    score_scale = HEAD_DIM ** (-0.5)
    positions = jnp.arange(SEQ, dtype=jnp.int32)
    keys_wide = key_rows.astype(jnp.float32)
    values_wide = value_rows.astype(jnp.float32)

    def one_block(block_id):
        first_row = block_id * key_span
        query_block = lax.dynamic_slice_in_dim(queries, first_row, key_span, 0).astype(jnp.float32)
        query_block = query_block.reshape(key_span, KV_HEADS, GROUP, HEAD_DIM)
        query_pos = first_row + jnp.arange(key_span, dtype=jnp.int32)
        scores = jnp.einsum('tkgd,skd->kgts', query_block, keys_wide) * score_scale
        allowed = query_pos[:, None] >= positions[None, :]
        scores = jnp.where(allowed, scores, -jnp.inf)
        top_rows = lax.optimization_barrier(jnp.max(scores, axis=-1, keepdims=True))
        log_total = top_rows + jnp.log(lax.optimization_barrier(jnp.sum(jnp.exp(scores - top_rows), axis=-1, keepdims=True)))
        prob_rows = jnp.exp(scores - log_total)
        mixture = jnp.einsum('kgts,skd->tkgd', prob_rows, values_wide, precision=lax.Precision.HIGHEST).reshape(key_span, QW)
        return (mixture.astype(jnp.bfloat16), log_total[..., 0])
    mixtures, log_totals = lax.map(one_block, jnp.arange(SEQ // key_span))
    log_totals = jnp.transpose(log_totals, (1, 2, 0, 3)).reshape(KV_HEADS, GROUP, SEQ)
    return (mixtures.reshape(SEQ, QW), log_totals)

def attention_backward(queries, key_rows, value_rows, log_totals, grad_mix, mixture):
    key_span = min(512, SEQ)
    score_scale = HEAD_DIM ** (-0.5)
    positions = jnp.arange(SEQ, dtype=jnp.int32)
    keys_wide = key_rows.astype(jnp.float32)
    values_wide = value_rows.astype(jnp.float32)
    row_delta = lax.optimization_barrier(jnp.sum((grad_mix.astype(jnp.float32) * mixture.astype(jnp.float32)).reshape(SEQ, KV_HEADS, GROUP, HEAD_DIM), axis=-1))
    row_delta = jnp.transpose(row_delta, (1, 2, 0))

    def one_block(loop_state, block_id):
        key_grad, value_grad = loop_state
        first_row = block_id * key_span
        query_block = lax.dynamic_slice_in_dim(queries, first_row, key_span, 0).astype(jnp.float32)
        query_block = query_block.reshape(key_span, KV_HEADS, GROUP, HEAD_DIM)
        grad_block = lax.dynamic_slice_in_dim(grad_mix, first_row, key_span, 0).astype(jnp.float32)
        grad_block = grad_block.reshape(key_span, KV_HEADS, GROUP, HEAD_DIM)
        lse_block = lax.dynamic_slice_in_dim(log_totals, first_row, key_span, 2)
        delta_block = lax.dynamic_slice_in_dim(row_delta, first_row, key_span, 2)
        query_pos = first_row + jnp.arange(key_span, dtype=jnp.int32)
        scores = jnp.einsum('tkgd,skd->kgts', query_block, keys_wide) * score_scale
        allowed = query_pos[:, None] >= positions[None, :]
        prob_rows = jnp.where(allowed, jnp.exp(scores - lse_block[..., None]), 0.0)
        rounded = lax.optimization_barrier(prob_rows.astype(jnp.bfloat16)).astype(jnp.float32)
        value_grad = value_grad + jnp.einsum('kgts,tkgd->skd', rounded, grad_block)
        prob_grad = jnp.einsum('tkgd,skd->kgts', grad_block, values_wide)
        score_grad = (prob_rows * (prob_grad - delta_block[..., None])).astype(jnp.bfloat16)
        score_grad = lax.optimization_barrier(score_grad).astype(jnp.float32)
        query_grad = jnp.einsum('kgts,skd->tkgd', score_grad, keys_wide).reshape(key_span, HEADS, HEAD_DIM) * score_scale
        key_grad = key_grad + jnp.einsum('kgts,tkgd->skd', score_grad, query_block) * score_scale
        return ((key_grad, value_grad), query_grad)
    zero_rows = jnp.zeros((SEQ, KV_HEADS, HEAD_DIM), jnp.float32)
    (key_grad, value_grad), query_grads = lax.scan(one_block, (zero_rows, zero_rows), jnp.arange(SEQ // key_span))
    return (query_grads.reshape(SEQ, HEADS, HEAD_DIM), key_grad, value_grad)

def layer_forward(layer_in, params, cosine, sine_rows):
    wq_all, wk_all, wv_all, wo_all, gain_attn, wg_all, wu_all, wd_all, gain_ffn = params
    normed_a, inverse_a = normalize(layer_in, gain_attn)
    normed_a = normed_a.astype(jnp.bfloat16)
    queries, key_rows, value_rows = project(normed_a, wq_all, wk_all, wv_all, cosine, sine_rows)
    mixture, log_totals = attention_forward(queries, key_rows, value_rows)
    after_attn = layer_in + jnp.dot(mixture, wo_all, preferred_element_type=jnp.float32)
    normed_f, inverse_f = normalize(after_attn, gain_ffn)
    normed_f = normed_f.astype(jnp.bfloat16)
    gate_pre = jnp.dot(normed_f, wg_all, preferred_element_type=jnp.float32)
    up_proj = jnp.dot(normed_f, wu_all, preferred_element_type=jnp.float32)
    hidden = (jax.nn.silu(gate_pre) * up_proj).astype(jnp.bfloat16)
    layer_out = after_attn + jnp.dot(hidden, wd_all, preferred_element_type=jnp.float32)
    kept_rows = (normed_a, inverse_a, queries, key_rows, value_rows, mixture, log_totals, after_attn, normed_f, inverse_f, gate_pre, up_proj, hidden)
    return (layer_out, kept_rows)

def layer_backward(layer_in, kept_rows, out_rows, params, cosine, sine_rows):
    wq_all, wk_all, wv_all, wo_all, gain_attn, wg_all, wu_all, wd_all, gain_ffn = params
    normed_a, inverse_a, queries, key_rows, value_rows, mixture, log_totals, after_attn, normed_f, inverse_f, gate_pre, up_proj, hidden = kept_rows
    grad_b = out_rows.astype(jnp.bfloat16)
    grad_down = jnp.dot(hidden.T, grad_b, preferred_element_type=jnp.float32)
    hidden_grad = jnp.dot(grad_b, wd_all.T, preferred_element_type=jnp.float32)
    sigma_gate = jax.nn.sigmoid(gate_pre)
    gate_grad = (hidden_grad * up_proj * sigma_gate * (1.0 + gate_pre * (1.0 - sigma_gate))).astype(jnp.bfloat16)
    up_grad = (hidden_grad * gate_pre * sigma_gate).astype(jnp.bfloat16)
    grad_gate = jnp.dot(normed_f.T, gate_grad, preferred_element_type=jnp.float32)
    grad_up = jnp.dot(normed_f.T, up_grad, preferred_element_type=jnp.float32)
    normed_grad = jnp.dot(gate_grad, wg_all.T, preferred_element_type=jnp.float32) + jnp.dot(up_grad, wu_all.T, preferred_element_type=jnp.float32)
    back_f, gain_grad_f = normalize_back(after_attn, inverse_f, gain_ffn, normed_grad)
    attn_grad = out_rows + back_f
    attn_b = attn_grad.astype(jnp.bfloat16)
    grad_out = jnp.dot(mixture.T, attn_b, preferred_element_type=jnp.float32)
    mix_grad = jnp.dot(attn_b, wo_all.T, preferred_element_type=jnp.float32).astype(jnp.bfloat16)
    query_grad, key_grad, value_grad = attention_backward(queries, key_rows, value_rows, log_totals, mix_grad, mixture)
    query_b = unrotate(query_grad, cosine, sine_rows).reshape(SEQ, QW).astype(jnp.bfloat16)
    key_b = unrotate(key_grad, cosine, sine_rows).reshape(SEQ, KVW).astype(jnp.bfloat16)
    value_b = value_grad.reshape(SEQ, KVW).astype(jnp.bfloat16)
    grad_query = jnp.dot(normed_a.T, query_b, preferred_element_type=jnp.float32)
    grad_key = jnp.dot(normed_a.T, key_b, preferred_element_type=jnp.float32)
    grad_value = jnp.dot(normed_a.T, value_b, preferred_element_type=jnp.float32)
    normed_grad_a = jnp.dot(query_b, wq_all.T, preferred_element_type=jnp.float32) + jnp.dot(key_b, wk_all.T, preferred_element_type=jnp.float32) + jnp.dot(value_b, wv_all.T, preferred_element_type=jnp.float32)
    back_a, gain_grad_a = normalize_back(layer_in, inverse_a, gain_attn, normed_grad_a)
    return (attn_grad + back_a, (grad_query, grad_key, grad_value, grad_out, gain_grad_a, grad_gate, grad_up, grad_down, gain_grad_f))

def reference(block_input, out_grad, w_query, w_key, w_value, w_out, norm_attn, w_gate, w_up, w_down, norm_ffn):
    positions = jnp.arange(SEQ, dtype=jnp.int32)
    cosine, sine_rows = rope_tables(positions)
    all_weights = (w_query, w_key, w_value, w_out, norm_attn, w_gate, w_up, w_down, norm_ffn)
    inputs = block_input.reshape(MB * SEQS, SEQ, D)
    cotangents = out_grad.reshape(MB * SEQS, SEQ, D)

    def layer_params(layer_id):
        return tuple((weight[layer_id] for weight in all_weights))

    def one_sequence(running, seq_pair):
        seq_in, seq_grad = seq_pair
        layer_ins = []
        kept_all = []
        outputs = []
        current = seq_in
        for layer_id in range(N_SECTION):
            layer_ins.append(current)
            current, kept_rows = layer_forward(current, layer_params(layer_id), cosine, sine_rows)
            kept_all.append(kept_rows)
            outputs.append(current)
        grad_now = seq_grad
        in_grads = [grad_now] * N_SECTION
        running = list(running)
        for layer_id in reversed(range(N_SECTION)):
            grad_now, weight_grads = layer_backward(layer_ins[layer_id], kept_all[layer_id], grad_now, layer_params(layer_id), cosine, sine_rows)
            in_grads[layer_id] = grad_now
            running = [acc.at[layer_id].add(part_grad) for acc, part_grad in zip(running, weight_grads)]
        return (tuple(running), (jnp.stack(outputs), jnp.stack(in_grads)))
    start_sums = tuple((jnp.zeros(weight.shape, jnp.float32) for weight in all_weights))
    sums_out, (stacked_out, stacked_grad) = lax.scan(one_sequence, start_sums, (inputs, cotangents))
    section_out = jnp.transpose(stacked_out, (1, 0, 2, 3)).reshape(N_SECTION, MB, SEQS, SEQ, D)
    section_in_grad = jnp.transpose(stacked_grad, (1, 0, 2, 3)).reshape(N_SECTION, MB, SEQS, SEQ, D)
    return (section_out, section_in_grad, sums_out[0], sums_out[1], sums_out[2], sums_out[3], sums_out[4], sums_out[5], sums_out[6], sums_out[7], sums_out[8])
```

```python
import jax
import jax.numpy as jnp
from jax import lax
from jax.sharding import PartitionSpec as P

D = 960
HEADS = 15
KV_HEADS = 5
HEAD_DIM = 64
QW = 960
KVW = 320
GROUP = 3
EPSILON = 1e-05
ROPE_BASE = 10000.0
MASKED = -1e30
BF = jnp.bfloat16
F32 = jnp.float32


def dot(a, b):
    return jnp.dot(a, b, preferred_element_type=F32)


def rope_tables(positions):
    half_dim = HEAD_DIM // 2
    freq_rows = ROPE_BASE ** (-(jnp.arange(half_dim, dtype=F32) * 2.0 / HEAD_DIM))
    angles = positions.astype(F32)[:, None] * freq_rows[None, :]
    cosine = jnp.concatenate([jnp.cos(angles), jnp.cos(angles)], axis=1)
    sine_rows = jnp.concatenate([jnp.sin(angles), jnp.sin(angles)], axis=1)
    return (cosine, sine_rows)


def turn_half(u):
    half_dim = HEAD_DIM // 2
    return jnp.concatenate([-u[..., half_dim:], u[..., :half_dim]], axis=-1)


def rotate(u, cosine, sine_rows):
    return u * cosine[:, None, :] + turn_half(u) * sine_rows[:, None, :]


def unrotate(u, cosine, sine_rows):
    return u * cosine[:, None, :] - turn_half(u * sine_rows[:, None, :])


def normalize(x, gain):
    inverse = lax.rsqrt(jnp.mean(x * x, axis=-1, keepdims=True) + EPSILON)
    return (x * inverse * gain, inverse)


def normalize_back(x, inverse, gain, grad):
    scaled = grad * gain
    gain_grad = jnp.sum(grad * x * inverse, axis=0)
    value_grad = inverse * scaled - x * inverse**3 * jnp.mean(scaled * x, axis=-1, keepdims=True)
    return (value_grad, gain_grad)


def attend(q, k, v, query_pos):
    tok = q.shape[0]
    q = q.reshape(tok, KV_HEADS, GROUP, HEAD_DIM)
    scores = jnp.einsum("tkgd,skd->kgts", q, k, preferred_element_type=F32) * HEAD_DIM**-0.5
    allowed = query_pos[:, None] >= jnp.arange(k.shape[0], dtype=jnp.int32)[None, :]
    scores = jnp.where(allowed, scores, MASKED)
    peak = jnp.max(scores, axis=-1, keepdims=True)
    e = jnp.exp(scores - peak)
    total = jnp.sum(e, axis=-1, keepdims=True)
    probs = (e / total).astype(BF)
    o = jnp.einsum("kgts,skd->tkgd", probs, v, preferred_element_type=F32).reshape(tok, QW)
    return o.astype(BF), (peak + jnp.log(total))[..., 0]


def attend_back(q, k, v, lse, do, o, query_pos):
    tok = q.shape[0]
    q = q.reshape(tok, KV_HEADS, GROUP, HEAD_DIM)
    dor = do.reshape(tok, KV_HEADS, GROUP, HEAD_DIM)
    delta = jnp.sum((do.astype(F32) * o.astype(F32)).reshape(tok, KV_HEADS, GROUP, HEAD_DIM), axis=-1)
    delta = jnp.transpose(delta, (1, 2, 0))
    scale = HEAD_DIM**-0.5
    scores = jnp.einsum("tkgd,skd->kgts", q, k, preferred_element_type=F32) * scale
    allowed = query_pos[:, None] >= jnp.arange(k.shape[0], dtype=jnp.int32)[None, :]
    probs = jnp.where(allowed, jnp.exp(scores - lse[..., None]), 0.0)
    dv = jnp.einsum("kgts,tkgd->skd", probs.astype(BF), dor, preferred_element_type=F32)
    dp = jnp.einsum("tkgd,skd->kgts", dor, v, preferred_element_type=F32)
    ds = (probs * (dp - delta[..., None])).astype(BF)
    dq = jnp.einsum("kgts,skd->tkgd", ds, k, preferred_element_type=F32) * scale
    dk = jnp.einsum("kgts,tkgd->skd", ds, q, preferred_element_type=F32) * scale
    dkv = jnp.concatenate([dk.reshape(-1, KVW), dv.reshape(-1, KVW)], axis=1)
    return dq.reshape(tok, HEADS, HEAD_DIM), dkv


def layer_forward(x, w, cosine, sine, query_pos):
    wa, wg, wu, wd, ga, gf = w
    tok = x.shape[0]
    n1, r1 = normalize(x, ga)
    n1 = n1.astype(BF)
    qkv = dot(n1, wa[:, : QW + 2 * KVW])
    q = rotate(qkv[:, :QW].reshape(tok, HEADS, HEAD_DIM), cosine, sine).astype(BF)
    k = rotate(qkv[:, QW : QW + KVW].reshape(tok, KV_HEADS, HEAD_DIM), cosine, sine)
    kv = jnp.concatenate([k.reshape(tok, KVW), qkv[:, QW + KVW :]], axis=1).astype(BF)
    kv = lax.all_gather(kv, "ctx", axis=0, tiled=True)
    k = kv[:, :KVW].reshape(-1, KV_HEADS, HEAD_DIM)
    v = kv[:, KVW:].reshape(-1, KV_HEADS, HEAD_DIM)
    o, lse = attend(q, k, v, query_pos)
    h1 = x + dot(o, wa[:, QW + 2 * KVW :])
    n2, r2 = normalize(h1, gf)
    n2 = lax.all_gather(n2.astype(BF), "dp", axis=0, tiled=True)
    gate = dot(n2, wg)
    up = dot(n2, wu)
    hidden = (jax.nn.silu(gate) * up).astype(BF)
    part = dot(hidden, wd).astype(BF)
    out = h1 + lax.psum_scatter(part, "dp", scatter_dimension=0, tiled=True).astype(F32)
    return out, (x, n1, r1, q, k, v, o, lse, h1, n2, r2, gate, up, hidden)


def layer_backward(g, kept, w, cosine, sine, query_pos):
    wa, wg, wu, wd, ga, gf = w
    x, n1, r1, q, k, v, o, lse, h1, n2, r2, gate, up, hidden = kept
    tok = x.shape[0]
    gb = lax.all_gather(g.astype(BF), "dp", axis=0, tiled=True)
    grad_down = dot(hidden.T, gb)
    dh = dot(gb, wd.T)
    sigma = jax.nn.sigmoid(gate)
    dgate = (dh * up * sigma * (1.0 + gate * (1.0 - sigma))).astype(BF)
    dup = (dh * gate * sigma).astype(BF)
    grad_gate = dot(n2.T, dgate)
    grad_up = dot(n2.T, dup)
    part = (dot(dgate, wg.T) + dot(dup, wu.T)).astype(BF)
    dn2 = lax.psum_scatter(part, "dp", scatter_dimension=0, tiled=True).astype(F32)
    back_f, gain_f = normalize_back(h1, r2, gf, dn2)
    dh1 = g + back_f
    db = dh1.astype(BF)
    grad_out = dot(o.T, db)
    do = dot(db, wa[:, QW + 2 * KVW :].T).astype(BF)
    dq, dkv = attend_back(q, k, v, lse, do, o, query_pos)
    dkv = lax.psum_scatter(dkv.astype(BF), "ctx", scatter_dimension=0, tiled=True).astype(F32)
    dq = unrotate(dq, cosine, sine).reshape(tok, QW)
    dk = unrotate(dkv[:, :KVW].reshape(tok, KV_HEADS, HEAD_DIM), cosine, sine).reshape(tok, KVW)
    dqkv = jnp.concatenate([dq, dk, dkv[:, KVW:]], axis=1).astype(BF)
    grad_qkv = dot(n1.T, dqkv)
    dn1 = dot(dqkv, wa[:, : QW + 2 * KVW].T)
    back_a, gain_a = normalize_back(x, r1, ga, dn1)
    grads = (
        jnp.concatenate([grad_qkv, grad_out], axis=1).astype(BF),
        jnp.stack([gain_a, gain_f]),
        grad_gate.astype(BF),
        grad_up.astype(BF),
        grad_down.astype(BF),
    )
    return dh1 + back_a, grads


def swap_section(p0, p1, section_id):
    mine = jnp.where(section_id == 0, p0, p1)
    other = jnp.where(section_id == 0, p1, p0)
    count = lax.axis_size("section")
    got = lax.ppermute(other, "section", [(i, count - 1 - i) for i in range(count)])
    return mine.astype(F32) + got.astype(F32)


def own_layer(p0, p1, section_id):
    mine = jnp.where(section_id == 0, p0, p1)
    other = jnp.where(section_id == 0, p1, p0)
    count = lax.axis_size("section")
    got = lax.ppermute(other, "section", [(i, count - 1 - i) for i in range(count)])
    first = jnp.where(section_id == 0, mine, got)
    second = jnp.where(section_id == 0, got, mine)
    return jnp.stack([first, second])


def body(
    block_input, out_grad, w_query, w_key, w_value, w_out, norm_attn, w_gate, w_up, w_down, norm_ffn
):
    section_id = lax.axis_index("section")
    tok_rows = block_input.shape[2]
    query_pos = lax.axis_index("ctx") * tok_rows + jnp.arange(tok_rows, dtype=jnp.int32)
    cosine, sine = rope_tables(query_pos)
    x = lax.dynamic_index_in_dim(block_input[:, 0], section_id, 0, keepdims=False)
    g = lax.dynamic_index_in_dim(out_grad[:, 0], section_id, 0, keepdims=False)
    wa = jnp.concatenate([w_query[0], w_key[0], w_value[0], w_out[0]], axis=1)
    wa = lax.all_gather(lax.all_gather(wa, "dp", axis=0, tiled=True), "section")
    gains = jnp.stack([norm_attn[0], norm_ffn[0]])
    gains = lax.all_gather(lax.all_gather(gains, "dp", axis=1, tiled=True), "section").astype(F32)
    wg = lax.all_gather(w_gate[0], "section")
    wu = lax.all_gather(w_up[0], "section")
    wd = lax.all_gather(w_down[0], "section")
    layers = [(wa[l], wg[l], wu[l], wd[l], gains[l, 0], gains[l, 1]) for l in range(2)]
    out0, kept0 = layer_forward(x, layers[0], cosine, sine, query_pos)
    out1, kept1 = layer_forward(out0, layers[1], cosine, sine, query_pos)
    in1, grads1 = layer_backward(g, kept1, layers[1], cosine, sine, query_pos)
    in0, grads0 = layer_backward(in1, kept0, layers[0], cosine, sine, query_pos)
    section_outs = own_layer(out0, out1, section_id)
    in_grads = own_layer(in0, in1, section_id)
    ga, gn, gg, gu, gd = (
        swap_section(a, b, section_id) for a, b in zip(grads0, grads1)
    )
    ga = lax.psum_scatter(ga.astype(BF), "dp", scatter_dimension=0, tiled=True)
    ga = lax.psum(ga, "ctx").astype(F32)
    gn = lax.psum_scatter(gn, "dp", scatter_dimension=1, tiled=True)
    gn = lax.psum(gn, "ctx")
    gg = lax.psum(gg.astype(BF), "ctx").astype(F32)
    gu = lax.psum(gu.astype(BF), "ctx").astype(F32)
    gd = lax.psum(gd.astype(BF), "ctx").astype(F32)
    return (
        section_outs[None, :, None],
        in_grads[None, :, None],
        ga[None, :, :QW],
        ga[None, :, QW : QW + KVW],
        ga[None, :, QW + KVW : QW + 2 * KVW],
        ga[None, :, QW + 2 * KVW :],
        gn[None, 0],
        gg[None],
        gu[None],
        gd[None],
        gn[None, 1],
    )


def solution(mesh):
    return jax.shard_map(
        body,
        mesh=mesh,
        in_specs=(
            P(None, "dp", "ctx", None),
            P(None, "dp", "ctx", None),
            P("section", "dp", None),
            P("section", "dp", None),
            P("section", "dp", None),
            P("section", "dp", None),
            P("section", "dp"),
            P("section", None, "dp"),
            P("section", None, "dp"),
            P("section", "dp", None),
            P("section", "dp"),
        ),
        out_specs=(
            P("section", None, "dp", "ctx", None),
            P("section", None, "dp", "ctx", None),
            P("section", "dp", None),
            P("section", "dp", None),
            P("section", "dp", None),
            P("section", "dp", None),
            P("section", "dp"),
            P("section", None, "dp"),
            P("section", None, "dp"),
            P("section", "dp", None),
            P("section", "dp"),
        ),
        check_vma=False,
    )
```

```python
import functools
import math

import jax
import jax.numpy as jnp
from jax import lax
from jax.experimental import pallas as pl
from jax.experimental.pallas import tpu as pltpu
from jax.sharding import PartitionSpec as P

D = 960
HEADS = 15
KV_HEADS = 5
HEAD_DIM = 64
QW = 960
KVW = 320
GROUP = 3
EPSILON = 1e-05
ROPE_BASE = 10000.0
MASKED = -1e30
BF = jnp.bfloat16
F32 = jnp.float32


def dot(a, b):
    return jnp.dot(a, b, preferred_element_type=F32)


def rope_tables(positions):
    half_dim = HEAD_DIM // 2
    freq_rows = ROPE_BASE ** (-(jnp.arange(half_dim, dtype=F32) * 2.0 / HEAD_DIM))
    angles = positions.astype(F32)[:, None] * freq_rows[None, :]
    cosine = jnp.concatenate([jnp.cos(angles), jnp.cos(angles)], axis=1)
    sine_rows = jnp.concatenate([jnp.sin(angles), jnp.sin(angles)], axis=1)
    return (cosine, sine_rows)


def turn_half(u):
    half_dim = HEAD_DIM // 2
    return jnp.concatenate([-u[..., half_dim:], u[..., :half_dim]], axis=-1)


def rotate(u, cosine, sine_rows):
    return u * cosine[:, None, :] + turn_half(u) * sine_rows[:, None, :]


def unrotate(u, cosine, sine_rows):
    return u * cosine[:, None, :] - turn_half(u * sine_rows[:, None, :])


def normalize(x, gain):
    inverse = lax.rsqrt(jnp.mean(x * x, axis=-1, keepdims=True) + EPSILON)
    return (x * inverse * gain, inverse)


def normalize_back(x, inverse, gain, grad):
    scaled = grad * gain
    gain_grad = jnp.sum(grad * x * inverse, axis=0)
    value_grad = inverse * scaled - x * inverse**3 * jnp.mean(scaled * x, axis=-1, keepdims=True)
    return (value_grad, gain_grad)


def attend(q, k, v, query_pos):
    tok = q.shape[0]
    q = q.reshape(tok, KV_HEADS, GROUP, HEAD_DIM)
    scores = jnp.einsum("tkgd,skd->kgts", q, k, preferred_element_type=F32) * HEAD_DIM**-0.5
    allowed = query_pos[:, None] >= jnp.arange(k.shape[0], dtype=jnp.int32)[None, :]
    scores = jnp.where(allowed, scores, MASKED)
    peak = jnp.max(scores, axis=-1, keepdims=True)
    e = jnp.exp(scores - peak)
    total = jnp.sum(e, axis=-1, keepdims=True)
    probs = (e / total).astype(BF)
    o = jnp.einsum("kgts,skd->tkgd", probs, v, preferred_element_type=F32).reshape(tok, QW)
    return o.astype(BF), (peak + jnp.log(total))[..., 0]


def attend_back(q, k, v, lse, do, o, query_pos):
    tok = q.shape[0]
    q = q.reshape(tok, KV_HEADS, GROUP, HEAD_DIM)
    dor = do.reshape(tok, KV_HEADS, GROUP, HEAD_DIM)
    delta = jnp.sum((do.astype(F32) * o.astype(F32)).reshape(tok, KV_HEADS, GROUP, HEAD_DIM), axis=-1)
    delta = jnp.transpose(delta, (1, 2, 0))
    scale = HEAD_DIM**-0.5
    scores = jnp.einsum("tkgd,skd->kgts", q, k, preferred_element_type=F32) * scale
    allowed = query_pos[:, None] >= jnp.arange(k.shape[0], dtype=jnp.int32)[None, :]
    probs = jnp.where(allowed, jnp.exp(scores - lse[..., None]), 0.0)
    dv = jnp.einsum("kgts,tkgd->skd", probs.astype(BF), dor, preferred_element_type=F32)
    dp = jnp.einsum("tkgd,skd->kgts", dor, v, preferred_element_type=F32)
    ds = (probs * (dp - delta[..., None])).astype(BF)
    dq = jnp.einsum("kgts,skd->tkgd", ds, k, preferred_element_type=F32) * scale
    dk = jnp.einsum("kgts,tkgd->skd", ds, q, preferred_element_type=F32) * scale
    dkv = jnp.concatenate([dk.reshape(-1, KVW), dv.reshape(-1, KVW)], axis=1)
    return dq.reshape(tok, HEADS, HEAD_DIM), dkv


def layer_forward(x, w, cosine, sine, query_pos):
    wa, wg, wu, wd, ga, gf = w
    tok = x.shape[0]
    n1, r1 = normalize(x, ga)
    n1 = n1.astype(BF)
    qkv = dot(n1, wa[:, : QW + 2 * KVW])
    q = rotate(qkv[:, :QW].reshape(tok, HEADS, HEAD_DIM), cosine, sine).astype(BF)
    k = rotate(qkv[:, QW : QW + KVW].reshape(tok, KV_HEADS, HEAD_DIM), cosine, sine)
    kv = jnp.concatenate([k.reshape(tok, KVW), qkv[:, QW + KVW :]], axis=1).astype(BF)
    kv = lax.all_gather(kv, "ctx", axis=0, tiled=True)
    k = kv[:, :KVW].reshape(-1, KV_HEADS, HEAD_DIM)
    v = kv[:, KVW:].reshape(-1, KV_HEADS, HEAD_DIM)
    o, lse = attend(q, k, v, query_pos)
    h1 = x + dot(o, wa[:, QW + 2 * KVW :])
    n2, r2 = normalize(h1, gf)
    n2 = lax.all_gather(n2.astype(BF), "dp", axis=0, tiled=True)
    gate = dot(n2, wg)
    up = dot(n2, wu)
    hidden = (jax.nn.silu(gate) * up).astype(BF)
    part = dot(hidden, wd).astype(BF)
    out = h1 + lax.psum_scatter(part, "dp", scatter_dimension=0, tiled=True).astype(F32)
    return out, (x, n1, r1, q, k, v, o, lse, h1, n2, r2, gate, up, hidden)


def layer_backward(g, kept, w, cosine, sine, query_pos):
    wa, wg, wu, wd, ga, gf = w
    x, n1, r1, q, k, v, o, lse, h1, n2, r2, gate, up, hidden = kept
    tok = x.shape[0]
    gb = lax.all_gather(g.astype(BF), "dp", axis=0, tiled=True)
    grad_down = dot(hidden.T, gb)
    dh = dot(gb, wd.T)
    sigma = jax.nn.sigmoid(gate)
    dgate = (dh * up * sigma * (1.0 + gate * (1.0 - sigma))).astype(BF)
    dup = (dh * gate * sigma).astype(BF)
    grad_gate = dot(n2.T, dgate)
    grad_up = dot(n2.T, dup)
    part = (dot(dgate, wg.T) + dot(dup, wu.T)).astype(BF)
    dn2 = lax.psum_scatter(part, "dp", scatter_dimension=0, tiled=True).astype(F32)
    back_f, gain_f = normalize_back(h1, r2, gf, dn2)
    dh1 = g + back_f
    db = dh1.astype(BF)
    grad_out = dot(o.T, db)
    do = dot(db, wa[:, QW + 2 * KVW :].T).astype(BF)
    dq, dkv = attend_back(q, k, v, lse, do, o, query_pos)
    dkv = lax.psum_scatter(dkv.astype(BF), "ctx", scatter_dimension=0, tiled=True).astype(F32)
    dq = unrotate(dq, cosine, sine).reshape(tok, QW)
    dk = unrotate(dkv[:, :KVW].reshape(tok, KV_HEADS, HEAD_DIM), cosine, sine).reshape(tok, KVW)
    dqkv = jnp.concatenate([dq, dk, dkv[:, KVW:]], axis=1).astype(BF)
    grad_qkv = dot(n1.T, dqkv)
    dn1 = dot(dqkv, wa[:, : QW + 2 * KVW].T)
    back_a, gain_a = normalize_back(x, r1, ga, dn1)
    grads = (
        jnp.concatenate([grad_qkv, grad_out], axis=1).astype(BF),
        jnp.stack([gain_a, gain_f]),
        grad_gate.astype(BF),
        grad_up.astype(BF),
        grad_down.astype(BF),
    )
    return dh1 + back_a, grads


def swap_section(p0, p1, section_id):
    mine = jnp.where(section_id == 0, p0, p1)
    other = jnp.where(section_id == 0, p1, p0)
    count = lax.axis_size("section")
    got = lax.ppermute(other, "section", [(i, count - 1 - i) for i in range(count)])
    return mine.astype(F32) + got.astype(F32)


def own_layer(p0, p1, section_id):
    mine = jnp.where(section_id == 0, p0, p1)
    other = jnp.where(section_id == 0, p1, p0)
    count = lax.axis_size("section")
    got = lax.ppermute(other, "section", [(i, count - 1 - i) for i in range(count)])
    first = jnp.where(section_id == 0, mine, got)
    second = jnp.where(section_id == 0, got, mine)
    return jnp.stack([first, second])


def body_plain(
    block_input, out_grad, w_query, w_key, w_value, w_out, norm_attn, w_gate, w_up, w_down, norm_ffn
):
    section_id = lax.axis_index("section")
    tok_rows = block_input.shape[2]
    query_pos = lax.axis_index("ctx") * tok_rows + jnp.arange(tok_rows, dtype=jnp.int32)
    cosine, sine = rope_tables(query_pos)
    x = lax.dynamic_index_in_dim(block_input[:, 0], section_id, 0, keepdims=False)
    g = lax.dynamic_index_in_dim(out_grad[:, 0], section_id, 0, keepdims=False)
    wa = jnp.concatenate([w_query[0], w_key[0], w_value[0], w_out[0]], axis=1)
    wa = lax.all_gather(lax.all_gather(wa, "dp", axis=0, tiled=True), "section")
    gains = jnp.stack([norm_attn[0], norm_ffn[0]])
    gains = lax.all_gather(lax.all_gather(gains, "dp", axis=1, tiled=True), "section").astype(F32)
    wg = lax.all_gather(w_gate[0], "section")
    wu = lax.all_gather(w_up[0], "section")
    wd = lax.all_gather(w_down[0], "section")
    layers = [(wa[l], wg[l], wu[l], wd[l], gains[l, 0], gains[l, 1]) for l in range(2)]
    out0, kept0 = layer_forward(x, layers[0], cosine, sine, query_pos)
    out1, kept1 = layer_forward(out0, layers[1], cosine, sine, query_pos)
    in1, grads1 = layer_backward(g, kept1, layers[1], cosine, sine, query_pos)
    in0, grads0 = layer_backward(in1, kept0, layers[0], cosine, sine, query_pos)
    section_outs = own_layer(out0, out1, section_id)
    in_grads = own_layer(in0, in1, section_id)
    ga, gn, gg, gu, gd = (
        swap_section(a, b, section_id) for a, b in zip(grads0, grads1)
    )
    ga = lax.psum_scatter(ga.astype(BF), "dp", scatter_dimension=0, tiled=True)
    ga = lax.psum(ga, "ctx").astype(F32)
    gn = lax.psum_scatter(gn, "dp", scatter_dimension=1, tiled=True)
    gn = lax.psum(gn, "ctx")
    gg = lax.psum(gg.astype(BF), "ctx").astype(F32)
    gu = lax.psum(gu.astype(BF), "ctx").astype(F32)
    gd = lax.psum(gd.astype(BF), "ctx").astype(F32)
    return (
        section_outs[None, :, None],
        in_grads[None, :, None],
        ga[None, :, :QW],
        ga[None, :, QW : QW + KVW],
        ga[None, :, QW + KVW : QW + 2 * KVW],
        ga[None, :, QW + 2 * KVW :],
        gn[None, 0],
        gg[None],
        gu[None],
        gd[None],
        gn[None, 1],
    )


def t_dot(a, b):
    return lax.dot_general(a, b, (((0,), (0,)), ((), ())), preferred_element_type=F32)


def dot_t(a, b):
    return lax.dot_general(a, b, (((1,), (1,)), ((), ())), preferred_element_type=F32)


def shape_of(*dims, kind=BF):
    return jax.ShapeDtypeStruct(dims, kind)


def call(kernel, out_shape, *args, flops=0, grid=None, in_specs=None, out_specs=None, scratch=()):
    moved = sum(math.prod(a.shape) * a.dtype.itemsize for a in list(args) + list(out_shape))
    kwargs = {} if grid is None else {"grid": grid}
    held = moved + sum(math.prod(m.shape) * 4 for m in scratch)
    vmem = pl.BlockSpec(memory_space=pltpu.VMEM)
    smem = pl.BlockSpec(memory_space=pltpu.SMEM)
    return pl.pallas_call(
        kernel,
        out_shape=out_shape,
        in_specs=in_specs or [smem if a.dtype == jnp.int32 else vmem for a in args],
        out_specs=out_specs or [vmem] * len(out_shape),
        scratch_shapes=scratch,
        cost_estimate=pl.CostEstimate(flops=flops, bytes_accessed=moved, transcendentals=0),
        compiler_params=pltpu.CompilerParams(vmem_limit_bytes=min(60 << 20, held * 9 // 8 + (8 << 20))),
        **kwargs,
    )(*args)


def turn(u, cosine, sine, sign, first, last):
    rows, width = u.shape
    padded = -(-width // 128) * 128
    if padded > width:
        u = jnp.concatenate([u, jnp.zeros((rows, padded - width), F32)], axis=1)
    lane = lax.broadcasted_iota(jnp.int32, (rows, padded), 1)
    partner = jnp.where(
        lane % HEAD_DIM < HEAD_DIM // 2,
        pltpu.roll(u, padded - HEAD_DIM // 2, 1),
        pltpu.roll(u, HEAD_DIM // 2, 1),
    )
    cosine = jnp.concatenate([cosine] * (padded // 128), axis=1)
    sine = jnp.concatenate([sine] * (padded // 128), axis=1)
    turned = u * cosine + (partner * sine if sign > 0 else -(partner * sine))
    return jnp.where((lane >= first) & (lane < last), turned, u)[:, :width]


def inverse_norm(x):
    return lax.rsqrt(jnp.mean(x * x, axis=-1, keepdims=True) + EPSILON)


def project_kernel(count, *refs):
    parts, (order, w0, w1, cosine, sine, x_ref, n_ref, q_ref, kv_ref, gain_ref) = refs[:count], refs[count:]
    columns = jnp.concatenate([w0[:, GAINS:QKV], w1[:, GAINS:QKV]], axis=0)
    gains = lax.dot_general(columns, order[...], (((0,), (1,)), ((), ())), preferred_element_type=F32)
    gain_ref[...] = gains[:8]
    x = parts[0][...]
    for part in parts[1:]:
        x = x + part[...].astype(F32)
    x_ref[...] = x
    n = (x * inverse_norm(x) * gains[:1]).astype(BF)
    n = dot(n, order[...]).astype(BF)
    n_ref[...] = n
    half = w0.shape[0]
    out = dot(n[:, :half], w0[:, QKV:COLUMNS]) + dot(n[:, half:], w1[:, QKV:COLUMNS])
    kv = turn(out[:, : 2 * KVW], cosine[...], sine[...], 1, 0, KVW)
    kv_ref[...] = kv.astype(BF)
    q_ref[...] = turn(out[:, 2 * KVW :], cosine[...], sine[...], 1, 0, QW).astype(BF)


def run_project(parts, order, wa, tables):
    tok = parts[0].shape[0]
    args = list(parts) + [order, *wa, *tables]
    return call(
        functools.partial(project_kernel, len(parts)),
        [
            shape_of(tok, D, kind=F32),
            shape_of(tok, order.shape[1]),
            shape_of(tok, QW),
            shape_of(tok, 2 * KVW),
            shape_of(8, D, kind=F32),
        ],
        *args,
        flops=2 * tok * order.shape[1] * (D + QW + 2 * KVW),
    )


def causal(c, tok, count):
    shape = (GROUP * tok, count * tok)
    row = c * tok + lax.broadcasted_iota(jnp.int32, shape, 0) % tok
    lane = lax.broadcasted_iota(jnp.int32, shape, 1)
    key = jnp.zeros(shape, jnp.int32)
    for k in range(count):
        key = jnp.where(lane // tok == k, (c ^ k) * tok + lane % tok, key)
    return row >= key


def heads_of(x, j):
    return jnp.concatenate(
        [x[:, (GROUP * j + g) * HEAD_DIM : (GROUP * j + g + 1) * HEAD_DIM] for g in range(GROUP)], axis=0
    )


def attend_kernel(c_ref, x_ref, q_ref, kv0, kv1, kv2, kv3, gain, order, w0, w1, o_ref, op_ref, lse_ref, h_ref, n_ref):
    tok = q_ref.shape[0]
    kv = jnp.concatenate([kv0[...], kv1[...], kv2[...], kv3[...]], axis=0)
    q = q_ref[...]
    allowed = causal(c_ref[0], tok, 4)
    for j in range(KV_HEADS):
        k = kv[:, j * HEAD_DIM : (j + 1) * HEAD_DIM]
        v = kv[:, KVW + j * HEAD_DIM : KVW + (j + 1) * HEAD_DIM]
        scores = jnp.where(allowed, dot_t(heads_of(q, j), k) * HEAD_DIM**-0.5, MASKED)
        peak = jnp.max(scores, axis=-1, keepdims=True)
        e = jnp.exp(scores - peak)
        total = jnp.sum(e, axis=-1, keepdims=True)
        o = dot((e * (1.0 / total)).astype(BF), v).astype(BF)
        lse = peak + jnp.log(total)
        for g in range(GROUP):
            h = GROUP * j + g
            o_ref[:, h * HEAD_DIM : (h + 1) * HEAD_DIM] = o[g * tok : (g + 1) * tok]
            lse_ref[:, h : h + 1] = lse[g * tok : (g + 1) * tok]
    op = dot(o_ref[...], order[...]).astype(BF)
    op_ref[...] = op
    half = w0.shape[0]
    h1 = x_ref[...] + dot(op[:, :half], w0[:, WO:GAINS]) + dot(op[:, half:], w1[:, WO:GAINS])
    h_ref[...] = h1
    n_ref[...] = (h1 * inverse_norm(h1) * gain[1:2]).astype(BF)


def run_attend(c, x, q, kv, gain, order, wa):
    tok = q.shape[0]
    return call(
        attend_kernel,
        [
            shape_of(tok, QW),
            shape_of(tok, order.shape[1]),
            shape_of(tok, 16, kind=F32),
            shape_of(tok, D, kind=F32),
            shape_of(tok, D),
        ],
        c, x, q, *kv, gain, order, *wa,
        flops=2 * tok * (4 * tok * QW * 2 + order.shape[1] * D * 2),
    )


def ffn_kernel(h_ref, n0, n1, n2, n3, wg, wu, wd, gate_ref, up_ref, hidden_ref, p0, p1, p2, p3):
    n = jnp.concatenate([n0[...], n1[...], n2[...], n3[...]], axis=0)
    gate, up = dot(n, wg[...]), dot(n, wu[...])
    gate_ref[...], up_ref[...] = gate, up
    hidden = (gate * (1.0 / (1.0 + jnp.exp(-gate))) * up).astype(BF)
    hidden_ref[...] = hidden
    part = dot(hidden, wd[...])
    tok = n0.shape[0]
    p0[...] = h_ref[...] + part[:tok]
    for k, p in enumerate((p1, p2, p3), 1):
        p[...] = part[k * tok : (k + 1) * tok].astype(BF)


def run_ffn(h1, n2, wg, wu, wd):
    tok, width = h1.shape[0], wg.shape[1]
    return call(
        ffn_kernel,
        [shape_of(4 * tok, width, kind=F32)] * 2
        + [shape_of(4 * tok, width), shape_of(tok, D, kind=F32)]
        + [shape_of(tok, D)] * 3,
        h1, *n2, wg, wu, wd,
        flops=6 * 4 * tok * width * D,
    )


def ffn_back_kernel(g0, g1, g2, g3, gate_ref, up_ref, wg, wu, wd, dgate_ref, dup_ref, p0, p1, p2, p3):
    gb = jnp.concatenate([g0[...], g1[...], g2[...], g3[...]], axis=0)
    dh = dot_t(gb, wd[...])
    gate, up = gate_ref[...], up_ref[...]
    sigma = 1.0 / (1.0 + jnp.exp(-gate))
    dgate = (dh * up * sigma * (1.0 + gate * (1.0 - sigma))).astype(BF)
    dup = (dh * gate * sigma).astype(BF)
    dgate_ref[...], dup_ref[...] = dgate, dup
    part = dot_t(dgate, wg[...]) + dot_t(dup, wu[...])
    tok = g0.shape[0]
    p0[...] = part[:tok]
    for k, p in enumerate((p1, p2, p3), 1):
        p[...] = part[k * tok : (k + 1) * tok].astype(BF)


def run_ffn_back(gb, gate, up, wg, wu, wd):
    tok, width = gb[0].shape[0], wg.shape[1]
    return call(
        ffn_back_kernel,
        [shape_of(4 * tok, width)] * 2 + [shape_of(tok, D, kind=F32)] + [shape_of(tok, D)] * 3,
        *gb, gate, up, wg, wu, wd,
        flops=6 * 4 * tok * width * D,
    )


def ffn_grads_kernel(s_ref, dgate, dup, hidden, *refs):
    n, gb = (jnp.concatenate([r[...] for r in refs[k : k + 4]], axis=0) for k in (0, 4))
    gu_keep, gu_send, down_keep, down_send, down = refs[8:]
    s = s_ref[0]
    a, b = dgate[...], dup[...]
    first = s == 0
    gu_keep[...] = t_dot(n, jnp.where(first, a, b)).astype(BF)
    gu_send[...] = t_dot(n, jnp.where(first, b, a)).astype(BF)
    down[...] = t_dot(hidden[...], gb)
    half = down.shape[0] // 2
    down_keep[...] = down[pl.ds(pl.multiple_of(s * half, half), half), :].astype(BF)
    down_send[...] = down[pl.ds(pl.multiple_of((1 - s) * half, half), half), :].astype(BF)


def run_ffn_grads(s, dgate, dup, hidden, n2, gb):
    tok, width = dgate.shape
    return call(
        ffn_grads_kernel,
        [shape_of(D, width)] * 2 + [shape_of(width // 2, D)] * 2,
        s, dgate, dup, hidden, *n2, *gb,
        flops=6 * tok * width * D,
        scratch=[pltpu.VMEM((width, D), F32)],
    )


def attend_back_kernel(c_ref, *refs):
    parts, kv_refs = refs[:4], refs[4:8]
    h_ref, g_ref, q_ref, o_ref, lse_ref, gain, order, w0, w1, cosine, sine = refs[8:19]
    dh_ref, db_ref, gain_ref, dq_ref, d0, d1, d2, d3, dq_acc, dkv_acc = refs[19:]
    tok = q_ref.shape[0]
    dn = parts[0][...]
    for part in parts[1:]:
        dn = dn + part[...].astype(F32)
    h1 = h_ref[...]
    inverse = inverse_norm(h1)
    gain_ref[...] = jnp.sum(dn * h1 * inverse, axis=0, keepdims=True)
    scaled = dn * gain[1:2]
    dh = g_ref[...] + inverse * scaled - h1 * inverse**3 * jnp.mean(scaled * h1, axis=-1, keepdims=True)
    dh_ref[...] = dh
    db = dh.astype(BF)
    db_ref[...] = db
    dop = jnp.concatenate([dot_t(db, w0[:, WO:GAINS]), dot_t(db, w1[:, WO:GAINS])], axis=1).astype(BF)
    do = dot_t(dop, order[...]).astype(BF)
    kv = jnp.concatenate([r[...] for r in kv_refs], axis=0)
    q, o, lse_all = q_ref[...], o_ref[...], lse_ref[...]
    allowed = causal(c_ref[0], tok, 4)
    scale = HEAD_DIM**-0.5
    for j in range(KV_HEADS):
        k = kv[:, j * HEAD_DIM : (j + 1) * HEAD_DIM]
        v = kv[:, KVW + j * HEAD_DIM : KVW + (j + 1) * HEAD_DIM]
        qj, doj = heads_of(q, j), heads_of(do, j)
        delta = jnp.sum(doj.astype(F32) * heads_of(o, j).astype(F32), axis=-1, keepdims=True)
        lse = jnp.concatenate([lse_all[:, GROUP * j + g : GROUP * j + g + 1] for g in range(GROUP)], axis=0)
        probs = jnp.where(allowed, jnp.exp(dot_t(qj, k) * scale - lse), 0.0)
        dkv_acc[:, KVW + j * HEAD_DIM : KVW + (j + 1) * HEAD_DIM] = t_dot(probs.astype(BF), doj)
        ds = (probs * (dot_t(doj, v) - delta)).astype(BF)
        dkv_acc[:, j * HEAD_DIM : (j + 1) * HEAD_DIM] = t_dot(ds, qj) * scale
        dq = dot(ds, k) * scale
        for g in range(GROUP):
            h = GROUP * j + g
            dq_acc[:, h * HEAD_DIM : (h + 1) * HEAD_DIM] = dq[g * tok : (g + 1) * tok]
    dq_ref[...] = turn(dq_acc[...], cosine[...], sine[...], -1, 0, QW).astype(BF)
    d0[...] = dkv_acc[:tok]
    for k, d in enumerate((d1, d2, d3), 1):
        d[...] = dkv_acc[k * tok : (k + 1) * tok].astype(BF)


def run_attend_back(c, parts, kv, h1, g, q, o, lse, gain, order, wa, tables):
    tok = q.shape[0]
    return call(
        attend_back_kernel,
        [
            shape_of(tok, D, kind=F32),
            shape_of(tok, D),
            shape_of(1, D, kind=F32),
            shape_of(tok, QW),
            shape_of(tok, 2 * KVW, kind=F32),
        ]
        + [shape_of(tok, 2 * KVW)] * 3,
        c, *parts, *kv, h1, g, q, o, lse, gain, order, *wa, *tables,
        flops=2 * tok * (4 * tok * QW * 5 + order.shape[1] * D * 2),
        scratch=[pltpu.VMEM((tok, QW), F32), pltpu.VMEM((4 * tok, 2 * KVW), F32)],
    )


def project_back_kernel(*refs):
    parts, refs = refs[:4], refs[4:]
    dq_ref, x_ref, dh_ref, gain_f, gain, order, w0, w1, cosine, sine = refs[:10]
    in_ref, gb_ref, dqkv_ref, gains_ref = refs[10:]
    dkv = parts[0][...]
    for part in parts[1:]:
        dkv = dkv + part[...].astype(F32)
    dkv = turn(dkv, cosine[...], sine[...], -1, 0, KVW).astype(BF)
    dqkv_ref[:, : 2 * KVW] = dkv
    dqkv_ref[:, 2 * KVW :] = dq_ref[...]
    dqkv = dqkv_ref[...]
    ds = jnp.concatenate([dot_t(dqkv, w0[:, QKV:COLUMNS]), dot_t(dqkv, w1[:, QKV:COLUMNS])], axis=1)
    high = ds.astype(BF)
    low = (ds - high.astype(F32)).astype(BF)
    dn = dot_t(high, order[...]) + dot_t(low, order[...])
    x = x_ref[...]
    inverse = inverse_norm(x)
    gain_a = jnp.sum(dn * x * inverse, axis=0, keepdims=True)
    scaled = dn * gain[:1]
    out = dh_ref[...] + inverse * scaled - x * inverse**3 * jnp.mean(scaled * x, axis=-1, keepdims=True)
    in_ref[...] = out
    gb_ref[...] = out.astype(BF)
    row = lax.broadcasted_iota(jnp.int32, (16, D), 0)
    both = jnp.where(row == 0, gain_a, jnp.where(row == 1, gain_f[...], 0.0)).astype(BF)
    gains_ref[...] = dot(both, order[...]).astype(BF)


def run_project_back(parts, dq, x, dh1, gain_f, gain, order, wa, tables):
    tok = dq.shape[0]
    return call(
        project_back_kernel,
        [shape_of(tok, D, kind=F32), shape_of(tok, D), shape_of(tok, QW + 2 * KVW), shape_of(16, order.shape[1])],
        *parts, dq, x, dh1, gain_f, gain, order, *wa, *tables,
        flops=2 * tok * order.shape[1] * (2 * D + QW + 2 * KVW),
    )


def attention_grads_kernel(op0, op1, n0, n1, g0, g1, db_ref, dqkv_ref, keep_ref, send_ref):
    db, dqkv = db_ref[...], dqkv_ref[...]
    row = lax.broadcasted_iota(jnp.int32, (16, QKV - GAINS), 0)
    ones = (row == lax.broadcasted_iota(jnp.int32, (16, QKV - GAINS), 1)).astype(F32).astype(BF)
    for op, n, g, out in ((op0, n0, g0, keep_ref), (op1, n1, g1, send_ref)):
        out[:, WO:GAINS] = t_dot(op[...], db).astype(BF)
        out[:, GAINS:QKV] = t_dot(g[...], ones).astype(BF)
        out[:, QKV:COLUMNS] = t_dot(n[...], dqkv).astype(BF)
        out[:, COLUMNS:] = jnp.zeros((out.shape[0], WIDTH - COLUMNS), BF)


def run_attention_grads(op, db, n1, dqkv, gains):
    tok, rows = op.shape
    block = rows // 4

    def halves(height):
        return [pl.BlockSpec((height, block), lambda i: (0, i)), pl.BlockSpec((height, block), lambda i: (0, i + 2))]

    return call(
        attention_grads_kernel,
        [shape_of(rows // 2, WIDTH)] * 2,
        op, op, n1, n1, gains, gains, db, dqkv,
        flops=2 * tok * rows * COLUMNS,
        grid=(2,),
        in_specs=halves(tok) + halves(tok) + halves(16)
        + [pl.BlockSpec((tok, QW), lambda i: (0, 0)), pl.BlockSpec((tok, QW + 2 * KVW), lambda i: (0, 0))],
        out_specs=[pl.BlockSpec((block, WIDTH), lambda i: (i, 0))] * 2,
    )


def add_kernel(a, b, out):
    out[...] = (a[...].astype(F32) + b[...].astype(F32)).astype(BF)


def run_add(a, b):
    return call(add_kernel, [shape_of(*a.shape)], a, b)[0]


def split_sum_kernel(axis, *refs):
    pairs = len(refs) // 4
    for i in range(pairs):
        a, b = refs[2 * i : 2 * i + 2]
        keep, send = refs[2 * pairs + 2 * i : 2 * pairs + 2 * i + 2]
        total = (a[...].astype(F32) + b[...].astype(F32)).astype(BF)
        keep[...], send[...] = total[0], total[1]


def ffn_split_kernel(c_ref, gu_a, gu_b, down_a, down_b, *outs):
    c = c_ref[0]
    for a, b, out in ((gu_a, gu_b, outs[:4]), (down_a, down_b, outs[4:])):
        rows = a.shape[0] // 4
        for k in range(4):
            block = pl.ds(pl.multiple_of((c ^ k) * rows, rows), rows)
            out[k][...] = (a[block, :].astype(F32) + b[block, :].astype(F32)).astype(BF)


def run_ffn_split(c, gu_a, gu_b, down_a, down_b):
    out = [shape_of(v.shape[0] // 4, v.shape[1]) for v in (gu_a, down_a) for _ in range(4)]
    out = call(ffn_split_kernel, out, c, gu_a, gu_b, down_a, down_b)
    return out[:4], out[4:]


def ffn_total_kernel(*refs):
    for k in range(2):
        parts = refs[4 * k : 4 * k + 4]
        refs[8 + k][...] = sum(r[...].astype(F32) for r in parts).astype(BF)


def run_ffn_total(gu, down):
    return call(ffn_total_kernel, [shape_of(*gu[0].shape), shape_of(*down[0].shape)], *gu, *down)


def ffn_out_kernel(s_ref, c_ref, *refs):
    s, c = s_ref[0], c_ref[0]
    gu, gu_got, down, down_got, gate, up, whole = refs
    rows = gu.shape[0] // 4
    unit = down.shape[0] // 4
    first = s == 0
    for k in range(4):
        block = pl.ds(pl.multiple_of((c ^ k) * rows, rows), rows)
        a, b = (r[k * rows : (k + 1) * rows, :].astype(F32) for r in (gu, gu_got))
        gate[block, :] = jnp.where(first, a, b)
        up[block, :] = jnp.where(first, b, a)
        for half, r in ((s, down), (1 - s, down_got)):
            block = pl.ds(pl.multiple_of((half * 4 + (c ^ k)) * unit, unit), unit)
            whole[block, :] = r[k * unit : (k + 1) * unit, :].astype(F32)


def run_ffn_out(s, c, gu, gu_got, down, down_got):
    out = [shape_of(*gu.shape, kind=F32)] * 2 + [shape_of(2 * down.shape[0], down.shape[1], kind=F32)]
    return call(ffn_out_kernel, out, s, c, gu, gu_got, down, down_got)


def first_split_kernel(keep_ref, got_ref, a_keep, a_send, b_keep, b_send):
    total = (keep_ref[...].astype(F32) + got_ref[...].astype(F32)).astype(BF)
    for i in range(2):
        a_keep[i], a_send[i] = total[2 * i, :2], total[2 * i + 1, :2]
        b_keep[i], b_send[i] = total[i, 2:], total[2 + i, 2:]


def run_first_split(keep, got):
    shape = (4, 4, keep.shape[0] // 16, keep.shape[1])
    return call(
        first_split_kernel,
        [shape_of(2, 2, *shape[2:])] * 4,
        keep.reshape(shape), got.reshape(shape),
    )


def run_split_sum(a, a1, b, b1):
    out = [shape_of(*a.shape[1:])] * 2 + [shape_of(*b.shape[1:])] * 2
    return call(functools.partial(split_sum_kernel, 0), out, a, a1, b, b1)


def dp_split_kernel(a, a1, b, b1, own, s1, s2, s3):
    x = a[...].astype(F32) + a1[...].astype(F32)
    y = b[...].astype(F32) + b1[...].astype(F32)
    own[...] = x[0]
    s1[...], s2[...], s3[...] = x[1].astype(BF), y[0].astype(BF), y[1].astype(BF)


def run_dp_split(a, a1, b, b1):
    shape = a.shape[1:]
    return call(dp_split_kernel, [shape_of(*shape, kind=F32)] + [shape_of(*shape)] * 3, a, a1, b, b1)


def owner_sum_kernel(s_ref, *refs):
    now, later = (sum(r[...].astype(F32) for r in refs[k : k + 4]).astype(BF) for k in (0, 4))
    keep, send = refs[8:]
    first = s_ref[0] == 0
    keep[...] = jnp.where(first, now, later)
    send[...] = jnp.where(first, later, now)


def run_owner_sum(s, now, later):
    return call(owner_sum_kernel, [shape_of(*now[0].shape)] * 2, s, *now, *later)


def attention_out_kernel(order, u0, u1, u2, u3, wo, gains, wk, wv, wq):
    rows = jnp.concatenate([u[h] for u in (u0, u1, u2, u3) for h in range(2)], axis=0)
    out = dot(order[...], rows)
    wo[...] = out[:, WO:GAINS]
    gains[...] = out[:, GAINS:QKV]
    turned = lax.dot_general(
        rows[:, QKV : QKV + 2 * KVW], order[...], (((0,), (1,)), ((), ())), preferred_element_type=F32
    )
    wk[...], wv[...] = turned[:KVW], turned[KVW:]
    wq[...] = out[:, QKV + 2 * KVW : COLUMNS]


def run_attention_out(order, units):
    rows = order.shape[0]
    shapes = ((rows, QW), (rows, QKV - GAINS), (KVW, rows), (KVW, rows), (rows, QW))
    return call(
        attention_out_kernel,
        [shape_of(*shape, kind=F32) for shape in shapes],
        order, *units,
        flops=2 * rows * order.shape[1] * COLUMNS,
    )


def swap(x, axis, bit):
    return lax.ppermute(x, axis, [(i, i ^ bit) for i in range(lax.axis_size(axis))])


def spread(x, axis):
    return [x] + [swap(x, axis, k) for k in range(1, 4)]


def deliver(blocks, axis):
    return [blocks[0]] + [swap(b, axis, k) for k, b in enumerate(blocks[1:], 1)]


def pick(x, index, axis=0):
    return lax.dynamic_index_in_dim(x, index, axis, keepdims=False)


def tie(*values):
    return lax.optimization_barrier(values)


def plane_gather(a, b):
    a1, b1 = swap(a, "ctx", 2), swap(b, "ctx", 1)
    a2, b2 = swap(jnp.stack([a, a1]), "ctx", 1), swap(jnp.stack([b, b1]), "ctx", 2)
    return jnp.stack([a, a2[0], a1, a2[1]]), jnp.stack([b, b1, b2[0], b2[1]])


WO, GAINS, QKV = 0, QW, QW + 64
COLUMNS = QKV + QW + 2 * KVW
WIDTH = COLUMNS + 64
PAD = 256


def row_orders(s, c, d):
    p = jnp.arange(4 * PAD, dtype=jnp.int32)
    h, cc, zz, j = (p // 512) ^ s, (p // 128) % 4, (p // 32) % 4, p % 32
    orders = []
    for ci, zi in ((cc ^ c, zz ^ d), (cc, zz)):
        row = ci * 64 + h * 32 + j
        feature = jnp.where(row < D // 4, zi * (D // 4) + row, -1)
        orders.append((jnp.arange(D, dtype=jnp.int32)[:, None] == feature[None, :]).astype(BF))
    p = jnp.arange(PAD, dtype=jnp.int32)
    out = ((p // 64) ^ c) * 64 + (((p // 32) % 2) ^ s) * 32 + p % 32
    orders.append((jnp.arange(D // 4, dtype=jnp.int32)[:, None] == out[None, :]).astype(BF))
    return orders


def body_fast(
    block_input, out_grad, w_query, w_key, w_value, w_out, norm_attn, w_gate, w_up, w_down, norm_ffn
):
    s, c, d = (lax.axis_index(n) for n in ("section", "ctx", "dp"))
    s1, c1 = (i.astype(jnp.int32).reshape(1) for i in (s, c))
    tok = block_input.shape[2]
    cosine, sine = rope_tables(c * tok + jnp.arange(tok, dtype=jnp.int32))
    sign = jnp.where(jnp.arange(HEAD_DIM) < HEAD_DIM // 2, -1.0, 1.0)
    tables = (jnp.tile(cosine, (1, 2)), jnp.tile(sine * sign, (1, 2)))
    order0, order1, order_out = row_orders(s, c, d)
    x = pick(block_input[:, 0], s)
    g = pick(out_grad[:, 0], s)

    def by_layer(own, got):
        return jnp.where(s == 0, own, got), jnp.where(s == 0, got, own)

    def own_rows(w):
        return pick(jnp.pad(w, ((0, PAD - w.shape[0]), (0, 0))).reshape(4, 2, 32, w.shape[1]), c)

    gains = own_rows(jnp.stack([norm_attn[0], norm_ffn[0]], axis=1))
    gains = jnp.pad(gains, ((0, 0), (0, 0), (0, QKV - GAINS - 2)))
    own = [own_rows(w[0]) for w in (w_out, w_key, w_value, w_query)]
    own = jnp.concatenate([own[0], gains, *own[1:], jnp.zeros((2, 32, WIDTH - COLUMNS), BF)], axis=2)
    unit0, unit1 = by_layer(pick(own, s), swap(pick(own, 1 - s), "section", 1))
    ffn = [by_layer(w[0], swap(w[0], "section", 1)) for w in (w_gate, w_up, w_down)]
    gb1 = g.astype(BF)
    z, (ffn, order0, order1, order_out, tables, x, g, gb1, unit1) = tie(
        spread(unit0, "dp"), (ffn, order0, order1, order_out, tables, x, g, gb1, unit1)
    )

    def first_step(a, b):
        return a, swap(a, "ctx", 2), b, swap(b, "ctx", 1)

    def second_step(a, a1, b, b1):
        return a, a1, swap(jnp.stack([a, a1]), "ctx", 1), b, b1, swap(jnp.stack([b, b1]), "ctx", 2)

    def whole_half(a, a1, a2, b, b1, b2):
        a, b = jnp.stack([a, a2[0], a1, a2[1]]), jnp.stack([b, b1, b2[0], b2[1]])
        return jnp.concatenate([a, b], axis=1).reshape(512, WIDTH)

    steps = second_step(*first_step(jnp.stack(z[:2]), jnp.stack(z[2:])))
    mine, gb1_2, unit1 = tie(whole_half(*steps), swap(gb1, "dp", 2), unit1)
    wa0 = (mine, swap(mine, "section", 1))

    def nothing(*values):
        return values

    def forward(parts, wa, order, w, beside, values):
        x, n1, q, kv, gains = run_project(parts, order, wa, tables)
        kv, values = tie(spread(kv, "ctx"), beside[0](*values))
        o, op, lse, h1, n2 = run_attend(c1, x, q, kv, gains, order, wa)
        n2, values = tie(spread(n2, "dp"), beside[1](*values))
        gate, up, hidden, *parts = run_ffn(h1, n2, *w)
        if beside[2] is not None:
            parts, values = tie(deliver(parts, "dp"), beside[2](*values))
        return parts, (x, n1, q, kv, o, op, lse, h1, n2, gate, up, hidden, gains), values

    def backward(g, gb, kept, wa, order, w, beside, values, late):
        x, n1, q, kv, o, op, lse, h1, n2, gate, up, hidden, gains = kept
        dgate, dup, *parts = run_ffn_back(gb, gate, up, *w)
        parts = deliver(parts, "dp")
        values = beside[0](*values)
        gu_keep, gu_send, down_keep, down_send = run_ffn_grads(s1, dgate, dup, hidden, n2, gb)
        sums = run_ffn_split(c1, gu_keep, swap(gu_send, "section", 1), down_keep, swap(down_send, "section", 1))
        parts, sums, values = tie(parts, sums, values)
        sums = [deliver(v, "ctx") for v in sums]
        values = beside[1](*values)
        dh1, db, gain_f, dq, *dkv = run_attend_back(c1, parts, kv, h1, g, q, o, lse, gains, order, wa, tables)
        dkv, values, late = tie(dkv, values, late)
        dkv, values = tie(deliver(dkv, "ctx"), beside[2](*values))
        g, gb, dqkv, gains = run_project_back(dkv, dq, x, dh1, gain_f, gains, order, wa, tables)
        return g, gb, (op, db, n1, dqkv, gains), sums, values, late

    w0, w1 = ([pair[l] for pair in ffn] for l in range(2))
    parts, kept0, steps = forward(
        [x], wa0, order0, w0,
        (
            lambda unit: spread(unit, "dp"),
            lambda *z: first_step(jnp.stack(z[:2]), jnp.stack(z[2:])),
            second_step,
        ),
        (unit1,),
    )
    mine = whole_half(*steps)
    wa1 = (mine, swap(mine, "section", 1))
    out1, kept1, (gb1_1, gb1_3) = forward(
        parts, wa1, order0, w1, (lambda v: (swap(v, "dp", 1), swap(v, "dp", 3)), nothing, None), (gb1,)
    )
    out0 = kept1[0]
    gb = [gb1, gb1_1, gb1_2, gb1_3]
    in1, gb, operands, ffn1, out1, _ = backward(
        g, gb, kept1, wa1, order0, w1,
        (
            nothing,
            lambda own, p1, p2, p3: (own, swap(p1, "dp", 1), p2, swap(p3, "dp", 3)),
            nothing,
        ),
        out1, (),
    )
    gb, operands, ffn1 = tie(spread(gb, "dp"), operands, ffn1)
    ffn1 = [spread(v, "ctx") for v in run_ffn_total(*ffn1)]
    keep, send = run_attention_grads(*operands)
    gb, keep, send = tie(gb, keep, send)

    def scatter_first(a, a1, b, b1):
        return a, swap(a1, "ctx", 1), b, swap(b1, "ctx", 2)

    def scatter_second(a, a1, b, b1):
        return a, swap(a1, "ctx", 2), b, swap(b1, "ctx", 1)

    in0, _, operands, ffn0, later, ffn1 = backward(
        in1, gb, kept0, wa0, order0, w0,
        (
            lambda keep, got: scatter_first(*run_first_split(keep, got)),
            lambda *steps: scatter_second(*run_split_sum(*steps)),
            lambda *steps: deliver(run_dp_split(*steps), "dp"),
        ),
        (keep, swap(send, "section", 1)), ffn1,
    )
    keep, send = run_attention_grads(*operands)
    got, ffn0 = tie(swap(send, "section", 1), ffn0)
    steps = scatter_first(*run_first_split(keep, got))
    ffn0 = [spread(v, "ctx") for v in run_ffn_total(*ffn0)]
    steps, out1_2 = tie(steps, swap(out1[2], "dp", 2))
    out1 = out1[0] + sum(p.astype(F32) for p in (out1[1], out1_2, out1[3]))
    blocks = run_dp_split(*scatter_second(*run_split_sum(*steps)))
    blocks, ffn0 = tie(deliver(blocks, "dp"), ffn0)
    keep, send = run_owner_sum(s1, blocks, later)
    unit = jnp.stack([keep, swap(send, "section", 1)])
    (gu, gu_send), (down, down_send) = (
        by_layer(jnp.concatenate(a, axis=0), jnp.concatenate(b, axis=0)) for a, b in zip(ffn0, ffn1)
    )
    gate, up, down = run_ffn_out(s1, c1, gu, swap(gu_send, "section", 1), down, swap(down_send, "section", 1))
    units, gate, up, down = tie(spread(unit, "ctx"), gate, up, down)
    wo, gains, wk, wv, wq = run_attention_out(order_out, units)

    def own_layer(p0, p1):
        keep, send = by_layer(p0, p1)
        got = swap(send, "section", 1)
        return jnp.stack(by_layer(keep, got))

    return (
        own_layer(out0, out1)[None, :, None],
        own_layer(in0, in1)[None, :, None],
        wq[None],
        wk.T[None],
        wv.T[None],
        wo[None],
        gains[None, :, 0],
        gate[None],
        up[None],
        down[None],
        gains[None, :, 1],
    )


def body(*args):
    sizes = [lax.axis_size(name) for name in ("section", "ctx", "dp")]
    return (body_fast if sizes == [2, 4, 4] else body_plain)(*args)


def solution(mesh):
    return jax.shard_map(
        body,
        mesh=mesh,
        in_specs=(
            P(None, "dp", "ctx", None),
            P(None, "dp", "ctx", None),
            P("section", "dp", None),
            P("section", "dp", None),
            P("section", "dp", None),
            P("section", "dp", None),
            P("section", "dp"),
            P("section", None, "dp"),
            P("section", None, "dp"),
            P("section", "dp", None),
            P("section", "dp"),
        ),
        out_specs=(
            P("section", None, "dp", "ctx", None),
            P("section", None, "dp", "ctx", None),
            P("section", "dp", None),
            P("section", "dp", None),
            P("section", "dp", None),
            P("section", "dp", None),
            P("section", "dp"),
            P("section", None, "dp"),
            P("section", None, "dp"),
            P("section", "dp", None),
            P("section", "dp"),
        ),
        check_vma=False,
    )
```

```python
import functools
import math

import jax
import jax.numpy as jnp
from jax import lax
from jax.experimental import pallas as pl
from jax.experimental.pallas import tpu as pltpu
from jax.sharding import PartitionSpec as P

D = 960
HEADS = 15
KV_HEADS = 5
HEAD_DIM = 64
QW = 960
KVW = 320
GROUP = 3
EPSILON = 1e-05
ROPE_BASE = 10000.0
MASKED = -1e30
BF = jnp.bfloat16
F32 = jnp.float32


def dot(a, b):
    return jnp.dot(a, b, preferred_element_type=F32)


def rope_tables(positions):
    half_dim = HEAD_DIM // 2
    freq_rows = ROPE_BASE ** (-(jnp.arange(half_dim, dtype=F32) * 2.0 / HEAD_DIM))
    angles = positions.astype(F32)[:, None] * freq_rows[None, :]
    cosine = jnp.concatenate([jnp.cos(angles), jnp.cos(angles)], axis=1)
    sine_rows = jnp.concatenate([jnp.sin(angles), jnp.sin(angles)], axis=1)
    return (cosine, sine_rows)


def turn_half(u):
    half_dim = HEAD_DIM // 2
    return jnp.concatenate([-u[..., half_dim:], u[..., :half_dim]], axis=-1)


def rotate(u, cosine, sine_rows):
    return u * cosine[:, None, :] + turn_half(u) * sine_rows[:, None, :]


def unrotate(u, cosine, sine_rows):
    return u * cosine[:, None, :] - turn_half(u * sine_rows[:, None, :])


def normalize(x, gain):
    inverse = lax.rsqrt(jnp.mean(x * x, axis=-1, keepdims=True) + EPSILON)
    return (x * inverse * gain, inverse)


def normalize_back(x, inverse, gain, grad):
    scaled = grad * gain
    gain_grad = jnp.sum(grad * x * inverse, axis=0)
    value_grad = inverse * scaled - x * inverse**3 * jnp.mean(scaled * x, axis=-1, keepdims=True)
    return (value_grad, gain_grad)


def attend(q, k, v, query_pos):
    tok = q.shape[0]
    q = q.reshape(tok, KV_HEADS, GROUP, HEAD_DIM)
    scores = jnp.einsum("tkgd,skd->kgts", q, k, preferred_element_type=F32) * HEAD_DIM**-0.5
    allowed = query_pos[:, None] >= jnp.arange(k.shape[0], dtype=jnp.int32)[None, :]
    scores = jnp.where(allowed, scores, MASKED)
    peak = jnp.max(scores, axis=-1, keepdims=True)
    e = jnp.exp(scores - peak)
    total = jnp.sum(e, axis=-1, keepdims=True)
    probs = (e / total).astype(BF)
    o = jnp.einsum("kgts,skd->tkgd", probs, v, preferred_element_type=F32).reshape(tok, QW)
    return o.astype(BF), (peak + jnp.log(total))[..., 0]


def attend_back(q, k, v, lse, do, o, query_pos):
    tok = q.shape[0]
    q = q.reshape(tok, KV_HEADS, GROUP, HEAD_DIM)
    dor = do.reshape(tok, KV_HEADS, GROUP, HEAD_DIM)
    delta = jnp.sum((do.astype(F32) * o.astype(F32)).reshape(tok, KV_HEADS, GROUP, HEAD_DIM), axis=-1)
    delta = jnp.transpose(delta, (1, 2, 0))
    scale = HEAD_DIM**-0.5
    scores = jnp.einsum("tkgd,skd->kgts", q, k, preferred_element_type=F32) * scale
    allowed = query_pos[:, None] >= jnp.arange(k.shape[0], dtype=jnp.int32)[None, :]
    probs = jnp.where(allowed, jnp.exp(scores - lse[..., None]), 0.0)
    dv = jnp.einsum("kgts,tkgd->skd", probs.astype(BF), dor, preferred_element_type=F32)
    dp = jnp.einsum("tkgd,skd->kgts", dor, v, preferred_element_type=F32)
    ds = (probs * (dp - delta[..., None])).astype(BF)
    dq = jnp.einsum("kgts,skd->tkgd", ds, k, preferred_element_type=F32) * scale
    dk = jnp.einsum("kgts,tkgd->skd", ds, q, preferred_element_type=F32) * scale
    dkv = jnp.concatenate([dk.reshape(-1, KVW), dv.reshape(-1, KVW)], axis=1)
    return dq.reshape(tok, HEADS, HEAD_DIM), dkv


def layer_forward(x, w, cosine, sine, query_pos):
    wa, wg, wu, wd, ga, gf = w
    tok = x.shape[0]
    n1, r1 = normalize(x, ga)
    n1 = n1.astype(BF)
    qkv = dot(n1, wa[:, : QW + 2 * KVW])
    q = rotate(qkv[:, :QW].reshape(tok, HEADS, HEAD_DIM), cosine, sine).astype(BF)
    k = rotate(qkv[:, QW : QW + KVW].reshape(tok, KV_HEADS, HEAD_DIM), cosine, sine)
    kv = jnp.concatenate([k.reshape(tok, KVW), qkv[:, QW + KVW :]], axis=1).astype(BF)
    kv = lax.all_gather(kv, "ctx", axis=0, tiled=True)
    k = kv[:, :KVW].reshape(-1, KV_HEADS, HEAD_DIM)
    v = kv[:, KVW:].reshape(-1, KV_HEADS, HEAD_DIM)
    o, lse = attend(q, k, v, query_pos)
    h1 = x + dot(o, wa[:, QW + 2 * KVW :])
    n2, r2 = normalize(h1, gf)
    n2 = lax.all_gather(n2.astype(BF), "dp", axis=0, tiled=True)
    gate = dot(n2, wg)
    up = dot(n2, wu)
    hidden = (jax.nn.silu(gate) * up).astype(BF)
    part = dot(hidden, wd).astype(BF)
    out = h1 + lax.psum_scatter(part, "dp", scatter_dimension=0, tiled=True).astype(F32)
    return out, (x, n1, r1, q, k, v, o, lse, h1, n2, r2, gate, up, hidden)


def layer_backward(g, kept, w, cosine, sine, query_pos):
    wa, wg, wu, wd, ga, gf = w
    x, n1, r1, q, k, v, o, lse, h1, n2, r2, gate, up, hidden = kept
    tok = x.shape[0]
    gb = lax.all_gather(g.astype(BF), "dp", axis=0, tiled=True)
    grad_down = dot(hidden.T, gb)
    dh = dot(gb, wd.T)
    sigma = jax.nn.sigmoid(gate)
    dgate = (dh * up * sigma * (1.0 + gate * (1.0 - sigma))).astype(BF)
    dup = (dh * gate * sigma).astype(BF)
    grad_gate = dot(n2.T, dgate)
    grad_up = dot(n2.T, dup)
    part = (dot(dgate, wg.T) + dot(dup, wu.T)).astype(BF)
    dn2 = lax.psum_scatter(part, "dp", scatter_dimension=0, tiled=True).astype(F32)
    back_f, gain_f = normalize_back(h1, r2, gf, dn2)
    dh1 = g + back_f
    db = dh1.astype(BF)
    grad_out = dot(o.T, db)
    do = dot(db, wa[:, QW + 2 * KVW :].T).astype(BF)
    dq, dkv = attend_back(q, k, v, lse, do, o, query_pos)
    dkv = lax.psum_scatter(dkv.astype(BF), "ctx", scatter_dimension=0, tiled=True).astype(F32)
    dq = unrotate(dq, cosine, sine).reshape(tok, QW)
    dk = unrotate(dkv[:, :KVW].reshape(tok, KV_HEADS, HEAD_DIM), cosine, sine).reshape(tok, KVW)
    dqkv = jnp.concatenate([dq, dk, dkv[:, KVW:]], axis=1).astype(BF)
    grad_qkv = dot(n1.T, dqkv)
    dn1 = dot(dqkv, wa[:, : QW + 2 * KVW].T)
    back_a, gain_a = normalize_back(x, r1, ga, dn1)
    grads = (
        jnp.concatenate([grad_qkv, grad_out], axis=1).astype(BF),
        jnp.stack([gain_a, gain_f]),
        grad_gate.astype(BF),
        grad_up.astype(BF),
        grad_down.astype(BF),
    )
    return dh1 + back_a, grads


def swap_section(p0, p1, section_id):
    mine = jnp.where(section_id == 0, p0, p1)
    other = jnp.where(section_id == 0, p1, p0)
    count = lax.axis_size("section")
    got = lax.ppermute(other, "section", [(i, count - 1 - i) for i in range(count)])
    return mine.astype(F32) + got.astype(F32)


def own_layer(p0, p1, section_id):
    mine = jnp.where(section_id == 0, p0, p1)
    other = jnp.where(section_id == 0, p1, p0)
    count = lax.axis_size("section")
    got = lax.ppermute(other, "section", [(i, count - 1 - i) for i in range(count)])
    first = jnp.where(section_id == 0, mine, got)
    second = jnp.where(section_id == 0, got, mine)
    return jnp.stack([first, second])


def body_plain(
    block_input, out_grad, w_query, w_key, w_value, w_out, norm_attn, w_gate, w_up, w_down, norm_ffn
):
    section_id = lax.axis_index("section")
    tok_rows = block_input.shape[2]
    query_pos = lax.axis_index("ctx") * tok_rows + jnp.arange(tok_rows, dtype=jnp.int32)
    cosine, sine = rope_tables(query_pos)
    x = lax.dynamic_index_in_dim(block_input[:, 0], section_id, 0, keepdims=False)
    g = lax.dynamic_index_in_dim(out_grad[:, 0], section_id, 0, keepdims=False)
    wa = jnp.concatenate([w_query[0], w_key[0], w_value[0], w_out[0]], axis=1)
    wa = lax.all_gather(lax.all_gather(wa, "dp", axis=0, tiled=True), "section")
    gains = jnp.stack([norm_attn[0], norm_ffn[0]])
    gains = lax.all_gather(lax.all_gather(gains, "dp", axis=1, tiled=True), "section").astype(F32)
    wg = lax.all_gather(w_gate[0], "section")
    wu = lax.all_gather(w_up[0], "section")
    wd = lax.all_gather(w_down[0], "section")
    layers = [(wa[l], wg[l], wu[l], wd[l], gains[l, 0], gains[l, 1]) for l in range(2)]
    out0, kept0 = layer_forward(x, layers[0], cosine, sine, query_pos)
    out1, kept1 = layer_forward(out0, layers[1], cosine, sine, query_pos)
    in1, grads1 = layer_backward(g, kept1, layers[1], cosine, sine, query_pos)
    in0, grads0 = layer_backward(in1, kept0, layers[0], cosine, sine, query_pos)
    section_outs = own_layer(out0, out1, section_id)
    in_grads = own_layer(in0, in1, section_id)
    ga, gn, gg, gu, gd = (
        swap_section(a, b, section_id) for a, b in zip(grads0, grads1)
    )
    ga = lax.psum_scatter(ga.astype(BF), "dp", scatter_dimension=0, tiled=True)
    ga = lax.psum(ga, "ctx").astype(F32)
    gn = lax.psum_scatter(gn, "dp", scatter_dimension=1, tiled=True)
    gn = lax.psum(gn, "ctx")
    gg = lax.psum(gg.astype(BF), "ctx").astype(F32)
    gu = lax.psum(gu.astype(BF), "ctx").astype(F32)
    gd = lax.psum(gd.astype(BF), "ctx").astype(F32)
    return (
        section_outs[None, :, None],
        in_grads[None, :, None],
        ga[None, :, :QW],
        ga[None, :, QW : QW + KVW],
        ga[None, :, QW + KVW : QW + 2 * KVW],
        ga[None, :, QW + 2 * KVW :],
        gn[None, 0],
        gg[None],
        gu[None],
        gd[None],
        gn[None, 1],
    )


def t_dot(a, b):
    return lax.dot_general(a, b, (((0,), (0,)), ((), ())), preferred_element_type=F32)


def dot_t(a, b):
    return lax.dot_general(a, b, (((1,), (1,)), ((), ())), preferred_element_type=F32)


def shape_of(*dims, kind=BF):
    return jax.ShapeDtypeStruct(dims, kind)


def call(kernel, out_shape, *args, flops=0, grid=None, in_specs=None, out_specs=None, scratch=()):
    moved = sum(math.prod(a.shape) * a.dtype.itemsize for a in list(args) + list(out_shape))
    kwargs = {} if grid is None else {"grid": grid}
    held = moved + sum(math.prod(m.shape) * 4 for m in scratch)
    vmem = pl.BlockSpec(memory_space=pltpu.VMEM)
    smem = pl.BlockSpec(memory_space=pltpu.SMEM)
    return pl.pallas_call(
        kernel,
        out_shape=out_shape,
        in_specs=in_specs or [smem if a.dtype == jnp.int32 else vmem for a in args],
        out_specs=out_specs or [vmem] * len(out_shape),
        scratch_shapes=scratch,
        cost_estimate=pl.CostEstimate(flops=flops, bytes_accessed=moved, transcendentals=0),
        compiler_params=pltpu.CompilerParams(vmem_limit_bytes=min(60 << 20, held * 9 // 8 + (8 << 20))),
        **kwargs,
    )(*args)


def turn(u, cosine, sine, sign, first, last):
    rows, width = u.shape
    padded = -(-width // 128) * 128
    if padded > width:
        u = jnp.concatenate([u, jnp.zeros((rows, padded - width), F32)], axis=1)
    lane = lax.broadcasted_iota(jnp.int32, (rows, padded), 1)
    partner = jnp.where(
        lane % HEAD_DIM < HEAD_DIM // 2,
        pltpu.roll(u, padded - HEAD_DIM // 2, 1),
        pltpu.roll(u, HEAD_DIM // 2, 1),
    )
    cosine = jnp.concatenate([cosine] * (padded // 128), axis=1)
    sine = jnp.concatenate([sine] * (padded // 128), axis=1)
    turned = u * cosine + (partner * sine if sign > 0 else -(partner * sine))
    return jnp.where((lane >= first) & (lane < last), turned, u)[:, :width]


def inverse_norm(x):
    return lax.rsqrt(jnp.mean(x * x, axis=-1, keepdims=True) + EPSILON)


def project_kernel(count, *refs):
    parts, (order, w0, w1, cosine, sine, x_ref, n_ref, q_ref, kv_ref, gain_ref) = refs[:count], refs[count:]
    columns = jnp.concatenate([w0[:, GAINS:QKV], w1[:, GAINS:QKV]], axis=0)
    gains = lax.dot_general(columns, order[...], (((0,), (1,)), ((), ())), preferred_element_type=F32)
    gain_ref[...] = gains[:8]
    x = parts[0][...]
    for part in parts[1:]:
        x = x + part[...].astype(F32)
    x_ref[...] = x
    n = (x * inverse_norm(x) * gains[:1]).astype(BF)
    n = dot(n, order[...]).astype(BF)
    n_ref[...] = n
    half = w0.shape[0]
    out = dot(n[:, :half], w0[:, QKV:COLUMNS]) + dot(n[:, half:], w1[:, QKV:COLUMNS])
    kv = turn(out[:, : 2 * KVW], cosine[...], sine[...], 1, 0, KVW)
    kv_ref[...] = kv.astype(BF)
    q_ref[...] = turn(out[:, 2 * KVW :], cosine[...], sine[...], 1, 0, QW).astype(BF)


def run_project(parts, order, wa, tables):
    tok = parts[0].shape[0]
    args = list(parts) + [order, *wa, *tables]
    return call(
        functools.partial(project_kernel, len(parts)),
        [
            shape_of(tok, D, kind=F32),
            shape_of(tok, order.shape[1]),
            shape_of(tok, QW),
            shape_of(tok, 2 * KVW),
            shape_of(8, D, kind=F32),
        ],
        *args,
        flops=2 * tok * order.shape[1] * (D + QW + 2 * KVW),
    )


def causal(c, tok, count):
    shape = (GROUP * tok, count * tok)
    row = c * tok + lax.broadcasted_iota(jnp.int32, shape, 0) % tok
    lane = lax.broadcasted_iota(jnp.int32, shape, 1)
    key = jnp.zeros(shape, jnp.int32)
    for k in range(count):
        key = jnp.where(lane // tok == k, (c ^ k) * tok + lane % tok, key)
    return row >= key


def heads_of(x, j):
    return jnp.concatenate(
        [x[:, (GROUP * j + g) * HEAD_DIM : (GROUP * j + g + 1) * HEAD_DIM] for g in range(GROUP)], axis=0
    )


def attend_kernel(c_ref, x_ref, q_ref, kv0, kv1, kv2, kv3, gain, order, w0, w1, o_ref, op_ref, lse_ref, h_ref, n_ref):
    tok = q_ref.shape[0]
    kv = jnp.concatenate([kv0[...], kv1[...], kv2[...], kv3[...]], axis=0)
    q = q_ref[...]
    allowed = causal(c_ref[0], tok, 4)
    for j in range(KV_HEADS):
        k = kv[:, j * HEAD_DIM : (j + 1) * HEAD_DIM]
        v = kv[:, KVW + j * HEAD_DIM : KVW + (j + 1) * HEAD_DIM]
        scores = jnp.where(allowed, dot_t(heads_of(q, j), k) * HEAD_DIM**-0.5, MASKED)
        peak = jnp.max(scores, axis=-1, keepdims=True)
        e = jnp.exp(scores - peak)
        total = jnp.sum(e, axis=-1, keepdims=True)
        o = dot((e * (1.0 / total)).astype(BF), v).astype(BF)
        lse = peak + jnp.log(total)
        for g in range(GROUP):
            h = GROUP * j + g
            o_ref[:, h * HEAD_DIM : (h + 1) * HEAD_DIM] = o[g * tok : (g + 1) * tok]
            lse_ref[:, h : h + 1] = lse[g * tok : (g + 1) * tok]
    op = dot(o_ref[...], order[...]).astype(BF)
    op_ref[...] = op
    half = w0.shape[0]
    h1 = x_ref[...] + dot(op[:, :half], w0[:, WO:GAINS]) + dot(op[:, half:], w1[:, WO:GAINS])
    h_ref[...] = h1
    n_ref[...] = (h1 * inverse_norm(h1) * gain[1:2]).astype(BF)


def run_attend(c, x, q, kv, gain, order, wa):
    tok = q.shape[0]
    return call(
        attend_kernel,
        [
            shape_of(tok, QW),
            shape_of(tok, order.shape[1]),
            shape_of(tok, 16, kind=F32),
            shape_of(tok, D, kind=F32),
            shape_of(tok, D),
        ],
        c, x, q, *kv, gain, order, *wa,
        flops=2 * tok * (4 * tok * QW * 2 + order.shape[1] * D * 2),
    )


def token_rows(d_ref, *refs):
    if len(refs) == 1:
        d = d_ref[0]
        return jnp.concatenate([refs[0][d ^ k] for k in range(4)], axis=0)
    return jnp.concatenate([r[...] for r in refs], axis=0)


def ffn_kernel(d_ref, h_ref, n_ref, wg, wu, wd, gate_ref, up_ref, hidden_ref, p0, p1, p2, p3):
    n = token_rows(d_ref, n_ref)
    gate, up = dot(n, wg[...]), dot(n, wu[...])
    gate_ref[...], up_ref[...] = gate, up
    hidden = (gate * (1.0 / (1.0 + jnp.exp(-gate))) * up).astype(BF)
    hidden_ref[...] = hidden
    part = dot(hidden, wd[...])
    tok = h_ref.shape[0]
    p0[...] = h_ref[...] + part[:tok]
    for k, p in enumerate((p1, p2, p3), 1):
        p[...] = part[k * tok : (k + 1) * tok].astype(BF)


def run_ffn(d, h1, n2, wg, wu, wd):
    tok, width = h1.shape[0], wg.shape[1]
    return call(
        ffn_kernel,
        [shape_of(4 * tok, width, kind=F32)] * 2
        + [shape_of(4 * tok, width), shape_of(tok, D, kind=F32)]
        + [shape_of(tok, D)] * 3,
        d, h1, n2, wg, wu, wd,
        flops=6 * 4 * tok * width * D,
    )


def ffn_back_kernel(d_ref, *refs):
    gate_ref, up_ref, wg, wu, wd, dgate_ref, dup_ref, p0, p1, p2, p3 = refs[-11:]
    gb = token_rows(d_ref, *refs[:-11])
    dh = dot_t(gb, wd[...])
    gate, up = gate_ref[...], up_ref[...]
    sigma = 1.0 / (1.0 + jnp.exp(-gate))
    dgate = (dh * up * sigma * (1.0 + gate * (1.0 - sigma))).astype(BF)
    dup = (dh * gate * sigma).astype(BF)
    dgate_ref[...], dup_ref[...] = dgate, dup
    part = dot_t(dgate, wg[...]) + dot_t(dup, wu[...])
    tok = p0.shape[0]
    p0[...] = part[:tok]
    for k, p in enumerate((p1, p2, p3), 1):
        p[...] = part[k * tok : (k + 1) * tok].astype(BF)


def run_ffn_back(d, gb, gate, up, wg, wu, wd):
    tok, width = gate.shape[0] // 4, wg.shape[1]
    return call(
        ffn_back_kernel,
        [shape_of(4 * tok, width)] * 2 + [shape_of(tok, D, kind=F32)] + [shape_of(tok, D)] * 3,
        d, *gb, gate, up, wg, wu, wd,
        flops=6 * 4 * tok * width * D,
    )


def ffn_grads_kernel(s_ref, d_ref, dgate, dup, hidden, n_ref, *refs):
    n, gb = token_rows(d_ref, n_ref), token_rows(d_ref, *refs[:-5])
    gu_keep, gu_send, down_keep, down_send, down = refs[-5:]
    s = s_ref[0]
    a, b = dgate[...], dup[...]
    first = s == 0
    gu_keep[...] = t_dot(n, jnp.where(first, a, b)).astype(BF)
    gu_send[...] = t_dot(n, jnp.where(first, b, a)).astype(BF)
    down[...] = t_dot(hidden[...], gb)
    half = down.shape[0] // 2
    down_keep[...] = down[pl.ds(pl.multiple_of(s * half, half), half), :].astype(BF)
    down_send[...] = down[pl.ds(pl.multiple_of((1 - s) * half, half), half), :].astype(BF)


def run_ffn_grads(s, d, dgate, dup, hidden, n2, gb):
    tok, width = dgate.shape
    return call(
        ffn_grads_kernel,
        [shape_of(D, width)] * 2 + [shape_of(width // 2, D)] * 2,
        s, d, dgate, dup, hidden, n2, *gb,
        flops=6 * tok * width * D,
        scratch=[pltpu.VMEM((width, D), F32)],
    )


def attend_back_kernel(c_ref, *refs):
    parts, kv_refs = refs[:4], refs[4:8]
    h_ref, g_ref, q_ref, o_ref, lse_ref, gain, order, w0, w1, cosine, sine = refs[8:19]
    dh_ref, db_ref, gain_ref, dq_ref, d0, d1, d2, d3, dq_acc, dkv_acc = refs[19:]
    tok = q_ref.shape[0]
    dn = parts[0][...]
    for part in parts[1:]:
        dn = dn + part[...].astype(F32)
    h1 = h_ref[...]
    inverse = inverse_norm(h1)
    gain_ref[...] = jnp.sum(dn * h1 * inverse, axis=0, keepdims=True)
    scaled = dn * gain[1:2]
    dh = g_ref[...] + inverse * scaled - h1 * inverse**3 * jnp.mean(scaled * h1, axis=-1, keepdims=True)
    dh_ref[...] = dh
    db = dh.astype(BF)
    db_ref[...] = db
    dop = jnp.concatenate([dot_t(db, w0[:, WO:GAINS]), dot_t(db, w1[:, WO:GAINS])], axis=1).astype(BF)
    do = dot_t(dop, order[...]).astype(BF)
    kv = jnp.concatenate([r[...] for r in kv_refs], axis=0)
    q, o, lse_all = q_ref[...], o_ref[...], lse_ref[...]
    allowed = causal(c_ref[0], tok, 4)
    scale = HEAD_DIM**-0.5
    for j in range(KV_HEADS):
        k = kv[:, j * HEAD_DIM : (j + 1) * HEAD_DIM]
        v = kv[:, KVW + j * HEAD_DIM : KVW + (j + 1) * HEAD_DIM]
        qj, doj = heads_of(q, j), heads_of(do, j)
        delta = jnp.sum(doj.astype(F32) * heads_of(o, j).astype(F32), axis=-1, keepdims=True)
        lse = jnp.concatenate([lse_all[:, GROUP * j + g : GROUP * j + g + 1] for g in range(GROUP)], axis=0)
        probs = jnp.where(allowed, jnp.exp(dot_t(qj, k) * scale - lse), 0.0)
        dkv_acc[:, KVW + j * HEAD_DIM : KVW + (j + 1) * HEAD_DIM] = t_dot(probs.astype(BF), doj)
        ds = (probs * (dot_t(doj, v) - delta)).astype(BF)
        dkv_acc[:, j * HEAD_DIM : (j + 1) * HEAD_DIM] = t_dot(ds, qj) * scale
        dq = dot(ds, k) * scale
        for g in range(GROUP):
            h = GROUP * j + g
            dq_acc[:, h * HEAD_DIM : (h + 1) * HEAD_DIM] = dq[g * tok : (g + 1) * tok]
    dq_ref[...] = turn(dq_acc[...], cosine[...], sine[...], -1, 0, QW).astype(BF)
    d0[...] = dkv_acc[:tok]
    for k, d in enumerate((d1, d2, d3), 1):
        d[...] = dkv_acc[k * tok : (k + 1) * tok].astype(BF)


def run_attend_back(c, parts, kv, h1, g, q, o, lse, gain, order, wa, tables):
    tok = q.shape[0]
    return call(
        attend_back_kernel,
        [
            shape_of(tok, D, kind=F32),
            shape_of(tok, D),
            shape_of(1, D, kind=F32),
            shape_of(tok, QW),
            shape_of(tok, 2 * KVW, kind=F32),
        ]
        + [shape_of(tok, 2 * KVW)] * 3,
        c, *parts, *kv, h1, g, q, o, lse, gain, order, *wa, *tables,
        flops=2 * tok * (4 * tok * QW * 5 + order.shape[1] * D * 2),
        scratch=[pltpu.VMEM((tok, QW), F32), pltpu.VMEM((4 * tok, 2 * KVW), F32)],
    )


def project_back_kernel(*refs):
    parts, refs = refs[:4], refs[4:]
    dq_ref, x_ref, dh_ref, gain_f, gain, order, w0, w1, cosine, sine = refs[:10]
    in_ref, gb_ref, dqkv_ref, gains_ref = refs[10:]
    dkv = parts[0][...]
    for part in parts[1:]:
        dkv = dkv + part[...].astype(F32)
    dkv = turn(dkv, cosine[...], sine[...], -1, 0, KVW).astype(BF)
    dqkv_ref[:, : 2 * KVW] = dkv
    dqkv_ref[:, 2 * KVW :] = dq_ref[...]
    dqkv = dqkv_ref[...]
    ds = jnp.concatenate([dot_t(dqkv, w0[:, QKV:COLUMNS]), dot_t(dqkv, w1[:, QKV:COLUMNS])], axis=1)
    high = ds.astype(BF)
    low = (ds - high.astype(F32)).astype(BF)
    dn = dot_t(high, order[...]) + dot_t(low, order[...])
    x = x_ref[...]
    inverse = inverse_norm(x)
    gain_a = jnp.sum(dn * x * inverse, axis=0, keepdims=True)
    scaled = dn * gain[:1]
    out = dh_ref[...] + inverse * scaled - x * inverse**3 * jnp.mean(scaled * x, axis=-1, keepdims=True)
    in_ref[...] = out
    gb_ref[...] = out.astype(BF)
    row = lax.broadcasted_iota(jnp.int32, (16, D), 0)
    both = jnp.where(row == 0, gain_a, jnp.where(row == 1, gain_f[...], 0.0)).astype(BF)
    gains_ref[...] = dot(both, order[...]).astype(BF)


def run_project_back(parts, dq, x, dh1, gain_f, gain, order, wa, tables):
    tok = dq.shape[0]
    return call(
        project_back_kernel,
        [shape_of(tok, D, kind=F32), shape_of(tok, D), shape_of(tok, QW + 2 * KVW), shape_of(16, order.shape[1])],
        *parts, dq, x, dh1, gain_f, gain, order, *wa, *tables,
        flops=2 * tok * order.shape[1] * (2 * D + QW + 2 * KVW),
    )


def attention_grads_kernel(op0, op1, n0, n1, g0, g1, db_ref, dqkv_ref, keep_ref, send_ref):
    db, dqkv = db_ref[...], dqkv_ref[...]
    row = lax.broadcasted_iota(jnp.int32, (16, QKV - GAINS), 0)
    ones = (row == lax.broadcasted_iota(jnp.int32, (16, QKV - GAINS), 1)).astype(F32).astype(BF)
    for op, n, g, out in ((op0, n0, g0, keep_ref), (op1, n1, g1, send_ref)):
        out[:, WO:GAINS] = t_dot(op[...], db).astype(BF)
        out[:, GAINS:QKV] = t_dot(g[...], ones).astype(BF)
        out[:, QKV:COLUMNS] = t_dot(n[...], dqkv).astype(BF)
        out[:, COLUMNS:] = jnp.zeros((out.shape[0], WIDTH - COLUMNS), BF)


def run_attention_grads(op, db, n1, dqkv, gains):
    tok, rows = op.shape
    block = rows // 4

    def halves(height):
        return [pl.BlockSpec((height, block), lambda i: (0, i)), pl.BlockSpec((height, block), lambda i: (0, i + 2))]

    return call(
        attention_grads_kernel,
        [shape_of(rows // 2, WIDTH)] * 2,
        op, op, n1, n1, gains, gains, db, dqkv,
        flops=2 * tok * rows * COLUMNS,
        grid=(2,),
        in_specs=halves(tok) + halves(tok) + halves(16)
        + [pl.BlockSpec((tok, QW), lambda i: (0, 0)), pl.BlockSpec((tok, QW + 2 * KVW), lambda i: (0, 0))],
        out_specs=[pl.BlockSpec((block, WIDTH), lambda i: (i, 0))] * 2,
    )


def add_kernel(a, b, out):
    out[...] = (a[...].astype(F32) + b[...].astype(F32)).astype(BF)


def run_add(a, b):
    return call(add_kernel, [shape_of(*a.shape)], a, b)[0]


def split_sum_kernel(axis, *refs):
    pairs = len(refs) // 4
    for i in range(pairs):
        a, b = refs[2 * i : 2 * i + 2]
        keep, send = refs[2 * pairs + 2 * i : 2 * pairs + 2 * i + 2]
        total = (a[...].astype(F32) + b[...].astype(F32)).astype(BF)
        keep[...], send[...] = total[0], total[1]


def pack(gu, down, out):
    rows, width = gu.shape
    unit = down.shape[0]
    out[:rows, :] = gu
    out[rows : rows + unit, :] = down[:, :width]
    out[rows + unit :, : width // 2] = down[: unit // 2, width:]
    out[rows + unit :, width // 2 :] = down[unit // 2 :, width:]


def unpack(packed, rows, unit):
    packed = packed.astype(F32)
    width = packed.shape[1]
    tail = packed[rows + unit :]
    tail = jnp.concatenate([tail[:, : width // 2], tail[:, width // 2 :]], axis=0)
    return packed[:rows], jnp.concatenate([packed[rows : rows + unit], tail], axis=1)


def ffn_split_kernel(c_ref, gu_a, gu_b, down_a, down_b, *outs):
    c = c_ref[0]
    for k, out in enumerate(outs):
        sums = []
        for a, b in ((gu_a, gu_b), (down_a, down_b)):
            rows = a.shape[0] // 4
            block = pl.ds(pl.multiple_of((c ^ k) * rows, rows), rows)
            sums.append((a[block, :].astype(F32) + b[block, :].astype(F32)).astype(BF))
        pack(*sums, out)


def run_ffn_split(c, gu_a, gu_b, down_a, down_b):
    width = gu_a.shape[1]
    rows = (gu_a.size + down_a.size) // (4 * width)
    return call(ffn_split_kernel, [shape_of(rows, width)] * 4, c, gu_a, gu_b, down_a, down_b)


def ffn_total_kernel(*refs):
    refs[4][...] = sum(r[...].astype(F32) for r in refs[:4]).astype(BF)


def run_ffn_total(blocks):
    return call(ffn_total_kernel, [shape_of(*blocks[0].shape)], *blocks)[0]


def ffn_pick_kernel(s_ref, *refs):
    first = s_ref[0] == 0
    rows = refs[0].shape[0]
    keep, send = refs[8:]
    for k in range(4):
        a, b = refs[k][...], refs[4 + k][...]
        keep[k * rows : (k + 1) * rows, :] = jnp.where(first, a, b)
        send[k * rows : (k + 1) * rows, :] = jnp.where(first, b, a)


def run_ffn_pick(s, layer0, layer1):
    rows, width = layer0[0].shape
    return call(ffn_pick_kernel, [shape_of(4 * rows, width)] * 2, s, *layer0, *layer1)


def ffn_out_kernel(s_ref, c_ref, keep, got, gate, up, whole):
    s, c = s_ref[0], c_ref[0]
    rows, unit = gate.shape[0] // 4, whole.shape[0] // 8
    size = keep.shape[0] // 4
    first = s == 0
    for k in range(4):
        (a, x), (b, y) = (unpack(r[k * size : (k + 1) * size, :], rows, unit) for r in (keep, got))
        block = pl.ds(pl.multiple_of((c ^ k) * rows, rows), rows)
        gate[block, :] = jnp.where(first, a, b)
        up[block, :] = jnp.where(first, b, a)
        for half, v in ((s, x), (1 - s, y)):
            whole[pl.ds(pl.multiple_of((half * 4 + (c ^ k)) * unit, unit), unit), :] = v


def run_ffn_out(s, c, keep, got):
    width = keep.shape[1]
    out = [shape_of(D, width, kind=F32)] * 2 + [shape_of(width, D, kind=F32)]
    return call(ffn_out_kernel, out, s, c, keep, got)


def first_split_kernel(keep_ref, got_ref, a_keep, a_send, b_keep, b_send):
    total = (keep_ref[...].astype(F32) + got_ref[...].astype(F32)).astype(BF)
    for i in range(2):
        a_keep[i], a_send[i] = total[2 * i, :2], total[2 * i + 1, :2]
        b_keep[i], b_send[i] = total[i, 2:], total[2 + i, 2:]


def run_first_split(keep, got):
    shape = (4, 4, keep.shape[0] // 16, keep.shape[1])
    return call(
        first_split_kernel,
        [shape_of(2, 2, *shape[2:])] * 4,
        keep.reshape(shape), got.reshape(shape),
    )


def run_split_sum(a, a1, b, b1):
    out = [shape_of(*a.shape[1:])] * 2 + [shape_of(*b.shape[1:])] * 2
    return call(functools.partial(split_sum_kernel, 0), out, a, a1, b, b1)


def dp_split_kernel(a, a1, b, b1, own, s1, s2, s3):
    x = a[...].astype(F32) + a1[...].astype(F32)
    y = b[...].astype(F32) + b1[...].astype(F32)
    own[...] = x[0]
    s1[...], s2[...], s3[...] = x[1].astype(BF), y[0].astype(BF), y[1].astype(BF)


def run_dp_split(a, a1, b, b1):
    shape = a.shape[1:]
    return call(dp_split_kernel, [shape_of(*shape, kind=F32)] + [shape_of(*shape)] * 3, a, a1, b, b1)


def owner_sum_kernel(s_ref, *refs):
    now, later = (sum(r[...].astype(F32) for r in refs[k : k + 4]).astype(BF) for k in (0, 4))
    keep, send = refs[8:]
    first = s_ref[0] == 0
    keep[...] = jnp.where(first, now, later)
    send[...] = jnp.where(first, later, now)


def run_owner_sum(s, now, later):
    return call(owner_sum_kernel, [shape_of(*now[0].shape)] * 2, s, *now, *later)


def attention_out_kernel(order, u0, u1, u2, u3, wo, gains, wk, wv, wq):
    rows = jnp.concatenate([u[h] for u in (u0, u1, u2, u3) for h in range(2)], axis=0)
    out = dot(order[...], rows)
    wo[...] = out[:, WO:GAINS]
    gains[...] = out[:, GAINS:QKV]
    turned = lax.dot_general(
        rows[:, QKV : QKV + 2 * KVW], order[...], (((0,), (1,)), ((), ())), preferred_element_type=F32
    )
    wk[...], wv[...] = turned[:KVW], turned[KVW:]
    wq[...] = out[:, QKV + 2 * KVW : COLUMNS]


def run_attention_out(order, units):
    rows = order.shape[0]
    shapes = ((rows, QW), (rows, QKV - GAINS), (KVW, rows), (KVW, rows), (rows, QW))
    return call(
        attention_out_kernel,
        [shape_of(*shape, kind=F32) for shape in shapes],
        order, *units,
        flops=2 * rows * order.shape[1] * COLUMNS,
    )


def swap(x, axis, bit):
    return lax.ppermute(x, axis, [(i, i ^ bit) for i in range(lax.axis_size(axis))])


def spread(x, axis):
    return [x] + [swap(x, axis, k) for k in range(1, 4)]


def deliver(blocks, axis):
    return [blocks[0]] + [swap(b, axis, k) for k, b in enumerate(blocks[1:], 1)]


def pick(x, index, axis=0):
    return lax.dynamic_index_in_dim(x, index, axis, keepdims=False)


def tie(*values):
    return lax.optimization_barrier(values)


def plane_gather(a, b):
    a1, b1 = swap(a, "ctx", 2), swap(b, "ctx", 1)
    a2, b2 = swap(jnp.stack([a, a1]), "ctx", 1), swap(jnp.stack([b, b1]), "ctx", 2)
    return jnp.stack([a, a2[0], a1, a2[1]]), jnp.stack([b, b1, b2[0], b2[1]])


WO, GAINS, QKV = 0, QW, QW + 64
COLUMNS = QKV + QW + 2 * KVW
WIDTH = COLUMNS + 64
PAD = 256


def row_orders(s, c, d):
    p = jnp.arange(4 * PAD, dtype=jnp.int32)
    row = (((p // 128) % 4) ^ c) * 64 + ((p // 512) ^ s) * 32 + p % 32
    feature = jnp.where(row < D // 4, (((p // 32) % 4) ^ d) * (D // 4) + row, -1)
    order = (jnp.arange(D, dtype=jnp.int32)[:, None] == feature[None, :]).astype(BF)
    p = jnp.arange(PAD, dtype=jnp.int32)
    out = ((p // 64) ^ c) * 64 + (((p // 32) % 2) ^ s) * 32 + p % 32
    return order, (jnp.arange(D // 4, dtype=jnp.int32)[:, None] == out[None, :]).astype(BF)


def body_fast(
    block_input, out_grad, w_query, w_key, w_value, w_out, norm_attn, w_gate, w_up, w_down, norm_ffn
):
    s, c, d = (lax.axis_index(n) for n in ("section", "ctx", "dp"))
    s1, c1, d1 = (i.astype(jnp.int32).reshape(1) for i in (s, c, d))
    tok = block_input.shape[2]
    cosine, sine = rope_tables(c * tok + jnp.arange(tok, dtype=jnp.int32))
    sign = jnp.where(jnp.arange(HEAD_DIM) < HEAD_DIM // 2, -1.0, 1.0)
    tables = (jnp.tile(cosine, (1, 2)), jnp.tile(sine * sign, (1, 2)))
    order0, order_out = row_orders(s, c, d)
    x = pick(block_input[:, 0], s)
    g = pick(out_grad[:, 0], s)

    def by_layer(own, got):
        return jnp.where(s == 0, own, got), jnp.where(s == 0, got, own)

    def own_rows(w):
        return pick(jnp.pad(w, ((0, PAD - w.shape[0]), (0, 0))).reshape(4, 2, 32, w.shape[1]), c)

    gains = own_rows(jnp.stack([norm_attn[0], norm_ffn[0]], axis=1))
    gains = jnp.pad(gains, ((0, 0), (0, 0), (0, QKV - GAINS - 2)))
    own = [own_rows(w[0]) for w in (w_out, w_key, w_value, w_query)]
    own = jnp.concatenate([own[0], gains, *own[1:], jnp.zeros((2, 32, WIDTH - COLUMNS), BF)], axis=2)
    unit0, unit1 = by_layer(pick(own, s), swap(pick(own, 1 - s), "section", 1))
    ffn = [by_layer(w[0], swap(w[0], "section", 1)) for w in (w_gate, w_up, w_down)]
    gb1 = g.astype(BF)
    z = spread(unit0, "dp")
    z[2:], (ffn, order0, order_out, tables, x, g, gb1, unit1) = tie(
        z[2:], (ffn, order0, order_out, tables, x, g, gb1, unit1)
    )

    def first_step(a, b):
        return a, swap(a, "ctx", 2), b, swap(b, "ctx", 1)

    def second_step(a, a1, b, b1):
        return a, a1, swap(jnp.stack([a, a1]), "ctx", 1), b, b1, swap(jnp.stack([b, b1]), "ctx", 2)

    def whole_half(a, a1, a2, b, b1, b2):
        a, b = jnp.stack([a, a2[0], a1, a2[1]]), jnp.stack([b, b1, b2[0], b2[1]])
        return jnp.concatenate([a, b], axis=1).reshape(512, WIDTH)

    steps = second_step(*first_step(jnp.stack(z[:2]), jnp.stack(z[2:])))
    mine, gb1_2, unit1 = tie(whole_half(*steps), swap(gb1, "dp", 2), unit1)
    wa0 = (mine, swap(mine, "section", 1))

    def nothing(*values):
        return values

    def forward(parts, wa, order, w, beside, values):
        x, n1, q, kv, gains = run_project(parts, order, wa, tables)
        kv, values = tie(spread(kv, "ctx"), beside[0](*values))
        o, op, lse, h1, n2 = run_attend(c1, x, q, kv, gains, order, wa)
        n2, values = tie(lax.all_gather(n2, "dp"), beside[1](*values))
        gate, up, hidden, *parts = run_ffn(d1, h1, n2, *w)
        if beside[2] is not None:
            parts, values = tie(deliver(parts, "dp"), beside[2](*values))
        return parts, (x, n1, q, kv, o, op, lse, h1, n2, gate, up, hidden, gains), values

    def backward(g, gb, kept, wa, order, w, beside, values):
        x, n1, q, kv, o, op, lse, h1, n2, gate, up, hidden, gains = kept
        dgate, dup, *parts = run_ffn_back(d1, gb, gate, up, *w)
        parts = deliver(parts, "dp")
        values = beside[0](*values)
        gu_keep, gu_send, down_keep, down_send = run_ffn_grads(s1, d1, dgate, dup, hidden, n2, gb)
        sums = run_ffn_split(c1, gu_keep, swap(gu_send, "section", 1), down_keep, swap(down_send, "section", 1))
        parts, sums, values = tie(parts, sums, values)
        values = beside[1](*values)
        dh1, db, gain_f, dq, *dkv = run_attend_back(c1, parts, kv, h1, g, q, o, lse, gains, order, wa, tables)
        dkv, values = tie(dkv, values)
        sums = deliver(sums, "ctx")
        dkv, values, sums = tie(deliver(dkv, "ctx"), beside[2](*values), sums)
        g, gb, dqkv, gains = run_project_back(dkv, dq, x, dh1, gain_f, gains, order, wa, tables)
        return g, gb, (op, db, n1, dqkv, gains), sums, values

    w0, w1 = ([pair[l] for pair in ffn] for l in range(2))
    parts, kept0, steps = forward(
        [x], wa0, order0, w0,
        (
            lambda unit: spread(unit, "dp"),
            lambda *z: first_step(jnp.stack(z[:2]), jnp.stack(z[2:])),
            second_step,
        ),
        (unit1,),
    )
    mine = whole_half(*steps)
    wa1 = (mine, swap(mine, "section", 1))
    out1, kept1, (gb1_1, gb1_3) = forward(
        parts, wa1, order0, w1, (lambda v: (swap(v, "dp", 1), swap(v, "dp", 3)), nothing, None), (gb1,)
    )
    out0 = kept1[0]
    gb = [gb1, gb1_1, gb1_2, gb1_3]
    in1, gb, operands, ffn1, out1 = backward(
        g, gb, kept1, wa1, order0, w1,
        (
            nothing,
            nothing,
            lambda own, p1, p2, p3: (own, swap(p1, "dp", 1), p2, swap(p3, "dp", 3)),
        ),
        out1,
    )
    ffn1 = spread(run_ffn_total(ffn1), "ctx")
    gb, operands, ffn1 = tie(lax.all_gather(gb, "dp"), operands, ffn1)
    keep, send = run_attention_grads(*operands)
    gb, keep, send = tie(gb, keep, send)

    def scatter_first(a, a1, b, b1):
        return a, swap(a1, "ctx", 1), b, swap(b1, "ctx", 2)

    def scatter_second(a, a1, b, b1):
        return a, swap(a1, "ctx", 2), b, swap(b1, "ctx", 1)

    in0, _, operands, ffn0, later = backward(
        in1, [gb], kept0, wa0, order0, w0,
        (
            lambda keep, got: scatter_first(*run_first_split(keep, got)),
            lambda *steps: scatter_second(*run_split_sum(*steps)),
            lambda *steps: deliver(run_dp_split(*steps), "dp"),
        ),
        (keep, swap(send, "section", 1)),
    )
    keep, send = run_attention_grads(*operands)
    steps = scatter_first(*run_first_split(keep, swap(send, "section", 1)))
    steps = tie(*steps)
    steps, ffn0 = tie(scatter_second(*run_split_sum(*steps)), ffn0)
    blocks = deliver(run_dp_split(*steps), "dp")
    ffn0 = spread(run_ffn_total(ffn0), "ctx")
    blocks, ffn0 = tie(blocks, ffn0)
    keep, send = run_owner_sum(s1, blocks, later)
    unit = jnp.stack([keep, swap(send, "section", 1)])
    keep, send = run_ffn_pick(s1, ffn0, ffn1)
    gate, up, down = run_ffn_out(s1, c1, keep, swap(send, "section", 1))
    units, gate, up, down, out1_2 = tie(spread(unit, "ctx"), gate, up, down, swap(out1[2], "dp", 2))
    out1 = out1[0] + sum(p.astype(F32) for p in (out1[1], out1_2, out1[3]))
    wo, gains, wk, wv, wq = run_attention_out(order_out, units)

    def own_layer(p0, p1):
        keep, send = by_layer(p0, p1)
        got = swap(send, "section", 1)
        return jnp.stack(by_layer(keep, got))

    return (
        own_layer(out0, out1)[None, :, None],
        own_layer(in0, in1)[None, :, None],
        wq[None],
        wk.T[None],
        wv.T[None],
        wo[None],
        gains[None, :, 0],
        gate[None],
        up[None],
        down[None],
        gains[None, :, 1],
    )


def body(*args):
    sizes = [lax.axis_size(name) for name in ("section", "ctx", "dp")]
    return (body_fast if sizes == [2, 4, 4] else body_plain)(*args)


def solution(mesh):
    return jax.shard_map(
        body,
        mesh=mesh,
        in_specs=(
            P(None, "dp", "ctx", None),
            P(None, "dp", "ctx", None),
            P("section", "dp", None),
            P("section", "dp", None),
            P("section", "dp", None),
            P("section", "dp", None),
            P("section", "dp"),
            P("section", None, "dp"),
            P("section", None, "dp"),
            P("section", "dp", None),
            P("section", "dp"),
        ),
        out_specs=(
            P("section", None, "dp", "ctx", None),
            P("section", None, "dp", "ctx", None),
            P("section", "dp", None),
            P("section", "dp", None),
            P("section", "dp", None),
            P("section", "dp", None),
            P("section", "dp"),
            P("section", None, "dp"),
            P("section", None, "dp"),
            P("section", "dp", None),
            P("section", "dp"),
        ),
        check_vma=False,
    )
```

```python
import functools
import math

import jax
import jax.numpy as jnp
from jax import lax
from jax.experimental import pallas as pl
from jax.experimental.pallas import tpu as pltpu
from jax.sharding import PartitionSpec as P

D = 960
HEADS = 15
KV_HEADS = 5
HEAD_DIM = 64
QW = 960
KVW = 320
GROUP = 3
EPSILON = 1e-05
ROPE_BASE = 10000.0
MASKED = -1e30
BF = jnp.bfloat16
F32 = jnp.float32


def dot(a, b):
    return jnp.dot(a, b, preferred_element_type=F32)


def rope_tables(positions):
    half_dim = HEAD_DIM // 2
    freq_rows = ROPE_BASE ** (-(jnp.arange(half_dim, dtype=F32) * 2.0 / HEAD_DIM))
    angles = positions.astype(F32)[:, None] * freq_rows[None, :]
    cosine = jnp.concatenate([jnp.cos(angles), jnp.cos(angles)], axis=1)
    sine_rows = jnp.concatenate([jnp.sin(angles), jnp.sin(angles)], axis=1)
    return (cosine, sine_rows)


def turn_half(u):
    half_dim = HEAD_DIM // 2
    return jnp.concatenate([-u[..., half_dim:], u[..., :half_dim]], axis=-1)


def rotate(u, cosine, sine_rows):
    return u * cosine[:, None, :] + turn_half(u) * sine_rows[:, None, :]


def unrotate(u, cosine, sine_rows):
    return u * cosine[:, None, :] - turn_half(u * sine_rows[:, None, :])


def normalize(x, gain):
    inverse = lax.rsqrt(jnp.mean(x * x, axis=-1, keepdims=True) + EPSILON)
    return (x * inverse * gain, inverse)


def normalize_back(x, inverse, gain, grad):
    scaled = grad * gain
    gain_grad = jnp.sum(grad * x * inverse, axis=0)
    value_grad = inverse * scaled - x * inverse**3 * jnp.mean(scaled * x, axis=-1, keepdims=True)
    return (value_grad, gain_grad)


def attend(q, k, v, query_pos):
    tok = q.shape[0]
    q = q.reshape(tok, KV_HEADS, GROUP, HEAD_DIM)
    scores = jnp.einsum("tkgd,skd->kgts", q, k, preferred_element_type=F32) * HEAD_DIM**-0.5
    allowed = query_pos[:, None] >= jnp.arange(k.shape[0], dtype=jnp.int32)[None, :]
    scores = jnp.where(allowed, scores, MASKED)
    peak = jnp.max(scores, axis=-1, keepdims=True)
    e = jnp.exp(scores - peak)
    total = jnp.sum(e, axis=-1, keepdims=True)
    probs = (e / total).astype(BF)
    o = jnp.einsum("kgts,skd->tkgd", probs, v, preferred_element_type=F32).reshape(tok, QW)
    return o.astype(BF), (peak + jnp.log(total))[..., 0]


def attend_back(q, k, v, lse, do, o, query_pos):
    tok = q.shape[0]
    q = q.reshape(tok, KV_HEADS, GROUP, HEAD_DIM)
    dor = do.reshape(tok, KV_HEADS, GROUP, HEAD_DIM)
    delta = jnp.sum((do.astype(F32) * o.astype(F32)).reshape(tok, KV_HEADS, GROUP, HEAD_DIM), axis=-1)
    delta = jnp.transpose(delta, (1, 2, 0))
    scale = HEAD_DIM**-0.5
    scores = jnp.einsum("tkgd,skd->kgts", q, k, preferred_element_type=F32) * scale
    allowed = query_pos[:, None] >= jnp.arange(k.shape[0], dtype=jnp.int32)[None, :]
    probs = jnp.where(allowed, jnp.exp(scores - lse[..., None]), 0.0)
    dv = jnp.einsum("kgts,tkgd->skd", probs.astype(BF), dor, preferred_element_type=F32)
    dp = jnp.einsum("tkgd,skd->kgts", dor, v, preferred_element_type=F32)
    ds = (probs * (dp - delta[..., None])).astype(BF)
    dq = jnp.einsum("kgts,skd->tkgd", ds, k, preferred_element_type=F32) * scale
    dk = jnp.einsum("kgts,tkgd->skd", ds, q, preferred_element_type=F32) * scale
    dkv = jnp.concatenate([dk.reshape(-1, KVW), dv.reshape(-1, KVW)], axis=1)
    return dq.reshape(tok, HEADS, HEAD_DIM), dkv


def layer_forward(x, w, cosine, sine, query_pos):
    wa, wg, wu, wd, ga, gf = w
    tok = x.shape[0]
    n1, r1 = normalize(x, ga)
    n1 = n1.astype(BF)
    qkv = dot(n1, wa[:, : QW + 2 * KVW])
    q = rotate(qkv[:, :QW].reshape(tok, HEADS, HEAD_DIM), cosine, sine).astype(BF)
    k = rotate(qkv[:, QW : QW + KVW].reshape(tok, KV_HEADS, HEAD_DIM), cosine, sine)
    kv = jnp.concatenate([k.reshape(tok, KVW), qkv[:, QW + KVW :]], axis=1).astype(BF)
    kv = lax.all_gather(kv, "ctx", axis=0, tiled=True)
    k = kv[:, :KVW].reshape(-1, KV_HEADS, HEAD_DIM)
    v = kv[:, KVW:].reshape(-1, KV_HEADS, HEAD_DIM)
    o, lse = attend(q, k, v, query_pos)
    h1 = x + dot(o, wa[:, QW + 2 * KVW :])
    n2, r2 = normalize(h1, gf)
    n2 = lax.all_gather(n2.astype(BF), "dp", axis=0, tiled=True)
    gate = dot(n2, wg)
    up = dot(n2, wu)
    hidden = (jax.nn.silu(gate) * up).astype(BF)
    part = dot(hidden, wd).astype(BF)
    out = h1 + lax.psum_scatter(part, "dp", scatter_dimension=0, tiled=True).astype(F32)
    return out, (x, n1, r1, q, k, v, o, lse, h1, n2, r2, gate, up, hidden)


def layer_backward(g, kept, w, cosine, sine, query_pos):
    wa, wg, wu, wd, ga, gf = w
    x, n1, r1, q, k, v, o, lse, h1, n2, r2, gate, up, hidden = kept
    tok = x.shape[0]
    gb = lax.all_gather(g.astype(BF), "dp", axis=0, tiled=True)
    grad_down = dot(hidden.T, gb)
    dh = dot(gb, wd.T)
    sigma = jax.nn.sigmoid(gate)
    dgate = (dh * up * sigma * (1.0 + gate * (1.0 - sigma))).astype(BF)
    dup = (dh * gate * sigma).astype(BF)
    grad_gate = dot(n2.T, dgate)
    grad_up = dot(n2.T, dup)
    part = (dot(dgate, wg.T) + dot(dup, wu.T)).astype(BF)
    dn2 = lax.psum_scatter(part, "dp", scatter_dimension=0, tiled=True).astype(F32)
    back_f, gain_f = normalize_back(h1, r2, gf, dn2)
    dh1 = g + back_f
    db = dh1.astype(BF)
    grad_out = dot(o.T, db)
    do = dot(db, wa[:, QW + 2 * KVW :].T).astype(BF)
    dq, dkv = attend_back(q, k, v, lse, do, o, query_pos)
    dkv = lax.psum_scatter(dkv.astype(BF), "ctx", scatter_dimension=0, tiled=True).astype(F32)
    dq = unrotate(dq, cosine, sine).reshape(tok, QW)
    dk = unrotate(dkv[:, :KVW].reshape(tok, KV_HEADS, HEAD_DIM), cosine, sine).reshape(tok, KVW)
    dqkv = jnp.concatenate([dq, dk, dkv[:, KVW:]], axis=1).astype(BF)
    grad_qkv = dot(n1.T, dqkv)
    dn1 = dot(dqkv, wa[:, : QW + 2 * KVW].T)
    back_a, gain_a = normalize_back(x, r1, ga, dn1)
    grads = (
        jnp.concatenate([grad_qkv, grad_out], axis=1).astype(BF),
        jnp.stack([gain_a, gain_f]),
        grad_gate.astype(BF),
        grad_up.astype(BF),
        grad_down.astype(BF),
    )
    return dh1 + back_a, grads


def swap_section(p0, p1, section_id):
    mine = jnp.where(section_id == 0, p0, p1)
    other = jnp.where(section_id == 0, p1, p0)
    count = lax.axis_size("section")
    got = lax.ppermute(other, "section", [(i, count - 1 - i) for i in range(count)])
    return mine.astype(F32) + got.astype(F32)


def own_layer(p0, p1, section_id):
    mine = jnp.where(section_id == 0, p0, p1)
    other = jnp.where(section_id == 0, p1, p0)
    count = lax.axis_size("section")
    got = lax.ppermute(other, "section", [(i, count - 1 - i) for i in range(count)])
    first = jnp.where(section_id == 0, mine, got)
    second = jnp.where(section_id == 0, got, mine)
    return jnp.stack([first, second])


def body_plain(
    block_input, out_grad, w_query, w_key, w_value, w_out, norm_attn, w_gate, w_up, w_down, norm_ffn
):
    section_id = lax.axis_index("section")
    tok_rows = block_input.shape[2]
    query_pos = lax.axis_index("ctx") * tok_rows + jnp.arange(tok_rows, dtype=jnp.int32)
    cosine, sine = rope_tables(query_pos)
    x = lax.dynamic_index_in_dim(block_input[:, 0], section_id, 0, keepdims=False)
    g = lax.dynamic_index_in_dim(out_grad[:, 0], section_id, 0, keepdims=False)
    wa = jnp.concatenate([w_query[0], w_key[0], w_value[0], w_out[0]], axis=1)
    wa = lax.all_gather(lax.all_gather(wa, "dp", axis=0, tiled=True), "section")
    gains = jnp.stack([norm_attn[0], norm_ffn[0]])
    gains = lax.all_gather(lax.all_gather(gains, "dp", axis=1, tiled=True), "section").astype(F32)
    wg = lax.all_gather(w_gate[0], "section")
    wu = lax.all_gather(w_up[0], "section")
    wd = lax.all_gather(w_down[0], "section")
    layers = [(wa[l], wg[l], wu[l], wd[l], gains[l, 0], gains[l, 1]) for l in range(2)]
    out0, kept0 = layer_forward(x, layers[0], cosine, sine, query_pos)
    out1, kept1 = layer_forward(out0, layers[1], cosine, sine, query_pos)
    in1, grads1 = layer_backward(g, kept1, layers[1], cosine, sine, query_pos)
    in0, grads0 = layer_backward(in1, kept0, layers[0], cosine, sine, query_pos)
    section_outs = own_layer(out0, out1, section_id)
    in_grads = own_layer(in0, in1, section_id)
    ga, gn, gg, gu, gd = (
        swap_section(a, b, section_id) for a, b in zip(grads0, grads1)
    )
    ga = lax.psum_scatter(ga.astype(BF), "dp", scatter_dimension=0, tiled=True)
    ga = lax.psum(ga, "ctx").astype(F32)
    gn = lax.psum_scatter(gn, "dp", scatter_dimension=1, tiled=True)
    gn = lax.psum(gn, "ctx")
    gg = lax.psum(gg.astype(BF), "ctx").astype(F32)
    gu = lax.psum(gu.astype(BF), "ctx").astype(F32)
    gd = lax.psum(gd.astype(BF), "ctx").astype(F32)
    return (
        section_outs[None, :, None],
        in_grads[None, :, None],
        ga[None, :, :QW],
        ga[None, :, QW : QW + KVW],
        ga[None, :, QW + KVW : QW + 2 * KVW],
        ga[None, :, QW + 2 * KVW :],
        gn[None, 0],
        gg[None],
        gu[None],
        gd[None],
        gn[None, 1],
    )


def t_dot(a, b):
    return lax.dot_general(a, b, (((0,), (0,)), ((), ())), preferred_element_type=F32)


def dot_t(a, b):
    return lax.dot_general(a, b, (((1,), (1,)), ((), ())), preferred_element_type=F32)


def shape_of(*dims, kind=BF):
    return jax.ShapeDtypeStruct(dims, kind)


def call(kernel, out_shape, *args, flops=0, grid=None, in_specs=None, out_specs=None, scratch=()):
    moved = sum(math.prod(a.shape) * a.dtype.itemsize for a in list(args) + list(out_shape))
    kwargs = {} if grid is None else {"grid": grid}
    held = moved + sum(math.prod(m.shape) * 4 for m in scratch)
    vmem = pl.BlockSpec(memory_space=pltpu.VMEM)
    smem = pl.BlockSpec(memory_space=pltpu.SMEM)
    return pl.pallas_call(
        kernel,
        out_shape=out_shape,
        in_specs=in_specs or [smem if a.dtype == jnp.int32 else vmem for a in args],
        out_specs=out_specs or [vmem] * len(out_shape),
        scratch_shapes=scratch,
        cost_estimate=pl.CostEstimate(flops=flops, bytes_accessed=moved, transcendentals=0),
        compiler_params=pltpu.CompilerParams(vmem_limit_bytes=min(60 << 20, held * 9 // 8 + (8 << 20))),
        **kwargs,
    )(*args)


def turn(u, cosine, sine, sign, first, last):
    rows, width = u.shape
    padded = -(-width // 128) * 128
    if padded > width:
        u = jnp.concatenate([u, jnp.zeros((rows, padded - width), F32)], axis=1)
    lane = lax.broadcasted_iota(jnp.int32, (rows, padded), 1)
    partner = jnp.where(
        lane % HEAD_DIM < HEAD_DIM // 2,
        pltpu.roll(u, padded - HEAD_DIM // 2, 1),
        pltpu.roll(u, HEAD_DIM // 2, 1),
    )
    cosine = jnp.concatenate([cosine[:rows]] * (padded // HEAD_DIM), axis=1)
    sine = jnp.concatenate([sine[:rows]] * (padded // HEAD_DIM), axis=1)
    turned = u * cosine + (partner * sine if sign > 0 else -(partner * sine))
    return jnp.where((lane >= first) & (lane < last), turned, u)[:, :width]


def inverse_norm(x):
    return lax.rsqrt(jnp.mean(x * x, axis=-1, keepdims=True) + EPSILON)


def project_kernel(count, *refs):
    parts, (order, w0, w1, cosine, sine, x_ref, n_ref, q_ref, kv_ref, gain_ref) = refs[:count], refs[count:]
    columns = jnp.concatenate([w0[:, GAINS - QKV :], w1[:, GAINS - QKV :]], axis=0)
    gains = lax.dot_general(columns, order[...], (((0,), (1,)), ((), ())), preferred_element_type=F32)
    gain_ref[...] = gains[:8]
    x = parts[0][...]
    for part in parts[1:]:
        x = x + part[...].astype(F32)
    x_ref[...] = x
    n = (x * inverse_norm(x) * gains[:1]).astype(BF)
    n = dot(n, order[...]).astype(BF)
    n_ref[...] = n
    half = w0.shape[0]
    out = dot(n[:, :half], w0[:, : GAINS - QKV]) + dot(n[:, half:], w1[:, : GAINS - QKV])
    kv = turn(out[:, : 2 * KVW], cosine[...], sine[...], 1, 0, KVW)
    kv_ref[...] = kv.astype(BF)
    q_ref[...] = turn(out[:, 2 * KVW :], cosine[...], sine[...], 1, 0, QW).astype(BF)


def run_project(parts, order, wa, tables):
    tok = parts[0].shape[0]
    args = list(parts) + [order, *wa, *tables]
    return call(
        functools.partial(project_kernel, len(parts)),
        [
            shape_of(tok, D, kind=F32),
            shape_of(tok, order.shape[1]),
            shape_of(tok, QW),
            shape_of(tok, 2 * KVW),
            shape_of(8, D, kind=F32),
        ],
        *args,
        flops=2 * tok * order.shape[1] * (D + QW + 2 * KVW),
    )


def project_all_kernel(*refs):
    x_ref, others = refs[0], refs[1:4]
    order, w0, w1, cosine, sine, n_ref, q_ref, kv0, kv1, kv2, kv3, gain_ref = refs[4:]
    columns = jnp.concatenate([w0[:, GAINS - QKV :], w1[:, GAINS - QKV :]], axis=0)
    gains = lax.dot_general(columns, order[...], (((0,), (1,)), ((), ())), preferred_element_type=F32)
    gain_ref[...] = gains[:8]
    x = x_ref[...]
    tok = x.shape[0]
    rows = [x * inverse_norm(x)] + [r[...].astype(F32) for r in others]
    n = (jnp.concatenate(rows, axis=0) * gains[:1]).astype(BF)
    n = dot(n, order[...]).astype(BF)
    n_ref[...] = n[:tok]
    half = w0.shape[0]
    kv = dot(n[:, :half], w0[:, : 2 * KVW]) + dot(n[:, half:], w1[:, : 2 * KVW])
    kv = turn(kv, cosine[...], sine[...], 1, 0, KVW).astype(BF)
    for k, out in enumerate((kv0, kv1, kv2, kv3)):
        out[...] = kv[k * tok : (k + 1) * tok]
    q = dot(n[:tok, :half], w0[:, 2 * KVW : GAINS - QKV]) + dot(n[:tok, half:], w1[:, 2 * KVW : GAINS - QKV])
    q_ref[...] = turn(q, cosine[...], sine[...], 1, 0, QW).astype(BF)


def run_project_all(x, others, order, wa, tables):
    tok = x.shape[0]
    n1, q, *kv, gains = call(
        project_all_kernel,
        [shape_of(tok, order.shape[1]), shape_of(tok, QW)]
        + [shape_of(tok, 2 * KVW)] * 4
        + [shape_of(8, D, kind=F32)],
        x, *others, order, *wa, *tables,
        flops=2 * tok * order.shape[1] * (4 * D + QW + 8 * KVW),
    )
    return x, n1, q, kv, gains


def causal(c, tok, count):
    shape = (GROUP * tok, count * tok)
    row = c * tok + lax.broadcasted_iota(jnp.int32, shape, 0) % tok
    lane = lax.broadcasted_iota(jnp.int32, shape, 1)
    key = jnp.zeros(shape, jnp.int32)
    for k in range(count):
        key = jnp.where(lane // tok == k, (c ^ k) * tok + lane % tok, key)
    return row >= key


def heads_of(x, j):
    return jnp.concatenate(
        [x[:, (GROUP * j + g) * HEAD_DIM : (GROUP * j + g + 1) * HEAD_DIM] for g in range(GROUP)], axis=0
    )


def attend_kernel(c_ref, x_ref, q_ref, kv0, kv1, kv2, kv3, gain, order, w0, w1, o_ref, op_ref, lse_ref, h_ref, n_ref):
    tok = q_ref.shape[0]
    kv = jnp.concatenate([kv0[...], kv1[...], kv2[...], kv3[...]], axis=0)
    q = q_ref[...]
    allowed = causal(c_ref[0], tok, 4)
    for j in range(KV_HEADS):
        k = kv[:, j * HEAD_DIM : (j + 1) * HEAD_DIM]
        v = kv[:, KVW + j * HEAD_DIM : KVW + (j + 1) * HEAD_DIM]
        scores = jnp.where(allowed, dot_t(heads_of(q, j), k) * HEAD_DIM**-0.5, MASKED)
        peak = jnp.max(scores, axis=-1, keepdims=True)
        e = jnp.exp(scores - peak)
        total = jnp.sum(e, axis=-1, keepdims=True)
        o = dot((e * (1.0 / total)).astype(BF), v).astype(BF)
        lse = peak + jnp.log(total)
        for g in range(GROUP):
            h = GROUP * j + g
            o_ref[:, h * HEAD_DIM : (h + 1) * HEAD_DIM] = o[g * tok : (g + 1) * tok]
            lse_ref[:, h : h + 1] = lse[g * tok : (g + 1) * tok]
    op = dot(o_ref[...], order[...]).astype(BF)
    op_ref[...] = op
    half = w0.shape[0]
    h1 = x_ref[...] + dot(op[:, :half], w0[:, :QW]) + dot(op[:, half:], w1[:, :QW])
    h_ref[...] = h1
    n_ref[...] = (h1 * inverse_norm(h1) * gain[1:2]).astype(BF)


def run_attend(c, x, q, kv, gain, order, wa):
    tok = q.shape[0]
    return call(
        attend_kernel,
        [
            shape_of(tok, QW),
            shape_of(tok, order.shape[1]),
            shape_of(tok, 16, kind=F32),
            shape_of(tok, D, kind=F32),
            shape_of(tok, D),
        ],
        c, x, q, *kv, gain, order, *wa,
        flops=2 * tok * (4 * tok * QW * 2 + order.shape[1] * D * 2),
    )


def token_rows(d_ref, *refs):
    if len(refs) == 1:
        d = d_ref[0]
        return jnp.concatenate([refs[0][d ^ k] for k in range(4)], axis=0)
    return jnp.concatenate([r[...] for r in refs], axis=0)


def ffn_kernel(d_ref, h_ref, n_ref, wg, wu, wd, gate_ref, up_ref, hidden_ref, p0, p1, p2, p3):
    n = token_rows(d_ref, n_ref)
    gate, up = dot(n, wg[...]), dot(n, wu[...])
    gate_ref[...], up_ref[...] = gate, up
    hidden = (gate * (1.0 / (1.0 + jnp.exp(-gate))) * up).astype(BF)
    hidden_ref[...] = hidden
    part = dot(hidden, wd[...])
    tok = h_ref.shape[0]
    p0[...] = h_ref[...] + part[:tok]
    for k, p in enumerate((p1, p2, p3), 1):
        p[...] = part[k * tok : (k + 1) * tok].astype(BF)


def run_ffn(d, h1, n2, wg, wu, wd):
    tok, width = h1.shape[0], wg.shape[1]
    return call(
        ffn_kernel,
        [shape_of(4 * tok, width, kind=F32)] * 2
        + [shape_of(4 * tok, width), shape_of(tok, D, kind=F32)]
        + [shape_of(tok, D)] * 3,
        d, h1, n2, wg, wu, wd,
        flops=6 * 4 * tok * width * D,
    )


def ffn_back_kernel(d_ref, *refs):
    gate_ref, up_ref, wg, wu, wd, dgate_ref, dup_ref, p0, p1, p2, p3 = refs[-11:]
    gb = token_rows(d_ref, *refs[:-11])
    dh = dot_t(gb, wd[...])
    gate, up = gate_ref[...], up_ref[...]
    sigma = 1.0 / (1.0 + jnp.exp(-gate))
    dgate = (dh * up * sigma * (1.0 + gate * (1.0 - sigma))).astype(BF)
    dup = (dh * gate * sigma).astype(BF)
    dgate_ref[...], dup_ref[...] = dgate, dup
    part = dot_t(dgate, wg[...]) + dot_t(dup, wu[...])
    tok = p0.shape[0]
    p0[...] = part[:tok]
    for k, p in enumerate((p1, p2, p3), 1):
        p[...] = part[k * tok : (k + 1) * tok].astype(BF)


def run_ffn_back(d, gb, gate, up, wg, wu, wd):
    tok, width = gate.shape[0] // 4, wg.shape[1]
    return call(
        ffn_back_kernel,
        [shape_of(4 * tok, width)] * 2 + [shape_of(tok, D, kind=F32)] + [shape_of(tok, D)] * 3,
        d, *gb, gate, up, wg, wu, wd,
        flops=6 * 4 * tok * width * D,
    )


def ffn_grads_kernel(s_ref, d_ref, dgate, dup, hidden, n_ref, *refs):
    n, gb = token_rows(d_ref, n_ref), token_rows(d_ref, *refs[:-5])
    gu_keep, gu_send, down_keep, down_send, down = refs[-5:]
    s = s_ref[0]
    a, b = dgate[...], dup[...]
    first = s == 0
    gu_keep[...] = t_dot(n, jnp.where(first, a, b)).astype(BF)
    gu_send[...] = t_dot(n, jnp.where(first, b, a)).astype(BF)
    down[...] = t_dot(hidden[...], gb)
    half = down.shape[0] // 2
    down_keep[...] = down[pl.ds(pl.multiple_of(s * half, half), half), :].astype(BF)
    down_send[...] = down[pl.ds(pl.multiple_of((1 - s) * half, half), half), :].astype(BF)


def run_ffn_grads(s, d, dgate, dup, hidden, n2, gb):
    tok, width = dgate.shape
    return call(
        ffn_grads_kernel,
        [shape_of(D, width)] * 2 + [shape_of(width // 2, D)] * 2,
        s, d, dgate, dup, hidden, n2, *gb,
        flops=6 * tok * width * D,
        scratch=[pltpu.VMEM((width, D), F32)],
    )


def attend_back_kernel(c_ref, *refs):
    parts, kv_refs = refs[:4], refs[4:8]
    h_ref, g_ref, q_ref, o_ref, lse_ref, gain, order, w0, w1, cosine, sine = refs[8:19]
    dh_ref, db_ref, gain_ref, dq_ref, d0, d1, d2, d3, dq_acc, dkv_acc = refs[19:]
    tok = q_ref.shape[0]
    dn = parts[0][...]
    for part in parts[1:]:
        dn = dn + part[...].astype(F32)
    h1 = h_ref[...]
    inverse = inverse_norm(h1)
    gain_ref[...] = jnp.sum(dn * h1 * inverse, axis=0, keepdims=True)
    scaled = dn * gain[1:2]
    dh = g_ref[...] + inverse * scaled - h1 * inverse**3 * jnp.mean(scaled * h1, axis=-1, keepdims=True)
    dh_ref[...] = dh
    db = dh.astype(BF)
    db_ref[...] = db
    dop = jnp.concatenate([dot_t(db, w0[:, :QW]), dot_t(db, w1[:, :QW])], axis=1).astype(BF)
    do = dot_t(dop, order[...]).astype(BF)
    kv = jnp.concatenate([r[...] for r in kv_refs], axis=0)
    q, o, lse_all = q_ref[...], o_ref[...], lse_ref[...]
    allowed = causal(c_ref[0], tok, 4)
    scale = HEAD_DIM**-0.5
    for j in range(KV_HEADS):
        k = kv[:, j * HEAD_DIM : (j + 1) * HEAD_DIM]
        v = kv[:, KVW + j * HEAD_DIM : KVW + (j + 1) * HEAD_DIM]
        qj, doj = heads_of(q, j), heads_of(do, j)
        delta = jnp.sum(doj.astype(F32) * heads_of(o, j).astype(F32), axis=-1, keepdims=True)
        lse = jnp.concatenate([lse_all[:, GROUP * j + g : GROUP * j + g + 1] for g in range(GROUP)], axis=0)
        probs = jnp.where(allowed, jnp.exp(dot_t(qj, k) * scale - lse), 0.0)
        dkv_acc[:, KVW + j * HEAD_DIM : KVW + (j + 1) * HEAD_DIM] = t_dot(probs.astype(BF), doj)
        ds = (probs * (dot_t(doj, v) - delta)).astype(BF)
        dkv_acc[:, j * HEAD_DIM : (j + 1) * HEAD_DIM] = t_dot(ds, qj) * scale
        dq = dot(ds, k) * scale
        for g in range(GROUP):
            h = GROUP * j + g
            dq_acc[:, h * HEAD_DIM : (h + 1) * HEAD_DIM] = dq[g * tok : (g + 1) * tok]
    dq_ref[...] = turn(dq_acc[...], cosine[...], sine[...], -1, 0, QW).astype(BF)
    d0[...] = dkv_acc[:tok]
    for k, d in enumerate((d1, d2, d3), 1):
        d[...] = dkv_acc[k * tok : (k + 1) * tok].astype(BF)


def run_attend_back(c, parts, kv, h1, g, q, o, lse, gain, order, wa, tables):
    tok = q.shape[0]
    return call(
        attend_back_kernel,
        [
            shape_of(tok, D, kind=F32),
            shape_of(tok, D),
            shape_of(1, D, kind=F32),
            shape_of(tok, QW),
            shape_of(tok, 2 * KVW, kind=F32),
        ]
        + [shape_of(tok, 2 * KVW)] * 3,
        c, *parts, *kv, h1, g, q, o, lse, gain, order, *wa, *tables,
        flops=2 * tok * (4 * tok * QW * 5 + order.shape[1] * D * 2),
        scratch=[pltpu.VMEM((tok, QW), F32), pltpu.VMEM((4 * tok, 2 * KVW), F32)],
    )


def project_back_kernel(*refs):
    parts, refs = refs[:4], refs[4:]
    dq_ref, x_ref, dh_ref, gain_f, gain, order, w0, w1, cosine, sine = refs[:10]
    in_ref, gb_ref, dqkv_ref, gains_ref = refs[10:]
    dkv = parts[0][...]
    for part in parts[1:]:
        dkv = dkv + part[...].astype(F32)
    dkv = turn(dkv, cosine[...], sine[...], -1, 0, KVW).astype(BF)
    dqkv_ref[:, : 2 * KVW] = dkv
    dqkv_ref[:, 2 * KVW :] = dq_ref[...]
    dqkv = dqkv_ref[...]
    ds = jnp.concatenate([dot_t(dqkv, w0[:, : GAINS - QKV]), dot_t(dqkv, w1[:, : GAINS - QKV])], axis=1)
    high = ds.astype(BF)
    low = (ds - high.astype(F32)).astype(BF)
    dn = dot_t(high, order[...]) + dot_t(low, order[...])
    x = x_ref[...]
    inverse = inverse_norm(x)
    gain_a = jnp.sum(dn * x * inverse, axis=0, keepdims=True)
    scaled = dn * gain[:1]
    out = dh_ref[...] + inverse * scaled - x * inverse**3 * jnp.mean(scaled * x, axis=-1, keepdims=True)
    in_ref[...] = out
    gb_ref[...] = out.astype(BF)
    row = lax.broadcasted_iota(jnp.int32, (16, D), 0)
    both = jnp.where(row == 0, gain_a, jnp.where(row == 1, gain_f[...], 0.0)).astype(BF)
    gains_ref[...] = dot(both, order[...]).astype(BF)


def run_project_back(parts, dq, x, dh1, gain_f, gain, order, wa, tables):
    tok = dq.shape[0]
    return call(
        project_back_kernel,
        [shape_of(tok, D, kind=F32), shape_of(tok, D), shape_of(tok, QW + 2 * KVW), shape_of(16, order.shape[1])],
        *parts, dq, x, dh1, gain_f, gain, order, *wa, *tables,
        flops=2 * tok * order.shape[1] * (2 * D + QW + 2 * KVW),
    )


def attention_grads_kernel(op0, op1, n0, n1, g0, g1, db_ref, dqkv_ref, keep_ref, send_ref):
    db, dqkv = db_ref[...], dqkv_ref[...]
    row = lax.broadcasted_iota(jnp.int32, (16, WIDTH - GAINS), 0)
    ones = (row == lax.broadcasted_iota(jnp.int32, (16, WIDTH - GAINS), 1)).astype(F32).astype(BF)
    for op, n, g, out in ((op0, n0, g0, keep_ref), (op1, n1, g1, send_ref)):
        out[:, WO:QW] = t_dot(op[...], db).astype(BF)
        out[:, QW:QKV] = jnp.zeros((out.shape[0], QKV - QW), BF)
        out[:, QKV:GAINS] = t_dot(n[...], dqkv).astype(BF)
        out[:, GAINS:] = t_dot(g[...], ones).astype(BF)


def run_attention_grads(op, db, n1, dqkv, gains):
    tok, rows = op.shape
    block = rows // 4

    def halves(height):
        return [pl.BlockSpec((height, block), lambda i: (0, i)), pl.BlockSpec((height, block), lambda i: (0, i + 2))]

    return call(
        attention_grads_kernel,
        [shape_of(rows // 2, WIDTH)] * 2,
        op, op, n1, n1, gains, gains, db, dqkv,
        flops=2 * tok * rows * WIDTH,
        grid=(2,),
        in_specs=halves(tok) + halves(tok) + halves(16)
        + [pl.BlockSpec((tok, QW), lambda i: (0, 0)), pl.BlockSpec((tok, QW + 2 * KVW), lambda i: (0, 0))],
        out_specs=[pl.BlockSpec((block, WIDTH), lambda i: (i, 0))] * 2,
    )


def add_kernel(a, b, out):
    out[...] = (a[...].astype(F32) + b[...].astype(F32)).astype(BF)


def run_add(a, b):
    return call(add_kernel, [shape_of(*a.shape)], a, b)[0]


def split_sum_kernel(axis, *refs):
    pairs = len(refs) // 4
    for i in range(pairs):
        a, b = refs[2 * i : 2 * i + 2]
        keep, send = refs[2 * pairs + 2 * i : 2 * pairs + 2 * i + 2]
        total = (a[...].astype(F32) + b[...].astype(F32)).astype(BF)
        keep[...], send[...] = total[0], total[1]


def pack(gu, down, out):
    rows, width = gu.shape
    unit = down.shape[0]
    out[:rows, :] = gu
    out[rows : rows + unit, :] = down[:, :width]
    out[rows + unit :, : width // 2] = down[: unit // 2, width:]
    out[rows + unit :, width // 2 :] = down[unit // 2 :, width:]


def unpack(packed, rows, unit):
    packed = packed.astype(F32)
    width = packed.shape[1]
    tail = packed[rows + unit :]
    tail = jnp.concatenate([tail[:, : width // 2], tail[:, width // 2 :]], axis=0)
    return packed[:rows], jnp.concatenate([packed[rows : rows + unit], tail], axis=1)


def ffn_split_kernel(c_ref, gu_a, gu_b, down_a, down_b, *outs):
    c = c_ref[0]
    for k, out in enumerate(outs):
        sums = []
        for a, b in ((gu_a, gu_b), (down_a, down_b)):
            rows = a.shape[0] // 4
            block = pl.ds(pl.multiple_of((c ^ k) * rows, rows), rows)
            sums.append((a[block, :].astype(F32) + b[block, :].astype(F32)).astype(BF))
        pack(*sums, out)


def run_ffn_split(c, gu_a, gu_b, down_a, down_b):
    width = gu_a.shape[1]
    rows = (gu_a.size + down_a.size) // (4 * width)
    return call(ffn_split_kernel, [shape_of(rows, width)] * 4, c, gu_a, gu_b, down_a, down_b)


def ffn_total_kernel(*refs):
    refs[4][...] = sum(r[...].astype(F32) for r in refs[:4]).astype(BF)


def run_ffn_total(blocks):
    return call(ffn_total_kernel, [shape_of(*blocks[0].shape)], *blocks)[0]


def ffn_pick_kernel(s_ref, *refs):
    first = s_ref[0] == 0
    rows = refs[0].shape[0]
    keep, send = refs[8:]
    for k in range(4):
        a, b = refs[k][...], refs[4 + k][...]
        keep[k * rows : (k + 1) * rows, :] = jnp.where(first, a, b)
        send[k * rows : (k + 1) * rows, :] = jnp.where(first, b, a)


def run_ffn_pick(s, layer0, layer1):
    rows, width = layer0[0].shape
    return call(ffn_pick_kernel, [shape_of(4 * rows, width)] * 2, s, *layer0, *layer1)


def ffn_out_kernel(s_ref, c_ref, keep, got, gate, up, whole):
    s, c = s_ref[0], c_ref[0]
    rows, unit = gate.shape[0] // 4, whole.shape[0] // 8
    size = keep.shape[0] // 4
    first = s == 0
    for k in range(4):
        (a, x), (b, y) = (unpack(r[k * size : (k + 1) * size, :], rows, unit) for r in (keep, got))
        block = pl.ds(pl.multiple_of((c ^ k) * rows, rows), rows)
        gate[block, :] = jnp.where(first, a, b)
        up[block, :] = jnp.where(first, b, a)
        for half, v in ((s, x), (1 - s, y)):
            whole[pl.ds(pl.multiple_of((half * 4 + (c ^ k)) * unit, unit), unit), :] = v


def run_ffn_out(s, c, keep, got):
    width = keep.shape[1]
    out = [shape_of(D, width, kind=F32)] * 2 + [shape_of(width, D, kind=F32)]
    return call(ffn_out_kernel, out, s, c, keep, got)


def first_split_kernel(keep_ref, got_ref, a_keep, a_send, b_keep, b_send):
    total = (keep_ref[...].astype(F32) + got_ref[...].astype(F32)).astype(BF)
    for i in range(2):
        a_keep[i], a_send[i] = total[2 * i, :2], total[2 * i + 1, :2]
        b_keep[i], b_send[i] = total[i, 2:], total[2 + i, 2:]


def run_first_split(keep, got):
    shape = (4, 4, keep.shape[0] // 16, keep.shape[1])
    return call(
        first_split_kernel,
        [shape_of(2, 2, *shape[2:])] * 4,
        keep.reshape(shape), got.reshape(shape),
    )


def run_split_sum(a, a1, b, b1):
    out = [shape_of(*a.shape[1:])] * 2 + [shape_of(*b.shape[1:])] * 2
    return call(functools.partial(split_sum_kernel, 0), out, a, a1, b, b1)


def dp_split_kernel(a, a1, b, b1, own, s1, s2, s3):
    x = a[...].astype(F32) + a1[...].astype(F32)
    y = b[...].astype(F32) + b1[...].astype(F32)
    own[...] = x[0]
    s1[...], s2[...], s3[...] = x[1].astype(BF), y[0].astype(BF), y[1].astype(BF)


def run_dp_split(a, a1, b, b1):
    shape = a.shape[1:]
    return call(dp_split_kernel, [shape_of(*shape, kind=F32)] + [shape_of(*shape)] * 3, a, a1, b, b1)


def owner_sum_kernel(s_ref, *refs):
    now, later = (sum(r[...].astype(F32) for r in refs[k : k + 4]).astype(BF) for k in (0, 4))
    keep, send = refs[8:]
    first = s_ref[0] == 0
    keep[...] = jnp.where(first, now, later)
    send[...] = jnp.where(first, later, now)


def run_owner_sum(s, now, later):
    return call(owner_sum_kernel, [shape_of(*now[0].shape)] * 2, s, *now, *later)


def attention_out_kernel(order, u0, u1, u2, u3, wo, gains, wk, wv, wq):
    rows = jnp.concatenate([u[h] for u in (u0, u1, u2, u3) for h in range(2)], axis=0)
    out = dot(order[...], rows)
    wo[...] = out[:, WO:QW]
    gains[...] = out[:, GAINS:]
    turned = lax.dot_general(
        rows[:, QKV : QKV + 2 * KVW], order[...], (((0,), (1,)), ((), ())), preferred_element_type=F32
    )
    wk[...], wv[...] = turned[:KVW], turned[KVW:]
    wq[...] = out[:, QKV + 2 * KVW : GAINS]


def run_attention_out(order, units):
    rows = order.shape[0]
    shapes = ((rows, QW), (rows, WIDTH - GAINS), (KVW, rows), (KVW, rows), (rows, QW))
    return call(
        attention_out_kernel,
        [shape_of(*shape, kind=F32) for shape in shapes],
        order, *units,
        flops=2 * rows * order.shape[1] * WIDTH,
    )


def swap(x, axis, bit):
    return lax.ppermute(x, axis, [(i, i ^ bit) for i in range(lax.axis_size(axis))])


def spread(x, axis):
    return [x] + [swap(x, axis, k) for k in range(1, 4)]


def deliver(blocks, axis):
    return [blocks[0]] + [swap(b, axis, k) for k, b in enumerate(blocks[1:], 1)]


def pick(x, index, axis=0):
    return lax.dynamic_index_in_dim(x, index, axis, keepdims=False)


def tie(*values):
    return lax.optimization_barrier(values)


def plane_gather(a, b):
    a1, b1 = swap(a, "ctx", 2), swap(b, "ctx", 1)
    a2, b2 = swap(jnp.stack([a, a1]), "ctx", 1), swap(jnp.stack([b, b1]), "ctx", 2)
    return jnp.stack([a, a2[0], a1, a2[1]]), jnp.stack([b, b1, b2[0], b2[1]])


WO, QKV = 0, QW + 64
GAINS = QKV + QW + 2 * KVW
WIDTH = GAINS + 64
PAD = 256


def row_orders(s, c, d):
    p = jnp.arange(4 * PAD, dtype=jnp.int32)
    row = (((p // 128) % 4) ^ c) * 64 + ((p // 512) ^ s) * 32 + p % 32
    feature = jnp.where(row < D // 4, (((p // 32) % 4) ^ d) * (D // 4) + row, -1)
    order = (jnp.arange(D, dtype=jnp.int32)[:, None] == feature[None, :]).astype(BF)
    p = jnp.arange(PAD, dtype=jnp.int32)
    out = ((p // 64) ^ c) * 64 + (((p // 32) % 2) ^ s) * 32 + p % 32
    return order, (jnp.arange(D // 4, dtype=jnp.int32)[:, None] == out[None, :]).astype(BF)


def body_fast(
    block_input, out_grad, w_query, w_key, w_value, w_out, norm_attn, w_gate, w_up, w_down, norm_ffn
):
    s, c, d = (lax.axis_index(n) for n in ("section", "ctx", "dp"))
    s1, c1, d1 = (i.astype(jnp.int32).reshape(1) for i in (s, c, d))
    tok = block_input.shape[2]
    cosine, sine = rope_tables(
        jnp.concatenate([(c ^ k) * tok + jnp.arange(tok, dtype=jnp.int32) for k in range(4)])
    )
    sign = jnp.where(jnp.arange(HEAD_DIM) < HEAD_DIM // 2, -1.0, 1.0)
    tables = cosine, sine * sign
    x = pick(block_input[:, 0], s)
    g = pick(out_grad[:, 0], s)

    def by_layer(own, got):
        return jnp.where(s == 0, own, got), jnp.where(s == 0, got, own)

    def own_rows(w):
        return pick(jnp.pad(w, ((0, PAD - w.shape[0]), (0, 0))).reshape(4, 2, 32, w.shape[1]), c)

    gains = own_rows(jnp.stack([norm_attn[0], norm_ffn[0]], axis=1))
    gains = jnp.pad(gains, ((0, 0), (0, 0), (0, WIDTH - GAINS - 2)))
    own = [own_rows(w[0]) for w in (w_out, w_key, w_value, w_query)]
    own = jnp.concatenate([own[0], jnp.zeros((2, 32, QKV - QW), BF), *own[1:], gains], axis=2)
    unit0, unit1 = by_layer(pick(own, s), swap(pick(own, 1 - s), "section", 1))
    ffn = [by_layer(w[0], swap(w[0], "section", 1)) for w in (w_gate, w_up, w_down)]
    gb1 = g.astype(BF)
    unit0, s, c, d, w_gate, w_up, w_down, x = tie(unit0, s, c, d, w_gate, w_up, w_down, x)
    z = spread(unit0, "dp")
    others = (x * inverse_norm(x)).astype(BF)
    z[2:], others = tie(z[2:], spread(others, "ctx")[1:])
    order0, order_out = row_orders(s, c, d)

    def first_step(a, b):
        return a, swap(a, "ctx", 2), b, swap(b, "ctx", 1)

    def second_step(a, a1, b, b1):
        return a, a1, swap(jnp.stack([a, a1]), "ctx", 1), b, b1, swap(jnp.stack([b, b1]), "ctx", 2)

    def whole_half(a, a1, a2, b, b1, b2):
        a, b = jnp.stack([a, a2[0], a1, a2[1]]), jnp.stack([b, b1, b2[0], b2[1]])
        whole = jnp.concatenate([a, b], axis=1).reshape(512, WIDTH)
        return whole[:, :QKV], whole[:, QKV:]

    steps = second_step(*first_step(jnp.stack(z[:2]), jnp.stack(z[2:])))
    mine, gb1_2, (ffn, order0, order_out, tables, x, g, gb1, unit1) = tie(
        whole_half(*steps), swap(gb1, "dp", 2), (ffn, order0, order_out, tables, x, g, gb1, unit1)
    )
    wa0 = [(w, swap(w, "section", 1)) for w in mine]

    def nothing(*values):
        return values

    def forward(parts, wa, order, w, beside, values, others=None):
        if others is None:
            x, n1, q, kv, gains = run_project(parts, order, wa[1], tables)
            kv, values = tie(spread(kv, "ctx"), beside[0](*values))
        else:
            x, n1, q, kv, gains = run_project_all(parts[0], others, order, wa[1], tables)
            values = beside[0](*values)
        o, op, lse, h1, n2 = run_attend(c1, x, q, kv, gains, order, wa[0])
        n2, values = tie(n2, values)
        n2, values = tie(lax.all_gather(n2, "dp"), beside[1](*values))
        gate, up, hidden, *parts = run_ffn(d1, h1, n2, *w)
        if beside[2] is not None:
            parts, values = tie(deliver(parts, "dp"), beside[2](*values))
        return parts, (x, n1, q, kv, o, op, lse, h1, n2, gate, up, hidden, gains), values

    def backward(g, gb, kept, wa, order, w, beside, values):
        x, n1, q, kv, o, op, lse, h1, n2, gate, up, hidden, gains = kept
        dgate, dup, *parts = run_ffn_back(d1, gb, gate, up, *w)
        parts = deliver(parts, "dp")
        values = beside[0](*values)
        gu_keep, gu_send, down_keep, down_send = run_ffn_grads(s1, d1, dgate, dup, hidden, n2, gb)
        sums = run_ffn_split(c1, gu_keep, swap(gu_send, "section", 1), down_keep, swap(down_send, "section", 1))
        parts, sums, values = tie(parts, sums, values)
        values = beside[1](*values)
        dh1, db, gain_f, dq, *dkv = run_attend_back(c1, parts, kv, h1, g, q, o, lse, gains, order, wa[0], tables)
        dkv, values = tie(dkv, values)
        sums = deliver(sums, "ctx")
        dkv, values, sums = tie(deliver(dkv, "ctx"), beside[2](*values), sums)
        g, gb, dqkv, gains = run_project_back(dkv, dq, x, dh1, gain_f, gains, order, wa[1], tables)
        return g, gb, (op, db, n1, dqkv, gains), sums, values

    w0, w1 = ([pair[l] for pair in ffn] for l in range(2))
    parts, kept0, steps = forward(
        [x], wa0, order0, w0,
        (
            lambda unit: spread(unit, "dp"),
            lambda *z: first_step(jnp.stack(z[:2]), jnp.stack(z[2:])),
            second_step,
        ),
        (unit1,), others,
    )
    mine = whole_half(*steps)
    wa1 = [(w, swap(w, "section", 1)) for w in mine]
    out1, kept1, (gb1_1, gb1_3) = forward(
        parts, wa1, order0, w1, (lambda v: (swap(v, "dp", 1), swap(v, "dp", 3)), nothing, None), (gb1,)
    )
    out0 = kept1[0]
    gb = [gb1, gb1_1, gb1_2, gb1_3]
    in1, gb, operands, ffn1, out1 = backward(
        g, gb, kept1, wa1, order0, w1,
        (
            nothing,
            nothing,
            lambda own, p1, p2, p3: (own, swap(p1, "dp", 1), p2, swap(p3, "dp", 3)),
        ),
        out1,
    )
    ffn1 = spread(run_ffn_total(ffn1), "ctx")
    gb, operands, ffn1 = tie(lax.all_gather(gb, "dp"), operands, ffn1)
    keep, send = run_attention_grads(*operands)
    gb, keep, send = tie(gb, keep, send)

    def scatter_first(a, a1, b, b1):
        return a, swap(a1, "ctx", 1), b, swap(b1, "ctx", 2)

    def scatter_second(a, a1, b, b1):
        return a, swap(a1, "ctx", 2), b, swap(b1, "ctx", 1)

    in0, _, operands, ffn0, later = backward(
        in1, [gb], kept0, wa0, order0, w0,
        (
            lambda keep, got: scatter_first(*run_first_split(keep, got)),
            lambda *steps: scatter_second(*run_split_sum(*steps)),
            lambda *steps: deliver(run_dp_split(*steps), "dp"),
        ),
        (keep, swap(send, "section", 1)),
    )
    keep, send = run_attention_grads(*operands)
    steps = scatter_first(*run_first_split(keep, swap(send, "section", 1)))
    steps = tie(*steps)
    steps, ffn0 = tie(scatter_second(*run_split_sum(*steps)), ffn0)
    blocks = deliver(run_dp_split(*steps), "dp")
    ffn0 = spread(run_ffn_total(ffn0), "ctx")
    blocks, ffn0 = tie(blocks, ffn0)
    keep, send = run_owner_sum(s1, blocks, later)
    unit = jnp.stack([keep, swap(send, "section", 1)])
    unit, ffn0, ffn1 = tie(unit, ffn0, ffn1)
    keep, send = run_ffn_pick(s1, ffn0, ffn1)
    gate, up, down = run_ffn_out(s1, c1, keep, swap(send, "section", 1))
    def own_layer(p0, p1):
        keep, send = by_layer(p0, p1)
        got = swap(send, "section", 1)
        return jnp.stack(by_layer(keep, got))

    units, gate, up, down, (in0, in1), out1_2 = tie(
        spread(unit, "ctx"), gate, up, down, (in0, in1), swap(out1[2], "dp", 2)
    )
    out1 = out1[0] + sum(p.astype(F32) for p in (out1[1], out1_2, out1[3]))
    wo, gains, wk, wv, wq = run_attention_out(order_out, units)
    return (
        own_layer(out0, out1)[None, :, None],
        own_layer(in0, in1)[None, :, None],
        wq[None],
        wk.T[None],
        wv.T[None],
        wo[None],
        gains[None, :, 0],
        gate[None],
        up[None],
        down[None],
        gains[None, :, 1],
    )


def body(*args):
    sizes = [lax.axis_size(name) for name in ("section", "ctx", "dp")]
    return (body_fast if sizes == [2, 4, 4] else body_plain)(*args)


def solution(mesh):
    return jax.shard_map(
        body,
        mesh=mesh,
        in_specs=(
            P(None, "dp", "ctx", None),
            P(None, "dp", "ctx", None),
            P("section", "dp", None),
            P("section", "dp", None),
            P("section", "dp", None),
            P("section", "dp", None),
            P("section", "dp"),
            P("section", None, "dp"),
            P("section", None, "dp"),
            P("section", "dp", None),
            P("section", "dp"),
        ),
        out_specs=(
            P("section", None, "dp", "ctx", None),
            P("section", None, "dp", "ctx", None),
            P("section", "dp", None),
            P("section", "dp", None),
            P("section", "dp", None),
            P("section", "dp", None),
            P("section", "dp"),
            P("section", None, "dp"),
            P("section", None, "dp"),
            P("section", "dp", None),
            P("section", "dp"),
        ),
        check_vma=False,
    )
```

```python
import functools
import math

import jax
import jax.numpy as jnp
from jax import lax
from jax.experimental import pallas as pl
from jax.experimental.pallas import tpu as pltpu
from jax.sharding import PartitionSpec as P

D = 960
HEADS = 15
KV_HEADS = 5
HEAD_DIM = 64
QW = 960
KVW = 320
GROUP = 3
EPSILON = 1e-05
ROPE_BASE = 10000.0
MASKED = -1e30
BF = jnp.bfloat16
F32 = jnp.float32


def dot(a, b):
    return jnp.dot(a, b, preferred_element_type=F32)


def rope_tables(positions):
    half_dim = HEAD_DIM // 2
    freq_rows = ROPE_BASE ** (-(jnp.arange(half_dim, dtype=F32) * 2.0 / HEAD_DIM))
    angles = positions.astype(F32)[:, None] * freq_rows[None, :]
    cosine = jnp.concatenate([jnp.cos(angles), jnp.cos(angles)], axis=1)
    sine_rows = jnp.concatenate([jnp.sin(angles), jnp.sin(angles)], axis=1)
    return (cosine, sine_rows)


def turn_half(u):
    half_dim = HEAD_DIM // 2
    return jnp.concatenate([-u[..., half_dim:], u[..., :half_dim]], axis=-1)


def rotate(u, cosine, sine_rows):
    return u * cosine[:, None, :] + turn_half(u) * sine_rows[:, None, :]


def unrotate(u, cosine, sine_rows):
    return u * cosine[:, None, :] - turn_half(u * sine_rows[:, None, :])


def normalize(x, gain):
    inverse = lax.rsqrt(jnp.mean(x * x, axis=-1, keepdims=True) + EPSILON)
    return (x * inverse * gain, inverse)


def normalize_back(x, inverse, gain, grad):
    scaled = grad * gain
    gain_grad = jnp.sum(grad * x * inverse, axis=0)
    value_grad = inverse * scaled - x * inverse**3 * jnp.mean(scaled * x, axis=-1, keepdims=True)
    return (value_grad, gain_grad)


def attend(q, k, v, query_pos):
    tok = q.shape[0]
    q = q.reshape(tok, KV_HEADS, GROUP, HEAD_DIM)
    scores = jnp.einsum("tkgd,skd->kgts", q, k, preferred_element_type=F32) * HEAD_DIM**-0.5
    allowed = query_pos[:, None] >= jnp.arange(k.shape[0], dtype=jnp.int32)[None, :]
    scores = jnp.where(allowed, scores, MASKED)
    peak = jnp.max(scores, axis=-1, keepdims=True)
    e = jnp.exp(scores - peak)
    total = jnp.sum(e, axis=-1, keepdims=True)
    probs = (e / total).astype(BF)
    o = jnp.einsum("kgts,skd->tkgd", probs, v, preferred_element_type=F32).reshape(tok, QW)
    return o.astype(BF), (peak + jnp.log(total))[..., 0]


def attend_back(q, k, v, lse, do, o, query_pos):
    tok = q.shape[0]
    q = q.reshape(tok, KV_HEADS, GROUP, HEAD_DIM)
    dor = do.reshape(tok, KV_HEADS, GROUP, HEAD_DIM)
    delta = jnp.sum((do.astype(F32) * o.astype(F32)).reshape(tok, KV_HEADS, GROUP, HEAD_DIM), axis=-1)
    delta = jnp.transpose(delta, (1, 2, 0))
    scale = HEAD_DIM**-0.5
    scores = jnp.einsum("tkgd,skd->kgts", q, k, preferred_element_type=F32) * scale
    allowed = query_pos[:, None] >= jnp.arange(k.shape[0], dtype=jnp.int32)[None, :]
    probs = jnp.where(allowed, jnp.exp(scores - lse[..., None]), 0.0)
    dv = jnp.einsum("kgts,tkgd->skd", probs.astype(BF), dor, preferred_element_type=F32)
    dp = jnp.einsum("tkgd,skd->kgts", dor, v, preferred_element_type=F32)
    ds = (probs * (dp - delta[..., None])).astype(BF)
    dq = jnp.einsum("kgts,skd->tkgd", ds, k, preferred_element_type=F32) * scale
    dk = jnp.einsum("kgts,tkgd->skd", ds, q, preferred_element_type=F32) * scale
    dkv = jnp.concatenate([dk.reshape(-1, KVW), dv.reshape(-1, KVW)], axis=1)
    return dq.reshape(tok, HEADS, HEAD_DIM), dkv


def layer_forward(x, w, cosine, sine, query_pos):
    wa, wg, wu, wd, ga, gf = w
    tok = x.shape[0]
    n1, r1 = normalize(x, ga)
    n1 = n1.astype(BF)
    qkv = dot(n1, wa[:, : QW + 2 * KVW])
    q = rotate(qkv[:, :QW].reshape(tok, HEADS, HEAD_DIM), cosine, sine).astype(BF)
    k = rotate(qkv[:, QW : QW + KVW].reshape(tok, KV_HEADS, HEAD_DIM), cosine, sine)
    kv = jnp.concatenate([k.reshape(tok, KVW), qkv[:, QW + KVW :]], axis=1).astype(BF)
    kv = lax.all_gather(kv, "ctx", axis=0, tiled=True)
    k = kv[:, :KVW].reshape(-1, KV_HEADS, HEAD_DIM)
    v = kv[:, KVW:].reshape(-1, KV_HEADS, HEAD_DIM)
    o, lse = attend(q, k, v, query_pos)
    h1 = x + dot(o, wa[:, QW + 2 * KVW :])
    n2, r2 = normalize(h1, gf)
    n2 = lax.all_gather(n2.astype(BF), "dp", axis=0, tiled=True)
    gate = dot(n2, wg)
    up = dot(n2, wu)
    hidden = (jax.nn.silu(gate) * up).astype(BF)
    part = dot(hidden, wd).astype(BF)
    out = h1 + lax.psum_scatter(part, "dp", scatter_dimension=0, tiled=True).astype(F32)
    return out, (x, n1, r1, q, k, v, o, lse, h1, n2, r2, gate, up, hidden)


def layer_backward(g, kept, w, cosine, sine, query_pos):
    wa, wg, wu, wd, ga, gf = w
    x, n1, r1, q, k, v, o, lse, h1, n2, r2, gate, up, hidden = kept
    tok = x.shape[0]
    gb = lax.all_gather(g.astype(BF), "dp", axis=0, tiled=True)
    grad_down = dot(hidden.T, gb)
    dh = dot(gb, wd.T)
    sigma = jax.nn.sigmoid(gate)
    dgate = (dh * up * sigma * (1.0 + gate * (1.0 - sigma))).astype(BF)
    dup = (dh * gate * sigma).astype(BF)
    grad_gate = dot(n2.T, dgate)
    grad_up = dot(n2.T, dup)
    part = (dot(dgate, wg.T) + dot(dup, wu.T)).astype(BF)
    dn2 = lax.psum_scatter(part, "dp", scatter_dimension=0, tiled=True).astype(F32)
    back_f, gain_f = normalize_back(h1, r2, gf, dn2)
    dh1 = g + back_f
    db = dh1.astype(BF)
    grad_out = dot(o.T, db)
    do = dot(db, wa[:, QW + 2 * KVW :].T).astype(BF)
    dq, dkv = attend_back(q, k, v, lse, do, o, query_pos)
    dkv = lax.psum_scatter(dkv.astype(BF), "ctx", scatter_dimension=0, tiled=True).astype(F32)
    dq = unrotate(dq, cosine, sine).reshape(tok, QW)
    dk = unrotate(dkv[:, :KVW].reshape(tok, KV_HEADS, HEAD_DIM), cosine, sine).reshape(tok, KVW)
    dqkv = jnp.concatenate([dq, dk, dkv[:, KVW:]], axis=1).astype(BF)
    grad_qkv = dot(n1.T, dqkv)
    dn1 = dot(dqkv, wa[:, : QW + 2 * KVW].T)
    back_a, gain_a = normalize_back(x, r1, ga, dn1)
    grads = (
        jnp.concatenate([grad_qkv, grad_out], axis=1).astype(BF),
        jnp.stack([gain_a, gain_f]),
        grad_gate.astype(BF),
        grad_up.astype(BF),
        grad_down.astype(BF),
    )
    return dh1 + back_a, grads


def swap_section(p0, p1, section_id):
    mine = jnp.where(section_id == 0, p0, p1)
    other = jnp.where(section_id == 0, p1, p0)
    count = lax.axis_size("section")
    got = lax.ppermute(other, "section", [(i, count - 1 - i) for i in range(count)])
    return mine.astype(F32) + got.astype(F32)


def own_layer(p0, p1, section_id):
    mine = jnp.where(section_id == 0, p0, p1)
    other = jnp.where(section_id == 0, p1, p0)
    count = lax.axis_size("section")
    got = lax.ppermute(other, "section", [(i, count - 1 - i) for i in range(count)])
    first = jnp.where(section_id == 0, mine, got)
    second = jnp.where(section_id == 0, got, mine)
    return jnp.stack([first, second])


def body_plain(
    block_input, out_grad, w_query, w_key, w_value, w_out, norm_attn, w_gate, w_up, w_down, norm_ffn
):
    section_id = lax.axis_index("section")
    tok_rows = block_input.shape[2]
    query_pos = lax.axis_index("ctx") * tok_rows + jnp.arange(tok_rows, dtype=jnp.int32)
    cosine, sine = rope_tables(query_pos)
    x = lax.dynamic_index_in_dim(block_input[:, 0], section_id, 0, keepdims=False)
    g = lax.dynamic_index_in_dim(out_grad[:, 0], section_id, 0, keepdims=False)
    wa = jnp.concatenate([w_query[0], w_key[0], w_value[0], w_out[0]], axis=1)
    wa = lax.all_gather(lax.all_gather(wa, "dp", axis=0, tiled=True), "section")
    gains = jnp.stack([norm_attn[0], norm_ffn[0]])
    gains = lax.all_gather(lax.all_gather(gains, "dp", axis=1, tiled=True), "section").astype(F32)
    wg = lax.all_gather(w_gate[0], "section")
    wu = lax.all_gather(w_up[0], "section")
    wd = lax.all_gather(w_down[0], "section")
    layers = [(wa[l], wg[l], wu[l], wd[l], gains[l, 0], gains[l, 1]) for l in range(2)]
    out0, kept0 = layer_forward(x, layers[0], cosine, sine, query_pos)
    out1, kept1 = layer_forward(out0, layers[1], cosine, sine, query_pos)
    in1, grads1 = layer_backward(g, kept1, layers[1], cosine, sine, query_pos)
    in0, grads0 = layer_backward(in1, kept0, layers[0], cosine, sine, query_pos)
    section_outs = own_layer(out0, out1, section_id)
    in_grads = own_layer(in0, in1, section_id)
    ga, gn, gg, gu, gd = (
        swap_section(a, b, section_id) for a, b in zip(grads0, grads1)
    )
    ga = lax.psum_scatter(ga.astype(BF), "dp", scatter_dimension=0, tiled=True)
    ga = lax.psum(ga, "ctx").astype(F32)
    gn = lax.psum_scatter(gn, "dp", scatter_dimension=1, tiled=True)
    gn = lax.psum(gn, "ctx")
    gg = lax.psum(gg.astype(BF), "ctx").astype(F32)
    gu = lax.psum(gu.astype(BF), "ctx").astype(F32)
    gd = lax.psum(gd.astype(BF), "ctx").astype(F32)
    return (
        section_outs[None, :, None],
        in_grads[None, :, None],
        ga[None, :, :QW],
        ga[None, :, QW : QW + KVW],
        ga[None, :, QW + KVW : QW + 2 * KVW],
        ga[None, :, QW + 2 * KVW :],
        gn[None, 0],
        gg[None],
        gu[None],
        gd[None],
        gn[None, 1],
    )


def t_dot(a, b):
    return lax.dot_general(a, b, (((0,), (0,)), ((), ())), preferred_element_type=F32)


def dot_t(a, b):
    return lax.dot_general(a, b, (((1,), (1,)), ((), ())), preferred_element_type=F32)


def shape_of(*dims, kind=BF):
    return jax.ShapeDtypeStruct(dims, kind)


def call(kernel, out_shape, *args, flops=0, grid=None, in_specs=None, out_specs=None, scratch=()):
    moved = sum(math.prod(a.shape) * a.dtype.itemsize for a in list(args) + list(out_shape))
    kwargs = {} if grid is None else {"grid": grid}
    held = moved + sum(math.prod(m.shape) * 4 for m in scratch)
    vmem = pl.BlockSpec(memory_space=pltpu.VMEM)
    smem = pl.BlockSpec(memory_space=pltpu.SMEM)
    return pl.pallas_call(
        kernel,
        out_shape=out_shape,
        in_specs=in_specs or [smem if a.dtype == jnp.int32 else vmem for a in args],
        out_specs=out_specs or [vmem] * len(out_shape),
        scratch_shapes=scratch,
        cost_estimate=pl.CostEstimate(flops=flops, bytes_accessed=moved, transcendentals=0),
        compiler_params=pltpu.CompilerParams(vmem_limit_bytes=min(60 << 20, held * 9 // 8 + (8 << 20))),
        **kwargs,
    )(*args)


def turn(u, cosine, sine, sign, first, last):
    rows, width = u.shape
    padded = -(-width // 128) * 128
    if padded > width:
        u = jnp.concatenate([u, jnp.zeros((rows, padded - width), F32)], axis=1)
    lane = lax.broadcasted_iota(jnp.int32, (rows, padded), 1)
    partner = jnp.where(
        lane % HEAD_DIM < HEAD_DIM // 2,
        pltpu.roll(u, padded - HEAD_DIM // 2, 1),
        pltpu.roll(u, HEAD_DIM // 2, 1),
    )
    cosine = jnp.concatenate([cosine[:rows]] * (padded // HEAD_DIM), axis=1)
    sine = jnp.concatenate([sine[:rows]] * (padded // HEAD_DIM), axis=1)
    turned = u * cosine + (partner * sine if sign > 0 else -(partner * sine))
    return jnp.where((lane >= first) & (lane < last), turned, u)[:, :width]


def inverse_norm(x):
    return lax.rsqrt(jnp.mean(x * x, axis=-1, keepdims=True) + EPSILON)


def project_kernel(count, *refs):
    parts, (order, w0, w1, cosine, sine, x_ref, n_ref, q_ref, kv_ref, gain_ref) = refs[:count], refs[count:]
    columns = jnp.concatenate([w0[:, GAINS - QKV :], w1[:, GAINS - QKV :]], axis=0)
    gains = lax.dot_general(columns, order[...], (((0,), (1,)), ((), ())), preferred_element_type=F32)
    gain_ref[...] = gains[:8]
    x = parts[0][...]
    for part in parts[1:]:
        x = x + part[...].astype(F32)
    x_ref[...] = x
    n = (x * inverse_norm(x) * gains[:1]).astype(BF)
    n = dot(n, order[...]).astype(BF)
    n_ref[...] = n
    half = w0.shape[0]
    out = dot(n[:, :half], w0[:, : GAINS - QKV]) + dot(n[:, half:], w1[:, : GAINS - QKV])
    kv = turn(out[:, : 2 * KVW], cosine[...], sine[...], 1, 0, KVW)
    kv_ref[...] = kv.astype(BF)
    q_ref[...] = turn(out[:, 2 * KVW :], cosine[...], sine[...], 1, 0, QW).astype(BF)


def run_project(parts, order, wa, tables):
    tok = parts[0].shape[0]
    args = list(parts) + [order, *wa, *tables]
    return call(
        functools.partial(project_kernel, len(parts)),
        [
            shape_of(tok, D, kind=F32),
            shape_of(tok, order.shape[1]),
            shape_of(tok, QW),
            shape_of(tok, 2 * KVW),
            shape_of(8, D, kind=F32),
        ],
        *args,
        flops=2 * tok * order.shape[1] * (D + QW + 2 * KVW),
    )


def project_all_kernel(*refs):
    x_ref, others = refs[0], refs[1:4]
    order, w0, w1, cosine, sine, n_ref, q_ref, kv0, kv1, kv2, kv3, gain_ref = refs[4:]
    columns = jnp.concatenate([w0[:, GAINS - QKV :], w1[:, GAINS - QKV :]], axis=0)
    gains = lax.dot_general(columns, order[...], (((0,), (1,)), ((), ())), preferred_element_type=F32)
    gain_ref[...] = gains[:8]
    x = x_ref[...]
    tok = x.shape[0]
    rows = [x * inverse_norm(x)] + [r[...].astype(F32) for r in others]
    n = (jnp.concatenate(rows, axis=0) * gains[:1]).astype(BF)
    n = dot(n, order[...]).astype(BF)
    n_ref[...] = n[:tok]
    half = w0.shape[0]
    kv = dot(n[:, :half], w0[:, : 2 * KVW]) + dot(n[:, half:], w1[:, : 2 * KVW])
    kv = turn(kv, cosine[...], sine[...], 1, 0, KVW).astype(BF)
    for k, out in enumerate((kv0, kv1, kv2, kv3)):
        out[...] = kv[k * tok : (k + 1) * tok]
    q = dot(n[:tok, :half], w0[:, 2 * KVW : GAINS - QKV]) + dot(n[:tok, half:], w1[:, 2 * KVW : GAINS - QKV])
    q_ref[...] = turn(q, cosine[...], sine[...], 1, 0, QW).astype(BF)


def run_project_all(x, others, order, wa, tables):
    tok = x.shape[0]
    n1, q, *kv, gains = call(
        project_all_kernel,
        [shape_of(tok, order.shape[1]), shape_of(tok, QW)]
        + [shape_of(tok, 2 * KVW)] * 4
        + [shape_of(8, D, kind=F32)],
        x, *others, order, *wa, *tables,
        flops=2 * tok * order.shape[1] * (4 * D + QW + 8 * KVW),
    )
    return x, n1, q, kv, gains


def causal(c, tok, count):
    shape = (GROUP * tok, count * tok)
    row = c * tok + lax.broadcasted_iota(jnp.int32, shape, 0) % tok
    lane = lax.broadcasted_iota(jnp.int32, shape, 1)
    key = jnp.zeros(shape, jnp.int32)
    for k in range(count):
        key = jnp.where(lane // tok == k, (c ^ k) * tok + lane % tok, key)
    return row >= key


def heads_of(x, j):
    return jnp.concatenate(
        [x[:, (GROUP * j + g) * HEAD_DIM : (GROUP * j + g + 1) * HEAD_DIM] for g in range(GROUP)], axis=0
    )


def attend_kernel(c_ref, x_ref, q_ref, kv0, kv1, kv2, kv3, gain, order, w0, w1, o_ref, op_ref, lse_ref, h_ref, n_ref):
    tok = q_ref.shape[0]
    kv = jnp.concatenate([kv0[...], kv1[...], kv2[...], kv3[...]], axis=0)
    q = q_ref[...]
    allowed = causal(c_ref[0], tok, 4)
    for j in range(KV_HEADS):
        k = kv[:, j * HEAD_DIM : (j + 1) * HEAD_DIM]
        v = kv[:, KVW + j * HEAD_DIM : KVW + (j + 1) * HEAD_DIM]
        scores = jnp.where(allowed, dot_t(heads_of(q, j), k) * HEAD_DIM**-0.5, MASKED)
        peak = jnp.max(scores, axis=-1, keepdims=True)
        e = jnp.exp(scores - peak)
        total = jnp.sum(e, axis=-1, keepdims=True)
        o = dot((e * (1.0 / total)).astype(BF), v).astype(BF)
        lse = peak + jnp.log(total)
        for g in range(GROUP):
            h = GROUP * j + g
            o_ref[:, h * HEAD_DIM : (h + 1) * HEAD_DIM] = o[g * tok : (g + 1) * tok]
            lse_ref[:, h : h + 1] = lse[g * tok : (g + 1) * tok]
    op = dot(o_ref[...], order[...]).astype(BF)
    op_ref[...] = op
    half = w0.shape[0]
    h1 = x_ref[...] + dot(op[:, :half], w0[:, :QW]) + dot(op[:, half:], w1[:, :QW])
    h_ref[...] = h1
    n_ref[...] = (h1 * inverse_norm(h1) * gain[1:2]).astype(BF)


def run_attend(c, x, q, kv, gain, order, wa):
    tok = q.shape[0]
    return call(
        attend_kernel,
        [
            shape_of(tok, QW),
            shape_of(tok, order.shape[1]),
            shape_of(tok, 16, kind=F32),
            shape_of(tok, D, kind=F32),
            shape_of(tok, D),
        ],
        c, x, q, *kv, gain, order, *wa,
        flops=2 * tok * (4 * tok * QW * 2 + order.shape[1] * D * 2),
    )


def token_rows(d_ref, *refs):
    if len(refs) == 1:
        d = d_ref[0]
        return jnp.concatenate([refs[0][d ^ k] for k in range(4)], axis=0)
    return jnp.concatenate([r[...] for r in refs], axis=0)


def ffn_kernel(d_ref, h_ref, n_ref, wg, wu, wd, gate_ref, up_ref, hidden_ref, p0, p1, p2, p3):
    n = token_rows(d_ref, n_ref)
    gate, up = dot(n, wg[...]), dot(n, wu[...])
    gate_ref[...], up_ref[...] = gate, up
    hidden = (gate * (1.0 / (1.0 + jnp.exp(-gate))) * up).astype(BF)
    hidden_ref[...] = hidden
    part = dot(hidden, wd[...])
    tok = h_ref.shape[0]
    p0[...] = h_ref[...] + part[:tok]
    for k, p in enumerate((p1, p2, p3), 1):
        p[...] = part[k * tok : (k + 1) * tok].astype(BF)


def run_ffn(d, h1, n2, wg, wu, wd):
    tok, width = h1.shape[0], wg.shape[1]
    return call(
        ffn_kernel,
        [shape_of(4 * tok, width, kind=F32)] * 2
        + [shape_of(4 * tok, width), shape_of(tok, D, kind=F32)]
        + [shape_of(tok, D)] * 3,
        d, h1, n2, wg, wu, wd,
        flops=6 * 4 * tok * width * D,
    )


def ffn_back_kernel(d_ref, *refs):
    gate_ref, up_ref, wg, wu, wd, dgate_ref, dup_ref, p0, p1, p2, p3 = refs[-11:]
    gb = token_rows(d_ref, *refs[:-11])
    dh = dot_t(gb, wd[...])
    gate, up = gate_ref[...], up_ref[...]
    sigma = 1.0 / (1.0 + jnp.exp(-gate))
    dgate = (dh * up * sigma * (1.0 + gate * (1.0 - sigma))).astype(BF)
    dup = (dh * gate * sigma).astype(BF)
    dgate_ref[...], dup_ref[...] = dgate, dup
    part = dot_t(dgate, wg[...]) + dot_t(dup, wu[...])
    tok = p0.shape[0]
    p0[...] = part[:tok]
    for k, p in enumerate((p1, p2, p3), 1):
        p[...] = part[k * tok : (k + 1) * tok].astype(BF)


def run_ffn_back(d, gb, gate, up, wg, wu, wd):
    tok, width = gate.shape[0] // 4, wg.shape[1]
    return call(
        ffn_back_kernel,
        [shape_of(4 * tok, width)] * 2 + [shape_of(tok, D, kind=F32)] + [shape_of(tok, D)] * 3,
        d, *gb, gate, up, wg, wu, wd,
        flops=6 * 4 * tok * width * D,
    )


def ffn_grads_kernel(s_ref, d_ref, dgate, dup, hidden, n_ref, *refs):
    n, gb = token_rows(d_ref, n_ref), token_rows(d_ref, *refs[:-5])
    gu_keep, gu_send, down_keep, down_send, down = refs[-5:]
    s = s_ref[0]
    a, b = dgate[...], dup[...]
    first = s == 0
    gu_keep[...] = t_dot(n, jnp.where(first, a, b)).astype(BF)
    gu_send[...] = t_dot(n, jnp.where(first, b, a)).astype(BF)
    down[...] = t_dot(hidden[...], gb)
    half = down.shape[0] // 2
    down_keep[...] = down[pl.ds(pl.multiple_of(s * half, half), half), :].astype(BF)
    down_send[...] = down[pl.ds(pl.multiple_of((1 - s) * half, half), half), :].astype(BF)


def run_ffn_grads(s, d, dgate, dup, hidden, n2, gb):
    tok, width = dgate.shape
    return call(
        ffn_grads_kernel,
        [shape_of(D, width)] * 2 + [shape_of(width // 2, D)] * 2,
        s, d, dgate, dup, hidden, n2, *gb,
        flops=6 * tok * width * D,
        scratch=[pltpu.VMEM((width, D), F32)],
    )


def attend_back_kernel(c_ref, *refs):
    parts, kv_refs = refs[:4], refs[4:8]
    h_ref, g_ref, q_ref, o_ref, lse_ref, gain, order, w0, w1, cosine, sine = refs[8:19]
    dh_ref, db_ref, gain_ref, dq_ref, d0, d1, d2, d3, dq_acc, dkv_acc = refs[19:]
    tok = q_ref.shape[0]
    dn = parts[0][...]
    for part in parts[1:]:
        dn = dn + part[...].astype(F32)
    h1 = h_ref[...]
    inverse = inverse_norm(h1)
    gain_ref[...] = jnp.sum(dn * h1 * inverse, axis=0, keepdims=True)
    scaled = dn * gain[1:2]
    dh = g_ref[...] + inverse * scaled - h1 * inverse**3 * jnp.mean(scaled * h1, axis=-1, keepdims=True)
    dh_ref[...] = dh
    db = dh.astype(BF)
    db_ref[...] = db
    dop = jnp.concatenate([dot_t(db, w0[:, :QW]), dot_t(db, w1[:, :QW])], axis=1).astype(BF)
    do = dot_t(dop, order[...]).astype(BF)
    kv = jnp.concatenate([r[...] for r in kv_refs], axis=0)
    q, o, lse_all = q_ref[...], o_ref[...], lse_ref[...]
    allowed = causal(c_ref[0], tok, 4)
    scale = HEAD_DIM**-0.5
    for j in range(KV_HEADS):
        k = kv[:, j * HEAD_DIM : (j + 1) * HEAD_DIM]
        v = kv[:, KVW + j * HEAD_DIM : KVW + (j + 1) * HEAD_DIM]
        qj, doj = heads_of(q, j), heads_of(do, j)
        delta = jnp.sum(doj.astype(F32) * heads_of(o, j).astype(F32), axis=-1, keepdims=True)
        lse = jnp.concatenate([lse_all[:, GROUP * j + g : GROUP * j + g + 1] for g in range(GROUP)], axis=0)
        probs = jnp.where(allowed, jnp.exp(dot_t(qj, k) * scale - lse), 0.0)
        dkv_acc[:, KVW + j * HEAD_DIM : KVW + (j + 1) * HEAD_DIM] = t_dot(probs.astype(BF), doj)
        ds = (probs * (dot_t(doj, v) - delta)).astype(BF)
        dkv_acc[:, j * HEAD_DIM : (j + 1) * HEAD_DIM] = t_dot(ds, qj) * scale
        dq = dot(ds, k) * scale
        for g in range(GROUP):
            h = GROUP * j + g
            dq_acc[:, h * HEAD_DIM : (h + 1) * HEAD_DIM] = dq[g * tok : (g + 1) * tok]
    dq_ref[...] = turn(dq_acc[...], cosine[...], sine[...], -1, 0, QW).astype(BF)
    d0[...] = dkv_acc[:tok]
    for k, d in enumerate((d1, d2, d3), 1):
        d[...] = dkv_acc[k * tok : (k + 1) * tok].astype(BF)


def run_attend_back(c, parts, kv, h1, g, q, o, lse, gain, order, wa, tables):
    tok = q.shape[0]
    return call(
        attend_back_kernel,
        [
            shape_of(tok, D, kind=F32),
            shape_of(tok, D),
            shape_of(1, D, kind=F32),
            shape_of(tok, QW),
            shape_of(tok, 2 * KVW, kind=F32),
        ]
        + [shape_of(tok, 2 * KVW)] * 3,
        c, *parts, *kv, h1, g, q, o, lse, gain, order, *wa, *tables,
        flops=2 * tok * (4 * tok * QW * 5 + order.shape[1] * D * 2),
        scratch=[pltpu.VMEM((tok, QW), F32), pltpu.VMEM((4 * tok, 2 * KVW), F32)],
    )


def project_back_kernel(*refs):
    parts, refs = refs[:4], refs[4:]
    dq_ref, x_ref, dh_ref, gain_f, gain, order, w0, w1, cosine, sine = refs[:10]
    in_ref, gb_ref, dqkv_ref, gains_ref = refs[10:]
    dkv = parts[0][...]
    for part in parts[1:]:
        dkv = dkv + part[...].astype(F32)
    dkv = turn(dkv, cosine[...], sine[...], -1, 0, KVW).astype(BF)
    dqkv_ref[:, : 2 * KVW] = dkv
    dqkv_ref[:, 2 * KVW :] = dq_ref[...]
    dqkv = dqkv_ref[...]
    ds = jnp.concatenate([dot_t(dqkv, w0[:, : GAINS - QKV]), dot_t(dqkv, w1[:, : GAINS - QKV])], axis=1)
    high = ds.astype(BF)
    low = (ds - high.astype(F32)).astype(BF)
    dn = dot_t(high, order[...]) + dot_t(low, order[...])
    x = x_ref[...]
    inverse = inverse_norm(x)
    gain_a = jnp.sum(dn * x * inverse, axis=0, keepdims=True)
    scaled = dn * gain[:1]
    out = dh_ref[...] + inverse * scaled - x * inverse**3 * jnp.mean(scaled * x, axis=-1, keepdims=True)
    in_ref[...] = out
    gb_ref[...] = out.astype(BF)
    row = lax.broadcasted_iota(jnp.int32, (16, D), 0)
    both = jnp.where(row == 0, gain_a, jnp.where(row == 1, gain_f[...], 0.0)).astype(BF)
    gains_ref[...] = dot(both, order[...]).astype(BF)


def run_project_back(parts, dq, x, dh1, gain_f, gain, order, wa, tables):
    tok = dq.shape[0]
    return call(
        project_back_kernel,
        [shape_of(tok, D, kind=F32), shape_of(tok, D), shape_of(tok, QW + 2 * KVW), shape_of(16, order.shape[1])],
        *parts, dq, x, dh1, gain_f, gain, order, *wa, *tables,
        flops=2 * tok * order.shape[1] * (2 * D + QW + 2 * KVW),
    )


def attention_grads_kernel(op0, op1, n0, n1, g0, g1, db_ref, dqkv_ref, keep_ref, send_ref):
    db, dqkv = db_ref[...], dqkv_ref[...]
    row = lax.broadcasted_iota(jnp.int32, (16, WIDTH - GAINS), 0)
    ones = (row == lax.broadcasted_iota(jnp.int32, (16, WIDTH - GAINS), 1)).astype(F32).astype(BF)
    for op, n, g, out in ((op0, n0, g0, keep_ref), (op1, n1, g1, send_ref)):
        out[:, WO:QW] = t_dot(op[...], db).astype(BF)
        out[:, QW:QKV] = jnp.zeros((out.shape[0], QKV - QW), BF)
        out[:, QKV:GAINS] = t_dot(n[...], dqkv).astype(BF)
        out[:, GAINS:] = t_dot(g[...], ones).astype(BF)


def run_attention_grads(op, db, n1, dqkv, gains):
    tok, rows = op.shape
    block = rows // 4

    def halves(height):
        return [pl.BlockSpec((height, block), lambda i: (0, i)), pl.BlockSpec((height, block), lambda i: (0, i + 2))]

    return call(
        attention_grads_kernel,
        [shape_of(rows // 2, WIDTH)] * 2,
        op, op, n1, n1, gains, gains, db, dqkv,
        flops=2 * tok * rows * WIDTH,
        grid=(2,),
        in_specs=halves(tok) + halves(tok) + halves(16)
        + [pl.BlockSpec((tok, QW), lambda i: (0, 0)), pl.BlockSpec((tok, QW + 2 * KVW), lambda i: (0, 0))],
        out_specs=[pl.BlockSpec((block, WIDTH), lambda i: (i, 0))] * 2,
    )


def add_kernel(a, b, out):
    out[...] = (a[...].astype(F32) + b[...].astype(F32)).astype(BF)


def run_add(a, b):
    return call(add_kernel, [shape_of(*a.shape)], a, b)[0]


def split_sum_kernel(axis, *refs):
    pairs = len(refs) // 4
    for i in range(pairs):
        a, b = refs[2 * i : 2 * i + 2]
        keep, send = refs[2 * pairs + 2 * i : 2 * pairs + 2 * i + 2]
        total = (a[...].astype(F32) + b[...].astype(F32)).astype(BF)
        keep[...], send[...] = total[0], total[1]


def pack(gu, down, out):
    rows, width = gu.shape
    unit = down.shape[0]
    out[:rows, :] = gu
    out[rows : rows + unit, :] = down[:, :width]
    out[rows + unit :, : width // 2] = down[: unit // 2, width:]
    out[rows + unit :, width // 2 :] = down[unit // 2 :, width:]


def unpack(packed, rows, unit):
    packed = packed.astype(F32)
    width = packed.shape[1]
    tail = packed[rows + unit :]
    tail = jnp.concatenate([tail[:, : width // 2], tail[:, width // 2 :]], axis=0)
    return packed[:rows], jnp.concatenate([packed[rows : rows + unit], tail], axis=1)


def ffn_split_kernel(c_ref, gu_a, gu_b, down_a, down_b, *outs):
    c = c_ref[0]
    for k, out in enumerate(outs):
        sums = []
        for a, b in ((gu_a, gu_b), (down_a, down_b)):
            rows = a.shape[0] // 4
            block = pl.ds(pl.multiple_of((c ^ k) * rows, rows), rows)
            sums.append((a[block, :].astype(F32) + b[block, :].astype(F32)).astype(BF))
        pack(*sums, out)


def run_ffn_split(c, gu_a, gu_b, down_a, down_b):
    width = gu_a.shape[1]
    rows = (gu_a.size + down_a.size) // (4 * width)
    return call(ffn_split_kernel, [shape_of(rows, width)] * 4, c, gu_a, gu_b, down_a, down_b)


def ffn_total_kernel(*refs):
    refs[4][...] = sum(r[...].astype(F32) for r in refs[:4]).astype(BF)


def run_ffn_total(blocks):
    return call(ffn_total_kernel, [shape_of(*blocks[0].shape)], *blocks)[0]


def ffn_pick_kernel(s_ref, *refs):
    first = s_ref[0] == 0
    rows = refs[0].shape[0]
    keep, send = refs[8:]
    for k in range(4):
        a, b = refs[k][...], refs[4 + k][...]
        keep[k * rows : (k + 1) * rows, :] = jnp.where(first, a, b)
        send[k * rows : (k + 1) * rows, :] = jnp.where(first, b, a)


def run_ffn_pick(s, layer0, layer1):
    rows, width = layer0[0].shape
    return call(ffn_pick_kernel, [shape_of(4 * rows, width)] * 2, s, *layer0, *layer1)


def ffn_out_kernel(s_ref, c_ref, keep, got, gate, up, whole):
    s, c = s_ref[0], c_ref[0]
    rows, unit = gate.shape[0] // 4, whole.shape[0] // 8
    size = keep.shape[0] // 4
    first = s == 0
    for k in range(4):
        (a, x), (b, y) = (unpack(r[k * size : (k + 1) * size, :], rows, unit) for r in (keep, got))
        block = pl.ds(pl.multiple_of((c ^ k) * rows, rows), rows)
        gate[block, :] = jnp.where(first, a, b)
        up[block, :] = jnp.where(first, b, a)
        for half, v in ((s, x), (1 - s, y)):
            whole[pl.ds(pl.multiple_of((half * 4 + (c ^ k)) * unit, unit), unit), :] = v


def run_ffn_out(s, c, keep, got):
    width = keep.shape[1]
    out = [shape_of(D, width, kind=F32)] * 2 + [shape_of(width, D, kind=F32)]
    return call(ffn_out_kernel, out, s, c, keep, got)


def first_split_kernel(keep_ref, got_ref, a_keep, a_send, b_keep, b_send):
    total = (keep_ref[...].astype(F32) + got_ref[...].astype(F32)).astype(BF)
    for i in range(2):
        a_keep[i], a_send[i] = total[2 * i, :2], total[2 * i + 1, :2]
        b_keep[i], b_send[i] = total[i, 2:], total[2 + i, 2:]


def run_first_split(keep, got):
    shape = (4, 4, keep.shape[0] // 16, keep.shape[1])
    return call(
        first_split_kernel,
        [shape_of(2, 2, *shape[2:])] * 4,
        keep.reshape(shape), got.reshape(shape),
    )


def run_split_sum(a, a1, b, b1):
    out = [shape_of(*a.shape[1:])] * 2 + [shape_of(*b.shape[1:])] * 2
    return call(functools.partial(split_sum_kernel, 0), out, a, a1, b, b1)


def dp_split_kernel(a, a1, b, b1, own, s1, s2, s3):
    x = a[...].astype(F32) + a1[...].astype(F32)
    y = b[...].astype(F32) + b1[...].astype(F32)
    own[...] = x[0]
    s1[...], s2[...], s3[...] = x[1].astype(BF), y[0].astype(BF), y[1].astype(BF)


def run_dp_split(a, a1, b, b1):
    shape = a.shape[1:]
    return call(dp_split_kernel, [shape_of(*shape, kind=F32)] + [shape_of(*shape)] * 3, a, a1, b, b1)


def owner_sum_kernel(s_ref, *refs):
    now, later = (sum(r[...].astype(F32) for r in refs[k : k + 4]).astype(BF) for k in (0, 4))
    keep, send = refs[8:]
    first = s_ref[0] == 0
    keep[...] = jnp.where(first, now, later)
    send[...] = jnp.where(first, later, now)


def run_owner_sum(s, now, later):
    return call(owner_sum_kernel, [shape_of(*now[0].shape)] * 2, s, *now, *later)


def attention_out_kernel(order, u0, u1, u2, u3, wo, gains, wk, wv, wq):
    rows = jnp.concatenate([u[h] for u in (u0, u1, u2, u3) for h in range(2)], axis=0)
    out = dot(order[...], rows)
    wo[...] = out[:, WO:QW]
    gains[...] = out[:, GAINS:]
    turned = lax.dot_general(
        rows[:, QKV : QKV + 2 * KVW], order[...], (((0,), (1,)), ((), ())), preferred_element_type=F32
    )
    wk[...], wv[...] = turned[:KVW], turned[KVW:]
    wq[...] = out[:, QKV + 2 * KVW : GAINS]


def run_attention_out(order, units):
    rows = order.shape[0]
    shapes = ((rows, QW), (rows, WIDTH - GAINS), (KVW, rows), (KVW, rows), (rows, QW))
    return call(
        attention_out_kernel,
        [shape_of(*shape, kind=F32) for shape in shapes],
        order, *units,
        flops=2 * rows * order.shape[1] * WIDTH,
    )


def swap(x, axis, bit):
    return lax.ppermute(x, axis, [(i, i ^ bit) for i in range(lax.axis_size(axis))])


def spread(x, axis):
    return [x] + [swap(x, axis, k) for k in range(1, 4)]


def deliver(blocks, axis):
    return [blocks[0]] + [swap(b, axis, k) for k, b in enumerate(blocks[1:], 1)]


def pick(x, index, axis=0):
    return lax.dynamic_index_in_dim(x, index, axis, keepdims=False)


def tie(*values):
    return lax.optimization_barrier(values)


def plane_gather(a, b):
    a1, b1 = swap(a, "ctx", 2), swap(b, "ctx", 1)
    a2, b2 = swap(jnp.stack([a, a1]), "ctx", 1), swap(jnp.stack([b, b1]), "ctx", 2)
    return jnp.stack([a, a2[0], a1, a2[1]]), jnp.stack([b, b1, b2[0], b2[1]])


WO, QKV = 0, QW + 64
GAINS = QKV + QW + 2 * KVW
WIDTH = GAINS + 64
PAD = 256


def row_orders(s, c, d):
    p = jnp.arange(4 * PAD, dtype=jnp.int32)
    row = (((p // 128) % 4) ^ c) * 64 + ((p // 512) ^ s) * 32 + p % 32
    feature = jnp.where(row < D // 4, (((p // 32) % 4) ^ d) * (D // 4) + row, -1)
    order = (jnp.arange(D, dtype=jnp.int32)[:, None] == feature[None, :]).astype(BF)
    p = jnp.arange(PAD, dtype=jnp.int32)
    out = ((p // 64) ^ c) * 64 + (((p // 32) % 2) ^ s) * 32 + p % 32
    return order, (jnp.arange(D // 4, dtype=jnp.int32)[:, None] == out[None, :]).astype(BF)


def body_fast(
    block_input, out_grad, w_query, w_key, w_value, w_out, norm_attn, w_gate, w_up, w_down, norm_ffn
):
    s, c, d = (lax.axis_index(n) for n in ("section", "ctx", "dp"))
    s1, c1, d1 = (i.astype(jnp.int32).reshape(1) for i in (s, c, d))
    tok = block_input.shape[2]
    cosine, sine = rope_tables(
        jnp.concatenate([(c ^ k) * tok + jnp.arange(tok, dtype=jnp.int32) for k in range(4)])
    )
    sign = jnp.where(jnp.arange(HEAD_DIM) < HEAD_DIM // 2, -1.0, 1.0)
    tables = cosine, sine * sign
    x = pick(block_input[:, 0], s)
    g = pick(out_grad[:, 0], s)

    def by_layer(own, got):
        return jnp.where(s == 0, own, got), jnp.where(s == 0, got, own)

    def own_rows(w):
        return pick(jnp.pad(w, ((0, PAD - w.shape[0]), (0, 0))).reshape(4, 2, 32, w.shape[1]), c)

    gains = own_rows(jnp.stack([norm_attn[0], norm_ffn[0]], axis=1))
    gains = jnp.pad(gains, ((0, 0), (0, 0), (0, WIDTH - GAINS - 2)))
    own = [own_rows(w[0]) for w in (w_out, w_key, w_value, w_query)]
    own = jnp.concatenate([own[0], jnp.zeros((2, 32, QKV - QW), BF), *own[1:], gains], axis=2)
    unit0, unit1 = by_layer(pick(own, s), swap(pick(own, 1 - s), "section", 1))
    ffn = [by_layer(w[0], swap(w[0], "section", 1)) for w in (w_gate, w_up, w_down)]
    unit0, s, c, d, w_gate, w_up, w_down, x = tie(unit0, s, c, d, w_gate, w_up, w_down, x)
    z = spread(unit0, "dp")
    others = (x * inverse_norm(x)).astype(BF)
    gb1 = g.astype(BF)
    z[2:], others, unit1, gb1 = tie(z[2:], spread(others, "ctx")[1:], unit1, gb1)
    order0, order_out = row_orders(s, c, d)

    def first_step(a, b):
        return a, swap(a, "ctx", 2), b, swap(b, "ctx", 1)

    def second_step(a, a1, b, b1):
        return a, a1, swap(jnp.stack([a, a1]), "ctx", 1), b, b1, swap(jnp.stack([b, b1]), "ctx", 2)

    def whole_half(a, a1, a2, b, b1, b2):
        a, b = jnp.stack([a, a2[0], a1, a2[1]]), jnp.stack([b, b1, b2[0], b2[1]])
        whole = jnp.concatenate([a, b], axis=1).reshape(512, WIDTH)
        return whole[:, :QKV], whole[:, QKV:]

    steps = second_step(*first_step(jnp.stack(z[:2]), jnp.stack(z[2:])))
    mine, gb1_2, z1, (ffn, order0, order_out, tables, x, g, gb1) = tie(
        whole_half(*steps), swap(gb1, "dp", 2), spread(unit1, "dp"), (ffn, order0, order_out, tables, x, g, gb1)
    )
    wa0 = [(w, swap(w, "section", 1)) for w in mine]

    def nothing(*values):
        return values

    def forward(parts, wa, order, w, beside, values, others=None):
        if others is None:
            x, n1, q, kv, gains = run_project(parts, order, wa[1], tables)
            kv, values = tie(spread(kv, "ctx"), beside[0](*values))
        else:
            x, n1, q, kv, gains = run_project_all(parts[0], others, order, wa[1], tables)
            values = beside[0](*values)
        o, op, lse, h1, n2 = run_attend(c1, x, q, kv, gains, order, wa[0])
        n2, values = tie(n2, values)
        n2, values = tie(lax.all_gather(n2, "dp"), beside[1](*values))
        gate, up, hidden, *parts = run_ffn(d1, h1, n2, *w)
        if beside[2] is not None:
            parts, values = tie(deliver(parts, "dp"), beside[2](*values))
        return parts, (x, n1, q, kv, o, op, lse, h1, n2, gate, up, hidden, gains), values

    def backward(g, gb, kept, wa, order, w, beside, values):
        x, n1, q, kv, o, op, lse, h1, n2, gate, up, hidden, gains = kept
        dgate, dup, *parts = run_ffn_back(d1, gb, gate, up, *w)
        parts = deliver(parts, "dp")
        values = beside[0](*values)
        gu_keep, gu_send, down_keep, down_send = run_ffn_grads(s1, d1, dgate, dup, hidden, n2, gb)
        sums = run_ffn_split(c1, gu_keep, swap(gu_send, "section", 1), down_keep, swap(down_send, "section", 1))
        parts, sums, values = tie(parts, sums, values)
        values = beside[1](*values)
        dh1, db, gain_f, dq, *dkv = run_attend_back(c1, parts, kv, h1, g, q, o, lse, gains, order, wa[0], tables)
        dkv, values = tie(dkv, values)
        sums = deliver(sums, "ctx")
        dkv, values, sums = tie(deliver(dkv, "ctx"), beside[2](*values), sums)
        g, gb, dqkv, gains = run_project_back(dkv, dq, x, dh1, gain_f, gains, order, wa[1], tables)
        return g, gb, (op, db, n1, dqkv, gains), sums, values

    w0, w1 = ([pair[l] for pair in ffn] for l in range(2))
    parts, kept0, wa1 = forward(
        [x], wa0, order0, w0,
        (
            lambda *z: first_step(jnp.stack(z[:2]), jnp.stack(z[2:])),
            second_step,
            lambda *steps: [(w, swap(w, "section", 1)) for w in whole_half(*steps)],
        ),
        z1, others,
    )
    out1, kept1, (gb1_1, gb1_3) = forward(
        parts, wa1, order0, w1, (lambda v: (swap(v, "dp", 1), swap(v, "dp", 3)), nothing, None), (gb1,)
    )
    out0 = kept1[0]
    gb = [gb1, gb1_1, gb1_2, gb1_3]
    in1, gb, operands, ffn1, out1 = backward(
        g, gb, kept1, wa1, order0, w1,
        (
            nothing,
            nothing,
            lambda own, p1, p2, p3: (own, swap(p1, "dp", 1), p2, swap(p3, "dp", 3)),
        ),
        out1,
    )
    ffn1 = spread(run_ffn_total(ffn1), "ctx")
    gb, operands, ffn1 = tie(lax.all_gather(gb, "dp"), operands, ffn1)
    keep, send = run_attention_grads(*operands)
    gb, keep, send = tie(gb, keep, send)

    def scatter_first(a, a1, b, b1):
        return a, swap(a1, "ctx", 1), b, swap(b1, "ctx", 2)

    def scatter_second(a, a1, b, b1):
        return a, swap(a1, "ctx", 2), b, swap(b1, "ctx", 1)

    in0, _, operands, ffn0, later = backward(
        in1, [gb], kept0, wa0, order0, w0,
        (
            lambda keep, got: scatter_first(*run_first_split(keep, got)),
            lambda *steps: scatter_second(*run_split_sum(*steps)),
            lambda *steps: deliver(run_dp_split(*steps), "dp"),
        ),
        (keep, swap(send, "section", 1)),
    )
    keep, send = run_attention_grads(*operands)
    steps = scatter_first(*run_first_split(keep, swap(send, "section", 1)))
    steps = tie(*steps)
    steps, ffn0 = tie(scatter_second(*run_split_sum(*steps)), ffn0)
    blocks = deliver(run_dp_split(*steps), "dp")
    ffn0 = spread(run_ffn_total(ffn0), "ctx")
    blocks, ffn0 = tie(blocks, ffn0)
    keep, send = run_owner_sum(s1, blocks, later)
    unit = jnp.stack([keep, swap(send, "section", 1)])
    unit, ffn0, ffn1 = tie(unit, ffn0, ffn1)
    keep, send = run_ffn_pick(s1, ffn0, ffn1)
    gate, up, down = run_ffn_out(s1, c1, keep, swap(send, "section", 1))
    def own_layer(p0, p1):
        keep, send = by_layer(p0, p1)
        got = swap(send, "section", 1)
        return jnp.stack(by_layer(keep, got))

    units, gate, up, down, (in0, in1), out1_2 = tie(
        spread(unit, "ctx"), gate, up, down, (in0, in1), swap(out1[2], "dp", 2)
    )
    out1 = out1[0] + sum(p.astype(F32) for p in (out1[1], out1_2, out1[3]))
    wo, gains, wk, wv, wq = run_attention_out(order_out, units)
    return (
        own_layer(out0, out1)[None, :, None],
        own_layer(in0, in1)[None, :, None],
        wq[None],
        wk.T[None],
        wv.T[None],
        wo[None],
        gains[None, :, 0],
        gate[None],
        up[None],
        down[None],
        gains[None, :, 1],
    )


def body(*args):
    sizes = [lax.axis_size(name) for name in ("section", "ctx", "dp")]
    return (body_fast if sizes == [2, 4, 4] else body_plain)(*args)


def solution(mesh):
    return jax.shard_map(
        body,
        mesh=mesh,
        in_specs=(
            P(None, "dp", "ctx", None),
            P(None, "dp", "ctx", None),
            P("section", "dp", None),
            P("section", "dp", None),
            P("section", "dp", None),
            P("section", "dp", None),
            P("section", "dp"),
            P("section", None, "dp"),
            P("section", None, "dp"),
            P("section", "dp", None),
            P("section", "dp"),
        ),
        out_specs=(
            P("section", None, "dp", "ctx", None),
            P("section", None, "dp", "ctx", None),
            P("section", "dp", None),
            P("section", "dp", None),
            P("section", "dp", None),
            P("section", "dp", None),
            P("section", "dp"),
            P("section", None, "dp"),
            P("section", None, "dp"),
            P("section", "dp", None),
            P("section", "dp"),
        ),
        check_vma=False,
    )
```

```python
import functools
import math

import jax
import jax.numpy as jnp
from jax import lax
from jax.experimental import pallas as pl
from jax.experimental.pallas import tpu as pltpu
from jax.sharding import PartitionSpec as P

D = 960
HEADS = 15
KV_HEADS = 5
HEAD_DIM = 64
QW = 960
KVW = 320
GROUP = 3
EPSILON = 1e-05
ROPE_BASE = 10000.0
MASKED = -1e30
BF = jnp.bfloat16
F32 = jnp.float32


def dot(a, b):
    return jnp.dot(a, b, preferred_element_type=F32)


def rope_tables(positions):
    half_dim = HEAD_DIM // 2
    freq_rows = ROPE_BASE ** (-(jnp.arange(half_dim, dtype=F32) * 2.0 / HEAD_DIM))
    angles = positions.astype(F32)[:, None] * freq_rows[None, :]
    cosine = jnp.concatenate([jnp.cos(angles), jnp.cos(angles)], axis=1)
    sine_rows = jnp.concatenate([jnp.sin(angles), jnp.sin(angles)], axis=1)
    return (cosine, sine_rows)


def turn_half(u):
    half_dim = HEAD_DIM // 2
    return jnp.concatenate([-u[..., half_dim:], u[..., :half_dim]], axis=-1)


def rotate(u, cosine, sine_rows):
    return u * cosine[:, None, :] + turn_half(u) * sine_rows[:, None, :]


def unrotate(u, cosine, sine_rows):
    return u * cosine[:, None, :] - turn_half(u * sine_rows[:, None, :])


def normalize(x, gain):
    inverse = lax.rsqrt(jnp.mean(x * x, axis=-1, keepdims=True) + EPSILON)
    return (x * inverse * gain, inverse)


def normalize_back(x, inverse, gain, grad):
    scaled = grad * gain
    gain_grad = jnp.sum(grad * x * inverse, axis=0)
    value_grad = inverse * scaled - x * inverse**3 * jnp.mean(scaled * x, axis=-1, keepdims=True)
    return (value_grad, gain_grad)


def attend(q, k, v, query_pos):
    tok = q.shape[0]
    q = q.reshape(tok, KV_HEADS, GROUP, HEAD_DIM)
    scores = jnp.einsum("tkgd,skd->kgts", q, k, preferred_element_type=F32) * HEAD_DIM**-0.5
    allowed = query_pos[:, None] >= jnp.arange(k.shape[0], dtype=jnp.int32)[None, :]
    scores = jnp.where(allowed, scores, MASKED)
    peak = jnp.max(scores, axis=-1, keepdims=True)
    e = jnp.exp(scores - peak)
    total = jnp.sum(e, axis=-1, keepdims=True)
    probs = (e / total).astype(BF)
    o = jnp.einsum("kgts,skd->tkgd", probs, v, preferred_element_type=F32).reshape(tok, QW)
    return o.astype(BF), (peak + jnp.log(total))[..., 0]


def attend_back(q, k, v, lse, do, o, query_pos):
    tok = q.shape[0]
    q = q.reshape(tok, KV_HEADS, GROUP, HEAD_DIM)
    dor = do.reshape(tok, KV_HEADS, GROUP, HEAD_DIM)
    delta = jnp.sum((do.astype(F32) * o.astype(F32)).reshape(tok, KV_HEADS, GROUP, HEAD_DIM), axis=-1)
    delta = jnp.transpose(delta, (1, 2, 0))
    scale = HEAD_DIM**-0.5
    scores = jnp.einsum("tkgd,skd->kgts", q, k, preferred_element_type=F32) * scale
    allowed = query_pos[:, None] >= jnp.arange(k.shape[0], dtype=jnp.int32)[None, :]
    probs = jnp.where(allowed, jnp.exp(scores - lse[..., None]), 0.0)
    dv = jnp.einsum("kgts,tkgd->skd", probs.astype(BF), dor, preferred_element_type=F32)
    dp = jnp.einsum("tkgd,skd->kgts", dor, v, preferred_element_type=F32)
    ds = (probs * (dp - delta[..., None])).astype(BF)
    dq = jnp.einsum("kgts,skd->tkgd", ds, k, preferred_element_type=F32) * scale
    dk = jnp.einsum("kgts,tkgd->skd", ds, q, preferred_element_type=F32) * scale
    dkv = jnp.concatenate([dk.reshape(-1, KVW), dv.reshape(-1, KVW)], axis=1)
    return dq.reshape(tok, HEADS, HEAD_DIM), dkv


def layer_forward(x, w, cosine, sine, query_pos):
    wa, wg, wu, wd, ga, gf = w
    tok = x.shape[0]
    n1, r1 = normalize(x, ga)
    n1 = n1.astype(BF)
    qkv = dot(n1, wa[:, : QW + 2 * KVW])
    q = rotate(qkv[:, :QW].reshape(tok, HEADS, HEAD_DIM), cosine, sine).astype(BF)
    k = rotate(qkv[:, QW : QW + KVW].reshape(tok, KV_HEADS, HEAD_DIM), cosine, sine)
    kv = jnp.concatenate([k.reshape(tok, KVW), qkv[:, QW + KVW :]], axis=1).astype(BF)
    kv = lax.all_gather(kv, "ctx", axis=0, tiled=True)
    k = kv[:, :KVW].reshape(-1, KV_HEADS, HEAD_DIM)
    v = kv[:, KVW:].reshape(-1, KV_HEADS, HEAD_DIM)
    o, lse = attend(q, k, v, query_pos)
    h1 = x + dot(o, wa[:, QW + 2 * KVW :])
    n2, r2 = normalize(h1, gf)
    n2 = lax.all_gather(n2.astype(BF), "dp", axis=0, tiled=True)
    gate = dot(n2, wg)
    up = dot(n2, wu)
    hidden = (jax.nn.silu(gate) * up).astype(BF)
    part = dot(hidden, wd).astype(BF)
    out = h1 + lax.psum_scatter(part, "dp", scatter_dimension=0, tiled=True).astype(F32)
    return out, (x, n1, r1, q, k, v, o, lse, h1, n2, r2, gate, up, hidden)


def layer_backward(g, kept, w, cosine, sine, query_pos):
    wa, wg, wu, wd, ga, gf = w
    x, n1, r1, q, k, v, o, lse, h1, n2, r2, gate, up, hidden = kept
    tok = x.shape[0]
    gb = lax.all_gather(g.astype(BF), "dp", axis=0, tiled=True)
    grad_down = dot(hidden.T, gb)
    dh = dot(gb, wd.T)
    sigma = jax.nn.sigmoid(gate)
    dgate = (dh * up * sigma * (1.0 + gate * (1.0 - sigma))).astype(BF)
    dup = (dh * gate * sigma).astype(BF)
    grad_gate = dot(n2.T, dgate)
    grad_up = dot(n2.T, dup)
    part = (dot(dgate, wg.T) + dot(dup, wu.T)).astype(BF)
    dn2 = lax.psum_scatter(part, "dp", scatter_dimension=0, tiled=True).astype(F32)
    back_f, gain_f = normalize_back(h1, r2, gf, dn2)
    dh1 = g + back_f
    db = dh1.astype(BF)
    grad_out = dot(o.T, db)
    do = dot(db, wa[:, QW + 2 * KVW :].T).astype(BF)
    dq, dkv = attend_back(q, k, v, lse, do, o, query_pos)
    dkv = lax.psum_scatter(dkv.astype(BF), "ctx", scatter_dimension=0, tiled=True).astype(F32)
    dq = unrotate(dq, cosine, sine).reshape(tok, QW)
    dk = unrotate(dkv[:, :KVW].reshape(tok, KV_HEADS, HEAD_DIM), cosine, sine).reshape(tok, KVW)
    dqkv = jnp.concatenate([dq, dk, dkv[:, KVW:]], axis=1).astype(BF)
    grad_qkv = dot(n1.T, dqkv)
    dn1 = dot(dqkv, wa[:, : QW + 2 * KVW].T)
    back_a, gain_a = normalize_back(x, r1, ga, dn1)
    grads = (
        jnp.concatenate([grad_qkv, grad_out], axis=1).astype(BF),
        jnp.stack([gain_a, gain_f]),
        grad_gate.astype(BF),
        grad_up.astype(BF),
        grad_down.astype(BF),
    )
    return dh1 + back_a, grads


def swap_section(p0, p1, section_id):
    mine = jnp.where(section_id == 0, p0, p1)
    other = jnp.where(section_id == 0, p1, p0)
    count = lax.axis_size("section")
    got = lax.ppermute(other, "section", [(i, count - 1 - i) for i in range(count)])
    return mine.astype(F32) + got.astype(F32)


def own_layer(p0, p1, section_id):
    mine = jnp.where(section_id == 0, p0, p1)
    other = jnp.where(section_id == 0, p1, p0)
    count = lax.axis_size("section")
    got = lax.ppermute(other, "section", [(i, count - 1 - i) for i in range(count)])
    first = jnp.where(section_id == 0, mine, got)
    second = jnp.where(section_id == 0, got, mine)
    return jnp.stack([first, second])


def body_plain(
    block_input, out_grad, w_query, w_key, w_value, w_out, norm_attn, w_gate, w_up, w_down, norm_ffn
):
    section_id = lax.axis_index("section")
    tok_rows = block_input.shape[2]
    query_pos = lax.axis_index("ctx") * tok_rows + jnp.arange(tok_rows, dtype=jnp.int32)
    cosine, sine = rope_tables(query_pos)
    x = lax.dynamic_index_in_dim(block_input[:, 0], section_id, 0, keepdims=False)
    g = lax.dynamic_index_in_dim(out_grad[:, 0], section_id, 0, keepdims=False)
    wa = jnp.concatenate([w_query[0], w_key[0], w_value[0], w_out[0]], axis=1)
    wa = lax.all_gather(lax.all_gather(wa, "dp", axis=0, tiled=True), "section")
    gains = jnp.stack([norm_attn[0], norm_ffn[0]])
    gains = lax.all_gather(lax.all_gather(gains, "dp", axis=1, tiled=True), "section").astype(F32)
    wg = lax.all_gather(w_gate[0], "section")
    wu = lax.all_gather(w_up[0], "section")
    wd = lax.all_gather(w_down[0], "section")
    layers = [(wa[l], wg[l], wu[l], wd[l], gains[l, 0], gains[l, 1]) for l in range(2)]
    out0, kept0 = layer_forward(x, layers[0], cosine, sine, query_pos)
    out1, kept1 = layer_forward(out0, layers[1], cosine, sine, query_pos)
    in1, grads1 = layer_backward(g, kept1, layers[1], cosine, sine, query_pos)
    in0, grads0 = layer_backward(in1, kept0, layers[0], cosine, sine, query_pos)
    section_outs = own_layer(out0, out1, section_id)
    in_grads = own_layer(in0, in1, section_id)
    ga, gn, gg, gu, gd = (
        swap_section(a, b, section_id) for a, b in zip(grads0, grads1)
    )
    ga = lax.psum_scatter(ga.astype(BF), "dp", scatter_dimension=0, tiled=True)
    ga = lax.psum(ga, "ctx").astype(F32)
    gn = lax.psum_scatter(gn, "dp", scatter_dimension=1, tiled=True)
    gn = lax.psum(gn, "ctx")
    gg = lax.psum(gg.astype(BF), "ctx").astype(F32)
    gu = lax.psum(gu.astype(BF), "ctx").astype(F32)
    gd = lax.psum(gd.astype(BF), "ctx").astype(F32)
    return (
        section_outs[None, :, None],
        in_grads[None, :, None],
        ga[None, :, :QW],
        ga[None, :, QW : QW + KVW],
        ga[None, :, QW + KVW : QW + 2 * KVW],
        ga[None, :, QW + 2 * KVW :],
        gn[None, 0],
        gg[None],
        gu[None],
        gd[None],
        gn[None, 1],
    )


def t_dot(a, b):
    return lax.dot_general(a, b, (((0,), (0,)), ((), ())), preferred_element_type=F32)


def dot_t(a, b):
    return lax.dot_general(a, b, (((1,), (1,)), ((), ())), preferred_element_type=F32)


def shape_of(*dims, kind=BF):
    return jax.ShapeDtypeStruct(dims, kind)


def call(kernel, out_shape, *args, flops=0, grid=None, in_specs=None, out_specs=None, scratch=()):
    moved = sum(math.prod(a.shape) * a.dtype.itemsize for a in list(args) + list(out_shape))
    kwargs = {} if grid is None else {"grid": grid}
    held = moved + sum(math.prod(m.shape) * 4 for m in scratch)
    vmem = pl.BlockSpec(memory_space=pltpu.VMEM)
    smem = pl.BlockSpec(memory_space=pltpu.SMEM)
    return pl.pallas_call(
        kernel,
        out_shape=out_shape,
        in_specs=in_specs or [smem if a.dtype == jnp.int32 else vmem for a in args],
        out_specs=out_specs or [vmem] * len(out_shape),
        scratch_shapes=scratch,
        cost_estimate=pl.CostEstimate(flops=flops, bytes_accessed=moved, transcendentals=0),
        compiler_params=pltpu.CompilerParams(vmem_limit_bytes=min(60 << 20, held * 9 // 8 + (8 << 20))),
        **kwargs,
    )(*args)


def turn(u, cosine, sine, sign, first, last):
    rows, width = u.shape
    padded = -(-width // 128) * 128
    if padded > width:
        u = jnp.concatenate([u, jnp.zeros((rows, padded - width), F32)], axis=1)
    lane = lax.broadcasted_iota(jnp.int32, (rows, padded), 1)
    partner = jnp.where(
        lane % HEAD_DIM < HEAD_DIM // 2,
        pltpu.roll(u, padded - HEAD_DIM // 2, 1),
        pltpu.roll(u, HEAD_DIM // 2, 1),
    )
    cosine = jnp.concatenate([cosine[:rows]] * (padded // HEAD_DIM), axis=1)
    sine = jnp.concatenate([sine[:rows]] * (padded // HEAD_DIM), axis=1)
    turned = u * cosine + (partner * sine if sign > 0 else -(partner * sine))
    return jnp.where((lane >= first) & (lane < last), turned, u)[:, :width]


def inverse_norm(x):
    return lax.rsqrt(jnp.mean(x * x, axis=-1, keepdims=True) + EPSILON)


def project_kernel(count, *refs):
    parts, (order, w0, w1, cosine, sine, x_ref, n_ref, q_ref, kv_ref, gain_ref) = refs[:count], refs[count:]
    columns = jnp.concatenate([w0[:, GAINS - QKV :], w1[:, GAINS - QKV :]], axis=0)
    gains = lax.dot_general(columns, order[...], (((0,), (1,)), ((), ())), preferred_element_type=F32)
    gain_ref[...] = gains[:8]
    x = parts[0][...]
    for part in parts[1:]:
        x = x + part[...].astype(F32)
    x_ref[...] = x
    n = (x * inverse_norm(x) * gains[:1]).astype(BF)
    n = dot(n, order[...]).astype(BF)
    n_ref[...] = n
    half = w0.shape[0]
    out = dot(n[:, :half], w0[:, : GAINS - QKV]) + dot(n[:, half:], w1[:, : GAINS - QKV])
    kv = turn(out[:, : 2 * KVW], cosine[...], sine[...], 1, 0, KVW)
    kv_ref[...] = kv.astype(BF)
    q_ref[...] = turn(out[:, 2 * KVW :], cosine[...], sine[...], 1, 0, QW).astype(BF)


def run_project(parts, order, wa, tables):
    tok = parts[0].shape[0]
    args = list(parts) + [order, *wa, *tables]
    return call(
        functools.partial(project_kernel, len(parts)),
        [
            shape_of(tok, D, kind=F32),
            shape_of(tok, order.shape[1]),
            shape_of(tok, QW),
            shape_of(tok, 2 * KVW),
            shape_of(8, D, kind=F32),
        ],
        *args,
        flops=2 * tok * order.shape[1] * (D + QW + 2 * KVW),
    )


def project_all_kernel(*refs):
    x_ref, others = refs[0], refs[1:4]
    order, w0, w1, cosine, sine, n_ref, q_ref, kv0, kv1, kv2, kv3, gain_ref = refs[4:]
    columns = jnp.concatenate([w0[:, GAINS - QKV :], w1[:, GAINS - QKV :]], axis=0)
    gains = lax.dot_general(columns, order[...], (((0,), (1,)), ((), ())), preferred_element_type=F32)
    gain_ref[...] = gains[:8]
    x = x_ref[...]
    tok = x.shape[0]
    rows = [x * inverse_norm(x)] + [r[...].astype(F32) for r in others]
    n = (jnp.concatenate(rows, axis=0) * gains[:1]).astype(BF)
    n = dot(n, order[...]).astype(BF)
    n_ref[...] = n[:tok]
    half = w0.shape[0]
    kv = dot(n[:, :half], w0[:, : 2 * KVW]) + dot(n[:, half:], w1[:, : 2 * KVW])
    kv = turn(kv, cosine[...], sine[...], 1, 0, KVW).astype(BF)
    for k, out in enumerate((kv0, kv1, kv2, kv3)):
        out[...] = kv[k * tok : (k + 1) * tok]
    q = dot(n[:tok, :half], w0[:, 2 * KVW : GAINS - QKV]) + dot(n[:tok, half:], w1[:, 2 * KVW : GAINS - QKV])
    q_ref[...] = turn(q, cosine[...], sine[...], 1, 0, QW).astype(BF)


def run_project_all(x, others, order, wa, tables):
    tok = x.shape[0]
    n1, q, *kv, gains = call(
        project_all_kernel,
        [shape_of(tok, order.shape[1]), shape_of(tok, QW)]
        + [shape_of(tok, 2 * KVW)] * 4
        + [shape_of(8, D, kind=F32)],
        x, *others, order, *wa, *tables,
        flops=2 * tok * order.shape[1] * (4 * D + QW + 8 * KVW),
    )
    return x, n1, q, kv, gains


def causal(c, tok, count):
    shape = (GROUP * tok, count * tok)
    row = c * tok + lax.broadcasted_iota(jnp.int32, shape, 0) % tok
    lane = lax.broadcasted_iota(jnp.int32, shape, 1)
    key = jnp.zeros(shape, jnp.int32)
    for k in range(count):
        key = jnp.where(lane // tok == k, (c ^ k) * tok + lane % tok, key)
    return row >= key


def heads_of(x, j):
    return jnp.concatenate(
        [x[:, (GROUP * j + g) * HEAD_DIM : (GROUP * j + g + 1) * HEAD_DIM] for g in range(GROUP)], axis=0
    )


def attend_kernel(c_ref, x_ref, q_ref, kv0, kv1, kv2, kv3, gain, order, w0, w1, o_ref, op_ref, lse_ref, h_ref, n_ref):
    tok = q_ref.shape[0]
    kv = jnp.concatenate([kv0[...], kv1[...], kv2[...], kv3[...]], axis=0)
    q = q_ref[...]
    allowed = causal(c_ref[0], tok, 4)
    for j in range(KV_HEADS):
        k = kv[:, j * HEAD_DIM : (j + 1) * HEAD_DIM]
        v = kv[:, KVW + j * HEAD_DIM : KVW + (j + 1) * HEAD_DIM]
        scores = jnp.where(allowed, dot_t(heads_of(q, j), k) * HEAD_DIM**-0.5, MASKED)
        peak = jnp.max(scores, axis=-1, keepdims=True)
        e = jnp.exp(scores - peak)
        total = jnp.sum(e, axis=-1, keepdims=True)
        o = dot((e * (1.0 / total)).astype(BF), v).astype(BF)
        lse = peak + jnp.log(total)
        for g in range(GROUP):
            h = GROUP * j + g
            o_ref[:, h * HEAD_DIM : (h + 1) * HEAD_DIM] = o[g * tok : (g + 1) * tok]
            lse_ref[:, h : h + 1] = lse[g * tok : (g + 1) * tok]
    op = dot(o_ref[...], order[...]).astype(BF)
    op_ref[...] = op
    half = w0.shape[0]
    h1 = x_ref[...] + dot(op[:, :half], w0[:, :QW]) + dot(op[:, half:], w1[:, :QW])
    h_ref[...] = h1
    n_ref[...] = (h1 * inverse_norm(h1) * gain[1:2]).astype(BF)


def run_attend(c, x, q, kv, gain, order, wa):
    tok = q.shape[0]
    return call(
        attend_kernel,
        [
            shape_of(tok, QW),
            shape_of(tok, order.shape[1]),
            shape_of(tok, 16, kind=F32),
            shape_of(tok, D, kind=F32),
            shape_of(tok, D),
        ],
        c, x, q, *kv, gain, order, *wa,
        flops=2 * tok * (4 * tok * QW * 2 + order.shape[1] * D * 2),
    )


def token_rows(d_ref, *refs):
    if len(refs) == 1:
        d = d_ref[0]
        return jnp.concatenate([refs[0][d ^ k] for k in range(4)], axis=0)
    return jnp.concatenate([r[...] for r in refs], axis=0)


def ffn_kernel(d_ref, h_ref, n_ref, wg, wu, wd, gate_ref, up_ref, hidden_ref, p0, p1, p2, p3):
    n = token_rows(d_ref, n_ref)
    gate, up = dot(n, wg[...]), dot(n, wu[...])
    gate_ref[...], up_ref[...] = gate, up
    hidden = (gate * (1.0 / (1.0 + jnp.exp(-gate))) * up).astype(BF)
    hidden_ref[...] = hidden
    part = dot(hidden, wd[...])
    tok = h_ref.shape[0]
    p0[...] = h_ref[...] + part[:tok]
    for k, p in enumerate((p1, p2, p3), 1):
        p[...] = part[k * tok : (k + 1) * tok].astype(BF)


def run_ffn(d, h1, n2, wg, wu, wd):
    tok, width = h1.shape[0], wg.shape[1]
    return call(
        ffn_kernel,
        [shape_of(4 * tok, width, kind=F32)] * 2
        + [shape_of(4 * tok, width), shape_of(tok, D, kind=F32)]
        + [shape_of(tok, D)] * 3,
        d, h1, n2, wg, wu, wd,
        flops=6 * 4 * tok * width * D,
    )


def ffn_back_kernel(d_ref, *refs):
    gate_ref, up_ref, wg, wu, wd, dgate_ref, dup_ref, p0, p1, p2, p3 = refs[-11:]
    gb = token_rows(d_ref, *refs[:-11])
    dh = dot_t(gb, wd[...])
    gate, up = gate_ref[...], up_ref[...]
    sigma = 1.0 / (1.0 + jnp.exp(-gate))
    dgate = (dh * up * sigma * (1.0 + gate * (1.0 - sigma))).astype(BF)
    dup = (dh * gate * sigma).astype(BF)
    dgate_ref[...], dup_ref[...] = dgate, dup
    part = dot_t(dgate, wg[...]) + dot_t(dup, wu[...])
    tok = p0.shape[0]
    p0[...] = part[:tok]
    for k, p in enumerate((p1, p2, p3), 1):
        p[...] = part[k * tok : (k + 1) * tok].astype(BF)


def run_ffn_back(d, gb, gate, up, wg, wu, wd):
    tok, width = gate.shape[0] // 4, wg.shape[1]
    return call(
        ffn_back_kernel,
        [shape_of(4 * tok, width)] * 2 + [shape_of(tok, D, kind=F32)] + [shape_of(tok, D)] * 3,
        d, *gb, gate, up, wg, wu, wd,
        flops=6 * 4 * tok * width * D,
    )


def ffn_grads_kernel(s_ref, d_ref, dgate, dup, hidden, n_ref, *refs):
    n, gb = token_rows(d_ref, n_ref), token_rows(d_ref, *refs[:-5])
    gu_keep, gu_send, down_keep, down_send, down = refs[-5:]
    s = s_ref[0]
    a, b = dgate[...], dup[...]
    first = s == 0
    gu_keep[...] = t_dot(n, jnp.where(first, a, b)).astype(BF)
    gu_send[...] = t_dot(n, jnp.where(first, b, a)).astype(BF)
    down[...] = t_dot(hidden[...], gb)
    half = down.shape[0] // 2
    down_keep[...] = down[pl.ds(pl.multiple_of(s * half, half), half), :].astype(BF)
    down_send[...] = down[pl.ds(pl.multiple_of((1 - s) * half, half), half), :].astype(BF)


def run_ffn_grads(s, d, dgate, dup, hidden, n2, gb):
    tok, width = dgate.shape
    return call(
        ffn_grads_kernel,
        [shape_of(D, width)] * 2 + [shape_of(width // 2, D)] * 2,
        s, d, dgate, dup, hidden, n2, *gb,
        flops=6 * tok * width * D,
        scratch=[pltpu.VMEM((width, D), F32)],
    )


def attend_back_kernel(c_ref, *refs):
    parts, kv_refs = refs[:4], refs[4:8]
    h_ref, g_ref, q_ref, o_ref, lse_ref, gain, order, w0, w1, cosine, sine = refs[8:19]
    dh_ref, db_ref, gain_ref, dq_ref, d0, d1, d2, d3, dq_acc, dkv_acc = refs[19:]
    tok = q_ref.shape[0]
    dn = parts[0][...]
    for part in parts[1:]:
        dn = dn + part[...].astype(F32)
    h1 = h_ref[...]
    inverse = inverse_norm(h1)
    gain_ref[...] = jnp.sum(dn * h1 * inverse, axis=0, keepdims=True)
    scaled = dn * gain[1:2]
    dh = g_ref[...] + inverse * scaled - h1 * inverse**3 * jnp.mean(scaled * h1, axis=-1, keepdims=True)
    dh_ref[...] = dh
    db = dh.astype(BF)
    db_ref[...] = db
    dop = jnp.concatenate([dot_t(db, w0[:, :QW]), dot_t(db, w1[:, :QW])], axis=1).astype(BF)
    do = dot_t(dop, order[...]).astype(BF)
    kv = jnp.concatenate([r[...] for r in kv_refs], axis=0)
    q, o, lse_all = q_ref[...], o_ref[...], lse_ref[...]
    allowed = causal(c_ref[0], tok, 4)
    scale = HEAD_DIM**-0.5
    for j in range(KV_HEADS):
        k = kv[:, j * HEAD_DIM : (j + 1) * HEAD_DIM]
        v = kv[:, KVW + j * HEAD_DIM : KVW + (j + 1) * HEAD_DIM]
        qj, doj = heads_of(q, j), heads_of(do, j)
        delta = jnp.sum(doj.astype(F32) * heads_of(o, j).astype(F32), axis=-1, keepdims=True)
        lse = jnp.concatenate([lse_all[:, GROUP * j + g : GROUP * j + g + 1] for g in range(GROUP)], axis=0)
        probs = jnp.where(allowed, jnp.exp(dot_t(qj, k) * scale - lse), 0.0)
        dkv_acc[:, KVW + j * HEAD_DIM : KVW + (j + 1) * HEAD_DIM] = t_dot(probs.astype(BF), doj)
        ds = (probs * (dot_t(doj, v) - delta)).astype(BF)
        dkv_acc[:, j * HEAD_DIM : (j + 1) * HEAD_DIM] = t_dot(ds, qj) * scale
        dq = dot(ds, k) * scale
        for g in range(GROUP):
            h = GROUP * j + g
            dq_acc[:, h * HEAD_DIM : (h + 1) * HEAD_DIM] = dq[g * tok : (g + 1) * tok]
    dq_ref[...] = turn(dq_acc[...], cosine[...], sine[...], -1, 0, QW).astype(BF)
    d0[...] = dkv_acc[:tok]
    for k, d in enumerate((d1, d2, d3), 1):
        d[...] = dkv_acc[k * tok : (k + 1) * tok].astype(BF)


def run_attend_back(c, parts, kv, h1, g, q, o, lse, gain, order, wa, tables):
    tok = q.shape[0]
    return call(
        attend_back_kernel,
        [
            shape_of(tok, D, kind=F32),
            shape_of(tok, D),
            shape_of(1, D, kind=F32),
            shape_of(tok, QW),
            shape_of(tok, 2 * KVW, kind=F32),
        ]
        + [shape_of(tok, 2 * KVW)] * 3,
        c, *parts, *kv, h1, g, q, o, lse, gain, order, *wa, *tables,
        flops=2 * tok * (4 * tok * QW * 5 + order.shape[1] * D * 2),
        scratch=[pltpu.VMEM((tok, QW), F32), pltpu.VMEM((4 * tok, 2 * KVW), F32)],
    )


def project_back_kernel(*refs):
    parts, refs = refs[:4], refs[4:]
    dq_ref, x_ref, dh_ref, gain_f, gain, order, w0, w1, cosine, sine = refs[:10]
    in_ref, gb_ref, dqkv_ref, gains_ref = refs[10:]
    dkv = parts[0][...]
    for part in parts[1:]:
        dkv = dkv + part[...].astype(F32)
    dkv = turn(dkv, cosine[...], sine[...], -1, 0, KVW).astype(BF)
    dqkv_ref[:, : 2 * KVW] = dkv
    dqkv_ref[:, 2 * KVW :] = dq_ref[...]
    dqkv = dqkv_ref[...]
    ds = jnp.concatenate([dot_t(dqkv, w0[:, : GAINS - QKV]), dot_t(dqkv, w1[:, : GAINS - QKV])], axis=1)
    high = ds.astype(BF)
    low = (ds - high.astype(F32)).astype(BF)
    dn = dot_t(high, order[...]) + dot_t(low, order[...])
    x = x_ref[...]
    inverse = inverse_norm(x)
    gain_a = jnp.sum(dn * x * inverse, axis=0, keepdims=True)
    scaled = dn * gain[:1]
    out = dh_ref[...] + inverse * scaled - x * inverse**3 * jnp.mean(scaled * x, axis=-1, keepdims=True)
    in_ref[...] = out
    gb_ref[...] = out.astype(BF)
    row = lax.broadcasted_iota(jnp.int32, (16, D), 0)
    both = jnp.where(row == 0, gain_a, jnp.where(row == 1, gain_f[...], 0.0)).astype(BF)
    gains_ref[...] = dot(both, order[...]).astype(BF)


def run_project_back(parts, dq, x, dh1, gain_f, gain, order, wa, tables):
    tok = dq.shape[0]
    return call(
        project_back_kernel,
        [shape_of(tok, D, kind=F32), shape_of(tok, D), shape_of(tok, QW + 2 * KVW), shape_of(16, order.shape[1])],
        *parts, dq, x, dh1, gain_f, gain, order, *wa, *tables,
        flops=2 * tok * order.shape[1] * (2 * D + QW + 2 * KVW),
    )


def attention_grads_kernel(op0, op1, n0, n1, g0, g1, db_ref, dqkv_ref, keep_ref, send_ref):
    db, dqkv = db_ref[...], dqkv_ref[...]
    row = lax.broadcasted_iota(jnp.int32, (16, WIDTH - GAINS), 0)
    ones = (row == lax.broadcasted_iota(jnp.int32, (16, WIDTH - GAINS), 1)).astype(F32).astype(BF)
    for op, n, g, out in ((op0, n0, g0, keep_ref), (op1, n1, g1, send_ref)):
        out[:, WO:QW] = t_dot(op[...], db).astype(BF)
        out[:, QW:QKV] = jnp.zeros((out.shape[0], QKV - QW), BF)
        out[:, QKV:GAINS] = t_dot(n[...], dqkv).astype(BF)
        out[:, GAINS:] = t_dot(g[...], ones).astype(BF)


def run_attention_grads(op, db, n1, dqkv, gains):
    tok, rows = op.shape
    block = rows // 4

    def halves(height):
        return [pl.BlockSpec((height, block), lambda i: (0, i)), pl.BlockSpec((height, block), lambda i: (0, i + 2))]

    return call(
        attention_grads_kernel,
        [shape_of(rows // 2, WIDTH)] * 2,
        op, op, n1, n1, gains, gains, db, dqkv,
        flops=2 * tok * rows * WIDTH,
        grid=(2,),
        in_specs=halves(tok) + halves(tok) + halves(16)
        + [pl.BlockSpec((tok, QW), lambda i: (0, 0)), pl.BlockSpec((tok, QW + 2 * KVW), lambda i: (0, 0))],
        out_specs=[pl.BlockSpec((block, WIDTH), lambda i: (i, 0))] * 2,
    )


def add_kernel(a, b, out):
    out[...] = (a[...].astype(F32) + b[...].astype(F32)).astype(BF)


def run_add(a, b):
    return call(add_kernel, [shape_of(*a.shape)], a, b)[0]


def split_sum_kernel(axis, *refs):
    pairs = len(refs) // 4
    for i in range(pairs):
        a, b = refs[2 * i : 2 * i + 2]
        keep, send = refs[2 * pairs + 2 * i : 2 * pairs + 2 * i + 2]
        total = (a[...].astype(F32) + b[...].astype(F32)).astype(BF)
        keep[...], send[...] = total[0], total[1]


def pack(gu, down, out):
    rows, width = gu.shape
    unit = down.shape[0]
    out[:rows, :] = gu
    out[rows : rows + unit, :] = down[:, :width]
    out[rows + unit :, : width // 2] = down[: unit // 2, width:]
    out[rows + unit :, width // 2 :] = down[unit // 2 :, width:]


def unpack(packed, rows, unit):
    packed = packed.astype(F32)
    width = packed.shape[1]
    tail = packed[rows + unit :]
    tail = jnp.concatenate([tail[:, : width // 2], tail[:, width // 2 :]], axis=0)
    return packed[:rows], jnp.concatenate([packed[rows : rows + unit], tail], axis=1)


def ffn_split_kernel(c_ref, gu_a, gu_b, down_a, down_b, *outs):
    c = c_ref[0]
    for k, out in enumerate(outs):
        sums = []
        for a, b in ((gu_a, gu_b), (down_a, down_b)):
            rows = a.shape[0] // 4
            block = pl.ds(pl.multiple_of((c ^ k) * rows, rows), rows)
            sums.append((a[block, :].astype(F32) + b[block, :].astype(F32)).astype(BF))
        pack(*sums, out)


def run_ffn_split(c, gu_a, gu_b, down_a, down_b):
    width = gu_a.shape[1]
    rows = (gu_a.size + down_a.size) // (4 * width)
    return call(ffn_split_kernel, [shape_of(rows, width)] * 4, c, gu_a, gu_b, down_a, down_b)


def ffn_total_kernel(*refs):
    refs[4][...] = sum(r[...].astype(F32) for r in refs[:4]).astype(BF)


def run_ffn_total(blocks):
    return call(ffn_total_kernel, [shape_of(*blocks[0].shape)], *blocks)[0]


def ffn_pick_kernel(s_ref, *refs):
    first = s_ref[0] == 0
    rows = refs[0].shape[0]
    keep, send = refs[8:]
    for k in range(4):
        a, b = refs[k][...], refs[4 + k][...]
        keep[k * rows : (k + 1) * rows, :] = jnp.where(first, a, b)
        send[k * rows : (k + 1) * rows, :] = jnp.where(first, b, a)


def run_ffn_pick(s, layer0, layer1):
    rows, width = layer0[0].shape
    return call(ffn_pick_kernel, [shape_of(4 * rows, width)] * 2, s, *layer0, *layer1)


def ffn_out_kernel(s_ref, c_ref, keep, got, gate, up, whole):
    s, c = s_ref[0], c_ref[0]
    rows, unit = gate.shape[0] // 4, whole.shape[0] // 8
    size = keep.shape[0] // 4
    first = s == 0
    for k in range(4):
        (a, x), (b, y) = (unpack(r[k * size : (k + 1) * size, :], rows, unit) for r in (keep, got))
        block = pl.ds(pl.multiple_of((c ^ k) * rows, rows), rows)
        gate[block, :] = jnp.where(first, a, b)
        up[block, :] = jnp.where(first, b, a)
        for half, v in ((s, x), (1 - s, y)):
            whole[pl.ds(pl.multiple_of((half * 4 + (c ^ k)) * unit, unit), unit), :] = v


def run_ffn_out(s, c, keep, got):
    width = keep.shape[1]
    out = [shape_of(D, width, kind=F32)] * 2 + [shape_of(width, D, kind=F32)]
    return call(ffn_out_kernel, out, s, c, keep, got)


def first_split_kernel(keep_ref, got_ref, a_keep, a_send, b_keep, b_send):
    total = (keep_ref[...].astype(F32) + got_ref[...].astype(F32)).astype(BF)
    for i in range(2):
        a_keep[i], a_send[i] = total[2 * i, :2], total[2 * i + 1, :2]
        b_keep[i], b_send[i] = total[i, 2:], total[2 + i, 2:]


def run_first_split(keep, got):
    shape = (4, 4, keep.shape[0] // 16, keep.shape[1])
    return call(
        first_split_kernel,
        [shape_of(2, 2, *shape[2:])] * 4,
        keep.reshape(shape), got.reshape(shape),
    )


def run_split_sum(a, a1, b, b1):
    out = [shape_of(*a.shape[1:])] * 2 + [shape_of(*b.shape[1:])] * 2
    return call(functools.partial(split_sum_kernel, 0), out, a, a1, b, b1)


def dp_split_kernel(a, a1, b, b1, own, s1, s2, s3):
    x = a[...].astype(F32) + a1[...].astype(F32)
    y = b[...].astype(F32) + b1[...].astype(F32)
    own[...] = x[0]
    s1[...], s2[...], s3[...] = x[1].astype(BF), y[0].astype(BF), y[1].astype(BF)


def run_dp_split(a, a1, b, b1):
    shape = a.shape[1:]
    return call(dp_split_kernel, [shape_of(*shape, kind=F32)] + [shape_of(*shape)] * 3, a, a1, b, b1)


def owner_sum_kernel(s_ref, *refs):
    now, later = (sum(r[...].astype(F32) for r in refs[k : k + 4]).astype(BF) for k in (0, 4))
    keep, send = refs[8:]
    first = s_ref[0] == 0
    keep[...] = jnp.where(first, now, later)
    send[...] = jnp.where(first, later, now)


def run_owner_sum(s, now, later):
    return call(owner_sum_kernel, [shape_of(*now[0].shape)] * 2, s, *now, *later)


def attention_out_kernel(order, u0, u1, u2, u3, wo, gains, wk, wv, wq):
    rows = jnp.concatenate([u[h] for u in (u0, u1, u2, u3) for h in range(2)], axis=0)
    out = dot(order[...], rows)
    wo[...] = out[:, WO:QW]
    gains[...] = out[:, GAINS:]
    turned = lax.dot_general(
        rows[:, QKV : QKV + 2 * KVW], order[...], (((0,), (1,)), ((), ())), preferred_element_type=F32
    )
    wk[...], wv[...] = turned[:KVW], turned[KVW:]
    wq[...] = out[:, QKV + 2 * KVW : GAINS]


def run_attention_out(order, units):
    rows = order.shape[0]
    shapes = ((rows, QW), (rows, WIDTH - GAINS), (KVW, rows), (KVW, rows), (rows, QW))
    return call(
        attention_out_kernel,
        [shape_of(*shape, kind=F32) for shape in shapes],
        order, *units,
        flops=2 * rows * order.shape[1] * WIDTH,
    )


def swap(x, axis, bit):
    return lax.ppermute(x, axis, [(i, i ^ bit) for i in range(lax.axis_size(axis))])


def spread(x, axis):
    return [x] + [swap(x, axis, k) for k in range(1, 4)]


def deliver(blocks, axis):
    return [blocks[0]] + [swap(b, axis, k) for k, b in enumerate(blocks[1:], 1)]


def pick(x, index, axis=0):
    return lax.dynamic_index_in_dim(x, index, axis, keepdims=False)


def tie(*values):
    return lax.optimization_barrier(values)


def plane_gather(a, b):
    a1, b1 = swap(a, "ctx", 2), swap(b, "ctx", 1)
    a2, b2 = swap(jnp.stack([a, a1]), "ctx", 1), swap(jnp.stack([b, b1]), "ctx", 2)
    return jnp.stack([a, a2[0], a1, a2[1]]), jnp.stack([b, b1, b2[0], b2[1]])


WO, QKV = 0, QW + 64
GAINS = QKV + QW + 2 * KVW
WIDTH = GAINS + 64
PAD = 256


def row_orders(s, c, d):
    p = jnp.arange(4 * PAD, dtype=jnp.int32)
    row = (((p // 128) % 4) ^ c) * 64 + ((p // 512) ^ s) * 32 + p % 32
    feature = jnp.where(row < D // 4, (((p // 32) % 4) ^ d) * (D // 4) + row, -1)
    order = (jnp.arange(D, dtype=jnp.int32)[:, None] == feature[None, :]).astype(BF)
    p = jnp.arange(PAD, dtype=jnp.int32)
    out = ((p // 64) ^ c) * 64 + (((p // 32) % 2) ^ s) * 32 + p % 32
    return order, (jnp.arange(D // 4, dtype=jnp.int32)[:, None] == out[None, :]).astype(BF)


def body_fast(
    block_input, out_grad, w_query, w_key, w_value, w_out, norm_attn, w_gate, w_up, w_down, norm_ffn
):
    s, c, d = (lax.axis_index(n) for n in ("section", "ctx", "dp"))
    s1, c1, d1 = (i.astype(jnp.int32).reshape(1) for i in (s, c, d))
    tok = block_input.shape[2]
    cosine, sine = rope_tables(
        jnp.concatenate([(c ^ k) * tok + jnp.arange(tok, dtype=jnp.int32) for k in range(4)])
    )
    sign = jnp.where(jnp.arange(HEAD_DIM) < HEAD_DIM // 2, -1.0, 1.0)
    tables = cosine, sine * sign
    x = pick(block_input[:, 0], s)
    g = pick(out_grad[:, 0], s)

    def by_layer(own, got):
        return jnp.where(s == 0, own, got), jnp.where(s == 0, got, own)

    def own_rows(w):
        return pick(jnp.pad(w, ((0, PAD - w.shape[0]), (0, 0))).reshape(4, 2, 32, w.shape[1]), c)

    gains = own_rows(jnp.stack([norm_attn[0], norm_ffn[0]], axis=1))
    gains = jnp.pad(gains, ((0, 0), (0, 0), (0, WIDTH - GAINS - 2)))
    own = [own_rows(w[0]) for w in (w_out, w_key, w_value, w_query)]
    own = jnp.concatenate([own[0], jnp.zeros((2, 32, QKV - QW), BF), *own[1:], gains], axis=2)
    unit0, unit1 = by_layer(pick(own, s), swap(pick(own, 1 - s), "section", 1))
    ffn = [by_layer(w[0], swap(w[0], "section", 1)) for w in (w_gate, w_up, w_down)]
    unit0, s, c, d, w_gate, w_up, w_down, x = tie(unit0, s, c, d, w_gate, w_up, w_down, x)
    z = spread(unit0, "dp")
    others = (x * inverse_norm(x)).astype(BF)
    gb1 = g.astype(BF)
    z[2:], others, unit1, gb1 = tie(z[2:], spread(others, "ctx")[1:], unit1, gb1)
    order0, order_out = row_orders(s, c, d)

    def first_step(a, b):
        return a, swap(a, "ctx", 2), b, swap(b, "ctx", 1)

    def second_step(a, a1, b, b1):
        return a, a1, swap(jnp.stack([a, a1]), "ctx", 1), b, b1, swap(jnp.stack([b, b1]), "ctx", 2)

    def whole_half(a, a1, a2, b, b1, b2):
        a, b = jnp.stack([a, a2[0], a1, a2[1]]), jnp.stack([b, b1, b2[0], b2[1]])
        whole = jnp.concatenate([a, b], axis=1).reshape(512, WIDTH)
        return whole[:, :QKV], whole[:, QKV:]

    steps = second_step(*first_step(jnp.stack(z[:2]), jnp.stack(z[2:])))
    mine, gb1_2, z1, (ffn, order0, order_out, tables, x, g, gb1) = tie(
        whole_half(*steps), swap(gb1, "dp", 2), spread(unit1, "dp"), (ffn, order0, order_out, tables, x, g, gb1)
    )
    wa0 = [(w, swap(w, "section", 1)) for w in mine]

    def nothing(*values):
        return values

    def forward(parts, wa, order, w, beside, values, others=None):
        if others is None:
            x, n1, q, kv, gains = run_project(parts, order, wa[1], tables)
            kv, values = tie(spread(kv, "ctx"), beside[0](*values))
        else:
            x, n1, q, kv, gains = run_project_all(parts[0], others, order, wa[1], tables)
            values = beside[0](*values)
        o, op, lse, h1, n2 = run_attend(c1, x, q, kv, gains, order, wa[0])
        n2, values = tie(n2, values)
        n2, values = tie(lax.all_gather(n2, "dp"), beside[1](*values))
        gate, up, hidden, *parts = run_ffn(d1, h1, n2, *w)
        if beside[2] is not None:
            parts, values = tie(deliver(parts, "dp"), beside[2](*values))
        return parts, (x, n1, q, kv, o, op, lse, h1, n2, gate, up, hidden, gains), values

    def backward(g, gb, kept, wa, order, w, beside, values):
        x, n1, q, kv, o, op, lse, h1, n2, gate, up, hidden, gains = kept
        dgate, dup, *parts = run_ffn_back(d1, gb, gate, up, *w)
        parts = deliver(parts, "dp")
        values = beside[0](*values)
        gu_keep, gu_send, down_keep, down_send = run_ffn_grads(s1, d1, dgate, dup, hidden, n2, gb)
        sums = run_ffn_split(c1, gu_keep, swap(gu_send, "section", 1), down_keep, swap(down_send, "section", 1))
        parts, sums, values = tie(parts, sums, values)
        values = beside[1](*values)
        dh1, db, gain_f, dq, *dkv = run_attend_back(c1, parts, kv, h1, g, q, o, lse, gains, order, wa[0], tables)
        dkv, values = tie(dkv, values)
        sums = deliver(sums, "ctx")
        dkv, values, sums = tie(deliver(dkv, "ctx"), beside[2](*values), sums)
        g, gb, dqkv, gains = run_project_back(dkv, dq, x, dh1, gain_f, gains, order, wa[1], tables)
        return g, gb, (op, db, n1, dqkv, gains), sums, values

    w0, w1 = ([pair[l] for pair in ffn] for l in range(2))
    parts, kept0, wa1 = forward(
        [x], wa0, order0, w0,
        (
            lambda *z: first_step(jnp.stack(z[:2]), jnp.stack(z[2:])),
            second_step,
            lambda *steps: [(w, swap(w, "section", 1)) for w in whole_half(*steps)],
        ),
        z1, others,
    )
    out1, kept1, (gb1_1, gb1_3) = forward(
        parts, wa1, order0, w1, (lambda v: (swap(v, "dp", 1), swap(v, "dp", 3)), nothing, None), (gb1,)
    )
    out0 = kept1[0]
    gb = [gb1, gb1_1, gb1_2, gb1_3]
    in1, gb, operands, ffn1, out1 = backward(
        g, gb, kept1, wa1, order0, w1,
        (
            nothing,
            nothing,
            lambda own, p1, p2, p3: (own, swap(p1, "dp", 1), p2, swap(p3, "dp", 3)),
        ),
        out1,
    )
    ffn1 = spread(run_ffn_total(ffn1), "ctx")
    gb, operands, ffn1 = tie(lax.all_gather(gb, "dp"), operands, ffn1)
    keep, send = run_attention_grads(*operands)
    gb, keep, send = tie(gb, keep, send)

    def scatter_first(a, a1, b, b1):
        return a, swap(a1, "ctx", 1), b, swap(b1, "ctx", 2)

    def scatter_second(a, a1, b, b1):
        return a, swap(a1, "ctx", 2), b, swap(b1, "ctx", 1)

    in0, _, operands, ffn0, later = backward(
        in1, [gb], kept0, wa0, order0, w0,
        (
            lambda keep, got: scatter_first(*run_first_split(keep, got)),
            lambda *steps: scatter_second(*run_split_sum(*steps)),
            lambda *steps: deliver(run_dp_split(*steps), "dp"),
        ),
        (keep, swap(send, "section", 1)),
    )
    keep, send = run_attention_grads(*operands)
    steps = scatter_first(*run_first_split(keep, swap(send, "section", 1)))
    steps, out1_2 = tie(steps, swap(out1[2], "dp", 2))
    out1 = out1[0] + sum(p.astype(F32) for p in (out1[1], out1_2, out1[3]))
    steps, ffn0 = tie(scatter_second(*run_split_sum(*steps)), ffn0)
    blocks = deliver(run_dp_split(*steps), "dp")
    ffn0 = spread(run_ffn_total(ffn0), "ctx")
    blocks, ffn0 = tie(blocks, ffn0)
    keep, send = run_owner_sum(s1, blocks, later)
    unit = jnp.stack([keep, swap(send, "section", 1)])
    unit, ffn0, ffn1 = tie(unit, ffn0, ffn1)
    keep, send = run_ffn_pick(s1, ffn0, ffn1)
    gate, up, down = run_ffn_out(s1, c1, keep, swap(send, "section", 1))
    def own_layer(p0, p1):
        keep, send = by_layer(p0, p1)
        got = swap(send, "section", 1)
        return jnp.stack(by_layer(keep, got))

    units, gate, up, down = tie(spread(unit, "ctx"), gate, up, down)
    wo, gains, wk, wv, wq = run_attention_out(order_out, units)
    return (
        own_layer(out0, out1)[None, :, None],
        own_layer(in0, in1)[None, :, None],
        wq[None],
        wk.T[None],
        wv.T[None],
        wo[None],
        gains[None, :, 0],
        gate[None],
        up[None],
        down[None],
        gains[None, :, 1],
    )


def body(*args):
    sizes = [lax.axis_size(name) for name in ("section", "ctx", "dp")]
    return (body_fast if sizes == [2, 4, 4] else body_plain)(*args)


def solution(mesh):
    return jax.shard_map(
        body,
        mesh=mesh,
        in_specs=(
            P(None, "dp", "ctx", None),
            P(None, "dp", "ctx", None),
            P("section", "dp", None),
            P("section", "dp", None),
            P("section", "dp", None),
            P("section", "dp", None),
            P("section", "dp"),
            P("section", None, "dp"),
            P("section", None, "dp"),
            P("section", "dp", None),
            P("section", "dp"),
        ),
        out_specs=(
            P("section", None, "dp", "ctx", None),
            P("section", None, "dp", "ctx", None),
            P("section", "dp", None),
            P("section", "dp", None),
            P("section", "dp", None),
            P("section", "dp", None),
            P("section", "dp"),
            P("section", None, "dp"),
            P("section", None, "dp"),
            P("section", "dp", None),
            P("section", "dp"),
        ),
        check_vma=False,
    )
```

```python
import functools
import math

import jax
import jax.numpy as jnp
from jax import lax
from jax.experimental import pallas as pl
from jax.experimental.pallas import tpu as pltpu
from jax.sharding import PartitionSpec as P

D = 960
HEADS = 15
KV_HEADS = 5
HEAD_DIM = 64
QW = 960
KVW = 320
GROUP = 3
EPSILON = 1e-05
ROPE_BASE = 10000.0
MASKED = -1e30
BF = jnp.bfloat16
F32 = jnp.float32


def dot(a, b):
    return jnp.dot(a, b, preferred_element_type=F32)


def rope_tables(positions):
    half_dim = HEAD_DIM // 2
    freq_rows = ROPE_BASE ** (-(jnp.arange(half_dim, dtype=F32) * 2.0 / HEAD_DIM))
    angles = positions.astype(F32)[:, None] * freq_rows[None, :]
    cosine = jnp.concatenate([jnp.cos(angles), jnp.cos(angles)], axis=1)
    sine_rows = jnp.concatenate([jnp.sin(angles), jnp.sin(angles)], axis=1)
    return (cosine, sine_rows)


def turn_half(u):
    half_dim = HEAD_DIM // 2
    return jnp.concatenate([-u[..., half_dim:], u[..., :half_dim]], axis=-1)


def rotate(u, cosine, sine_rows):
    return u * cosine[:, None, :] + turn_half(u) * sine_rows[:, None, :]


def unrotate(u, cosine, sine_rows):
    return u * cosine[:, None, :] - turn_half(u * sine_rows[:, None, :])


def normalize(x, gain):
    inverse = lax.rsqrt(jnp.mean(x * x, axis=-1, keepdims=True) + EPSILON)
    return (x * inverse * gain, inverse)


def normalize_back(x, inverse, gain, grad):
    scaled = grad * gain
    gain_grad = jnp.sum(grad * x * inverse, axis=0)
    value_grad = inverse * scaled - x * inverse**3 * jnp.mean(scaled * x, axis=-1, keepdims=True)
    return (value_grad, gain_grad)


def attend(q, k, v, query_pos):
    tok = q.shape[0]
    q = q.reshape(tok, KV_HEADS, GROUP, HEAD_DIM)
    scores = jnp.einsum("tkgd,skd->kgts", q, k, preferred_element_type=F32) * HEAD_DIM**-0.5
    allowed = query_pos[:, None] >= jnp.arange(k.shape[0], dtype=jnp.int32)[None, :]
    scores = jnp.where(allowed, scores, MASKED)
    peak = jnp.max(scores, axis=-1, keepdims=True)
    e = jnp.exp(scores - peak)
    total = jnp.sum(e, axis=-1, keepdims=True)
    probs = (e / total).astype(BF)
    o = jnp.einsum("kgts,skd->tkgd", probs, v, preferred_element_type=F32).reshape(tok, QW)
    return o.astype(BF), (peak + jnp.log(total))[..., 0]


def attend_back(q, k, v, lse, do, o, query_pos):
    tok = q.shape[0]
    q = q.reshape(tok, KV_HEADS, GROUP, HEAD_DIM)
    dor = do.reshape(tok, KV_HEADS, GROUP, HEAD_DIM)
    delta = jnp.sum((do.astype(F32) * o.astype(F32)).reshape(tok, KV_HEADS, GROUP, HEAD_DIM), axis=-1)
    delta = jnp.transpose(delta, (1, 2, 0))
    scale = HEAD_DIM**-0.5
    scores = jnp.einsum("tkgd,skd->kgts", q, k, preferred_element_type=F32) * scale
    allowed = query_pos[:, None] >= jnp.arange(k.shape[0], dtype=jnp.int32)[None, :]
    probs = jnp.where(allowed, jnp.exp(scores - lse[..., None]), 0.0)
    dv = jnp.einsum("kgts,tkgd->skd", probs.astype(BF), dor, preferred_element_type=F32)
    dp = jnp.einsum("tkgd,skd->kgts", dor, v, preferred_element_type=F32)
    ds = (probs * (dp - delta[..., None])).astype(BF)
    dq = jnp.einsum("kgts,skd->tkgd", ds, k, preferred_element_type=F32) * scale
    dk = jnp.einsum("kgts,tkgd->skd", ds, q, preferred_element_type=F32) * scale
    dkv = jnp.concatenate([dk.reshape(-1, KVW), dv.reshape(-1, KVW)], axis=1)
    return dq.reshape(tok, HEADS, HEAD_DIM), dkv


def layer_forward(x, w, cosine, sine, query_pos):
    wa, wg, wu, wd, ga, gf = w
    tok = x.shape[0]
    n1, r1 = normalize(x, ga)
    n1 = n1.astype(BF)
    qkv = dot(n1, wa[:, : QW + 2 * KVW])
    q = rotate(qkv[:, :QW].reshape(tok, HEADS, HEAD_DIM), cosine, sine).astype(BF)
    k = rotate(qkv[:, QW : QW + KVW].reshape(tok, KV_HEADS, HEAD_DIM), cosine, sine)
    kv = jnp.concatenate([k.reshape(tok, KVW), qkv[:, QW + KVW :]], axis=1).astype(BF)
    kv = lax.all_gather(kv, "ctx", axis=0, tiled=True)
    k = kv[:, :KVW].reshape(-1, KV_HEADS, HEAD_DIM)
    v = kv[:, KVW:].reshape(-1, KV_HEADS, HEAD_DIM)
    o, lse = attend(q, k, v, query_pos)
    h1 = x + dot(o, wa[:, QW + 2 * KVW :])
    n2, r2 = normalize(h1, gf)
    n2 = lax.all_gather(n2.astype(BF), "dp", axis=0, tiled=True)
    gate = dot(n2, wg)
    up = dot(n2, wu)
    hidden = (jax.nn.silu(gate) * up).astype(BF)
    part = dot(hidden, wd).astype(BF)
    out = h1 + lax.psum_scatter(part, "dp", scatter_dimension=0, tiled=True).astype(F32)
    return out, (x, n1, r1, q, k, v, o, lse, h1, n2, r2, gate, up, hidden)


def layer_backward(g, kept, w, cosine, sine, query_pos):
    wa, wg, wu, wd, ga, gf = w
    x, n1, r1, q, k, v, o, lse, h1, n2, r2, gate, up, hidden = kept
    tok = x.shape[0]
    gb = lax.all_gather(g.astype(BF), "dp", axis=0, tiled=True)
    grad_down = dot(hidden.T, gb)
    dh = dot(gb, wd.T)
    sigma = jax.nn.sigmoid(gate)
    dgate = (dh * up * sigma * (1.0 + gate * (1.0 - sigma))).astype(BF)
    dup = (dh * gate * sigma).astype(BF)
    grad_gate = dot(n2.T, dgate)
    grad_up = dot(n2.T, dup)
    part = (dot(dgate, wg.T) + dot(dup, wu.T)).astype(BF)
    dn2 = lax.psum_scatter(part, "dp", scatter_dimension=0, tiled=True).astype(F32)
    back_f, gain_f = normalize_back(h1, r2, gf, dn2)
    dh1 = g + back_f
    db = dh1.astype(BF)
    grad_out = dot(o.T, db)
    do = dot(db, wa[:, QW + 2 * KVW :].T).astype(BF)
    dq, dkv = attend_back(q, k, v, lse, do, o, query_pos)
    dkv = lax.psum_scatter(dkv.astype(BF), "ctx", scatter_dimension=0, tiled=True).astype(F32)
    dq = unrotate(dq, cosine, sine).reshape(tok, QW)
    dk = unrotate(dkv[:, :KVW].reshape(tok, KV_HEADS, HEAD_DIM), cosine, sine).reshape(tok, KVW)
    dqkv = jnp.concatenate([dq, dk, dkv[:, KVW:]], axis=1).astype(BF)
    grad_qkv = dot(n1.T, dqkv)
    dn1 = dot(dqkv, wa[:, : QW + 2 * KVW].T)
    back_a, gain_a = normalize_back(x, r1, ga, dn1)
    grads = (
        jnp.concatenate([grad_qkv, grad_out], axis=1).astype(BF),
        jnp.stack([gain_a, gain_f]),
        grad_gate.astype(BF),
        grad_up.astype(BF),
        grad_down.astype(BF),
    )
    return dh1 + back_a, grads


def swap_section(p0, p1, section_id):
    mine = jnp.where(section_id == 0, p0, p1)
    other = jnp.where(section_id == 0, p1, p0)
    count = lax.axis_size("section")
    got = lax.ppermute(other, "section", [(i, count - 1 - i) for i in range(count)])
    return mine.astype(F32) + got.astype(F32)


def own_layer(p0, p1, section_id):
    mine = jnp.where(section_id == 0, p0, p1)
    other = jnp.where(section_id == 0, p1, p0)
    count = lax.axis_size("section")
    got = lax.ppermute(other, "section", [(i, count - 1 - i) for i in range(count)])
    first = jnp.where(section_id == 0, mine, got)
    second = jnp.where(section_id == 0, got, mine)
    return jnp.stack([first, second])


def body_plain(
    block_input, out_grad, w_query, w_key, w_value, w_out, norm_attn, w_gate, w_up, w_down, norm_ffn
):
    section_id = lax.axis_index("section")
    tok_rows = block_input.shape[2]
    query_pos = lax.axis_index("ctx") * tok_rows + jnp.arange(tok_rows, dtype=jnp.int32)
    cosine, sine = rope_tables(query_pos)
    x = lax.dynamic_index_in_dim(block_input[:, 0], section_id, 0, keepdims=False)
    g = lax.dynamic_index_in_dim(out_grad[:, 0], section_id, 0, keepdims=False)
    wa = jnp.concatenate([w_query[0], w_key[0], w_value[0], w_out[0]], axis=1)
    wa = lax.all_gather(lax.all_gather(wa, "dp", axis=0, tiled=True), "section")
    gains = jnp.stack([norm_attn[0], norm_ffn[0]])
    gains = lax.all_gather(lax.all_gather(gains, "dp", axis=1, tiled=True), "section").astype(F32)
    wg = lax.all_gather(w_gate[0], "section")
    wu = lax.all_gather(w_up[0], "section")
    wd = lax.all_gather(w_down[0], "section")
    layers = [(wa[l], wg[l], wu[l], wd[l], gains[l, 0], gains[l, 1]) for l in range(2)]
    out0, kept0 = layer_forward(x, layers[0], cosine, sine, query_pos)
    out1, kept1 = layer_forward(out0, layers[1], cosine, sine, query_pos)
    in1, grads1 = layer_backward(g, kept1, layers[1], cosine, sine, query_pos)
    in0, grads0 = layer_backward(in1, kept0, layers[0], cosine, sine, query_pos)
    section_outs = own_layer(out0, out1, section_id)
    in_grads = own_layer(in0, in1, section_id)
    ga, gn, gg, gu, gd = (
        swap_section(a, b, section_id) for a, b in zip(grads0, grads1)
    )
    ga = lax.psum_scatter(ga.astype(BF), "dp", scatter_dimension=0, tiled=True)
    ga = lax.psum(ga, "ctx").astype(F32)
    gn = lax.psum_scatter(gn, "dp", scatter_dimension=1, tiled=True)
    gn = lax.psum(gn, "ctx")
    gg = lax.psum(gg.astype(BF), "ctx").astype(F32)
    gu = lax.psum(gu.astype(BF), "ctx").astype(F32)
    gd = lax.psum(gd.astype(BF), "ctx").astype(F32)
    return (
        section_outs[None, :, None],
        in_grads[None, :, None],
        ga[None, :, :QW],
        ga[None, :, QW : QW + KVW],
        ga[None, :, QW + KVW : QW + 2 * KVW],
        ga[None, :, QW + 2 * KVW :],
        gn[None, 0],
        gg[None],
        gu[None],
        gd[None],
        gn[None, 1],
    )


def t_dot(a, b):
    return lax.dot_general(a, b, (((0,), (0,)), ((), ())), preferred_element_type=F32)


def dot_t(a, b):
    return lax.dot_general(a, b, (((1,), (1,)), ((), ())), preferred_element_type=F32)


def shape_of(*dims, kind=BF):
    return jax.ShapeDtypeStruct(dims, kind)


def call(kernel, out_shape, *args, flops=0, grid=None, in_specs=None, out_specs=None, scratch=()):
    moved = sum(math.prod(a.shape) * a.dtype.itemsize for a in list(args) + list(out_shape))
    kwargs = {} if grid is None else {"grid": grid}
    held = moved + sum(math.prod(m.shape) * 4 for m in scratch)
    vmem = pl.BlockSpec(memory_space=pltpu.VMEM)
    smem = pl.BlockSpec(memory_space=pltpu.SMEM)
    return pl.pallas_call(
        kernel,
        out_shape=out_shape,
        in_specs=in_specs or [smem if a.dtype == jnp.int32 else vmem for a in args],
        out_specs=out_specs or [vmem] * len(out_shape),
        scratch_shapes=scratch,
        cost_estimate=pl.CostEstimate(flops=flops, bytes_accessed=moved, transcendentals=0),
        compiler_params=pltpu.CompilerParams(vmem_limit_bytes=min(60 << 20, held * 9 // 8 + (8 << 20))),
        **kwargs,
    )(*args)


def turn(u, cosine, sine, sign, first, last):
    rows, width = u.shape
    padded = -(-width // 128) * 128
    if padded > width:
        u = jnp.concatenate([u, jnp.zeros((rows, padded - width), F32)], axis=1)
    lane = lax.broadcasted_iota(jnp.int32, (rows, padded), 1)
    partner = jnp.where(
        lane % HEAD_DIM < HEAD_DIM // 2,
        pltpu.roll(u, padded - HEAD_DIM // 2, 1),
        pltpu.roll(u, HEAD_DIM // 2, 1),
    )
    cosine = jnp.concatenate([cosine[:rows]] * (padded // HEAD_DIM), axis=1)
    sine = jnp.concatenate([sine[:rows]] * (padded // HEAD_DIM), axis=1)
    turned = u * cosine + (partner * sine if sign > 0 else -(partner * sine))
    return jnp.where((lane >= first) & (lane < last), turned, u)[:, :width]


def inverse_norm(x):
    return lax.rsqrt(jnp.mean(x * x, axis=-1, keepdims=True) + EPSILON)


def project_kernel(count, *refs):
    parts, (order, w0, w1, cosine, sine, x_ref, n_ref, q_ref, kv_ref, gain_ref) = refs[:count], refs[count:]
    columns = jnp.concatenate([w0[:, GAINS - QKV :], w1[:, GAINS - QKV :]], axis=0)
    gains = lax.dot_general(columns, order[...], (((0,), (1,)), ((), ())), preferred_element_type=F32)
    gain_ref[...] = gains[:8]
    x = parts[0][...]
    for part in parts[1:]:
        x = x + part[...].astype(F32)
    x_ref[...] = x
    n = (x * inverse_norm(x) * gains[:1]).astype(BF)
    n = dot(n, order[...]).astype(BF)
    n_ref[...] = n
    half = w0.shape[0]
    out = dot(n[:, :half], w0[:, : GAINS - QKV]) + dot(n[:, half:], w1[:, : GAINS - QKV])
    kv = turn(out[:, : 2 * KVW], cosine[...], sine[...], 1, 0, KVW)
    kv_ref[...] = kv.astype(BF)
    q_ref[...] = turn(out[:, 2 * KVW :], cosine[...], sine[...], 1, 0, QW).astype(BF)


def run_project(parts, order, wa, tables):
    tok = parts[0].shape[0]
    args = list(parts) + [order, *wa, *tables]
    return call(
        functools.partial(project_kernel, len(parts)),
        [
            shape_of(tok, D, kind=F32),
            shape_of(tok, order.shape[1]),
            shape_of(tok, QW),
            shape_of(tok, 2 * KVW),
            shape_of(8, D, kind=F32),
        ],
        *args,
        flops=2 * tok * order.shape[1] * (D + QW + 2 * KVW),
    )


def project_all_kernel(*refs):
    x_ref, others = refs[0], refs[1:4]
    order, w0, w1, cosine, sine, n_ref, q_ref, kv0, kv1, kv2, kv3, gain_ref = refs[4:]
    columns = jnp.concatenate([w0[:, GAINS - QKV :], w1[:, GAINS - QKV :]], axis=0)
    gains = lax.dot_general(columns, order[...], (((0,), (1,)), ((), ())), preferred_element_type=F32)
    gain_ref[...] = gains[:8]
    x = x_ref[...]
    tok = x.shape[0]
    rows = [x * inverse_norm(x)] + [r[...].astype(F32) for r in others]
    n = (jnp.concatenate(rows, axis=0) * gains[:1]).astype(BF)
    n = dot(n, order[...]).astype(BF)
    n_ref[...] = n[:tok]
    half = w0.shape[0]
    kv = dot(n[:, :half], w0[:, : 2 * KVW]) + dot(n[:, half:], w1[:, : 2 * KVW])
    kv = turn(kv, cosine[...], sine[...], 1, 0, KVW).astype(BF)
    for k, out in enumerate((kv0, kv1, kv2, kv3)):
        out[...] = kv[k * tok : (k + 1) * tok]
    q = dot(n[:tok, :half], w0[:, 2 * KVW : GAINS - QKV]) + dot(n[:tok, half:], w1[:, 2 * KVW : GAINS - QKV])
    q_ref[...] = turn(q, cosine[...], sine[...], 1, 0, QW).astype(BF)


def run_project_all(x, others, order, wa, tables):
    tok = x.shape[0]
    n1, q, *kv, gains = call(
        project_all_kernel,
        [shape_of(tok, order.shape[1]), shape_of(tok, QW)]
        + [shape_of(tok, 2 * KVW)] * 4
        + [shape_of(8, D, kind=F32)],
        x, *others, order, *wa, *tables,
        flops=2 * tok * order.shape[1] * (4 * D + QW + 8 * KVW),
    )
    return x, n1, q, kv, gains


def causal(c, tok, count):
    shape = (GROUP * tok, count * tok)
    row = c * tok + lax.broadcasted_iota(jnp.int32, shape, 0) % tok
    lane = lax.broadcasted_iota(jnp.int32, shape, 1)
    key = jnp.zeros(shape, jnp.int32)
    for k in range(count):
        key = jnp.where(lane // tok == k, (c ^ k) * tok + lane % tok, key)
    return row >= key


def heads_of(x, j):
    return jnp.concatenate(
        [x[:, (GROUP * j + g) * HEAD_DIM : (GROUP * j + g + 1) * HEAD_DIM] for g in range(GROUP)], axis=0
    )


def attend_kernel(c_ref, x_ref, q_ref, kv0, kv1, kv2, kv3, gain, order, w0, w1, o_ref, op_ref, lse_ref, h_ref, n_ref):
    tok = q_ref.shape[0]
    kv = jnp.concatenate([kv0[...], kv1[...], kv2[...], kv3[...]], axis=0)
    q = q_ref[...]
    allowed = causal(c_ref[0], tok, 4)
    for j in range(KV_HEADS):
        k = kv[:, j * HEAD_DIM : (j + 1) * HEAD_DIM]
        v = kv[:, KVW + j * HEAD_DIM : KVW + (j + 1) * HEAD_DIM]
        scores = jnp.where(allowed, dot_t(heads_of(q, j), k) * HEAD_DIM**-0.5, MASKED)
        peak = jnp.max(scores, axis=-1, keepdims=True)
        e = jnp.exp(scores - peak)
        total = jnp.sum(e, axis=-1, keepdims=True)
        o = dot((e * (1.0 / total)).astype(BF), v).astype(BF)
        lse = peak + jnp.log(total)
        for g in range(GROUP):
            h = GROUP * j + g
            o_ref[:, h * HEAD_DIM : (h + 1) * HEAD_DIM] = o[g * tok : (g + 1) * tok]
            lse_ref[:, h : h + 1] = lse[g * tok : (g + 1) * tok]
    op = dot(o_ref[...], order[...]).astype(BF)
    op_ref[...] = op
    half = w0.shape[0]
    h1 = x_ref[...] + dot(op[:, :half], w0[:, :QW]) + dot(op[:, half:], w1[:, :QW])
    h_ref[...] = h1
    n_ref[...] = (h1 * inverse_norm(h1) * gain[1:2]).astype(BF)


def run_attend(c, x, q, kv, gain, order, wa):
    tok = q.shape[0]
    return call(
        attend_kernel,
        [
            shape_of(tok, QW),
            shape_of(tok, order.shape[1]),
            shape_of(tok, 16, kind=F32),
            shape_of(tok, D, kind=F32),
            shape_of(tok, D),
        ],
        c, x, q, *kv, gain, order, *wa,
        flops=2 * tok * (4 * tok * QW * 2 + order.shape[1] * D * 2),
    )


def token_rows(d_ref, *refs):
    if len(refs) == 1:
        d = d_ref[0]
        return jnp.concatenate([refs[0][d ^ k] for k in range(4)], axis=0)
    return jnp.concatenate([r[...] for r in refs], axis=0)


def ffn_kernel(d_ref, h_ref, n_ref, wg, wu, wd, gate_ref, up_ref, hidden_ref, p0, p1, p2, p3):
    n = token_rows(d_ref, n_ref)
    gate, up = dot(n, wg[...]), dot(n, wu[...])
    gate_ref[...], up_ref[...] = gate, up
    hidden = (gate * (1.0 / (1.0 + jnp.exp(-gate))) * up).astype(BF)
    hidden_ref[...] = hidden
    part = dot(hidden, wd[...])
    tok = h_ref.shape[0]
    p0[...] = h_ref[...] + part[:tok]
    for k, p in enumerate((p1, p2, p3), 1):
        p[...] = part[k * tok : (k + 1) * tok].astype(BF)


def run_ffn(d, h1, n2, wg, wu, wd):
    tok, width = h1.shape[0], wg.shape[1]
    return call(
        ffn_kernel,
        [shape_of(4 * tok, width, kind=F32)] * 2
        + [shape_of(4 * tok, width), shape_of(tok, D, kind=F32)]
        + [shape_of(tok, D)] * 3,
        d, h1, n2, wg, wu, wd,
        flops=6 * 4 * tok * width * D,
    )


def ffn_back_kernel(d_ref, *refs):
    gate_ref, up_ref, wg, wu, wd, dgate_ref, dup_ref, p0, p1, p2, p3 = refs[-11:]
    gb = token_rows(d_ref, *refs[:-11])
    dh = dot_t(gb, wd[...])
    gate, up = gate_ref[...], up_ref[...]
    sigma = 1.0 / (1.0 + jnp.exp(-gate))
    dgate = (dh * up * sigma * (1.0 + gate * (1.0 - sigma))).astype(BF)
    dup = (dh * gate * sigma).astype(BF)
    dgate_ref[...], dup_ref[...] = dgate, dup
    part = dot_t(dgate, wg[...]) + dot_t(dup, wu[...])
    tok = p0.shape[0]
    p0[...] = part[:tok]
    for k, p in enumerate((p1, p2, p3), 1):
        p[...] = part[k * tok : (k + 1) * tok].astype(BF)


def run_ffn_back(d, gb, gate, up, wg, wu, wd):
    tok, width = gate.shape[0] // 4, wg.shape[1]
    return call(
        ffn_back_kernel,
        [shape_of(4 * tok, width)] * 2 + [shape_of(tok, D, kind=F32)] + [shape_of(tok, D)] * 3,
        d, *gb, gate, up, wg, wu, wd,
        flops=6 * 4 * tok * width * D,
    )


def ffn_grads_kernel(s_ref, d_ref, dgate, dup, hidden, n_ref, *refs):
    n, gb = token_rows(d_ref, n_ref), token_rows(d_ref, *refs[:-5])
    gu_keep, gu_send, down_keep, down_send, down = refs[-5:]
    s = s_ref[0]
    a, b = dgate[...], dup[...]
    first = s == 0
    gu_keep[...] = t_dot(n, jnp.where(first, a, b)).astype(BF)
    gu_send[...] = t_dot(n, jnp.where(first, b, a)).astype(BF)
    down[...] = t_dot(hidden[...], gb)
    half = down.shape[0] // 2
    down_keep[...] = down[pl.ds(pl.multiple_of(s * half, half), half), :].astype(BF)
    down_send[...] = down[pl.ds(pl.multiple_of((1 - s) * half, half), half), :].astype(BF)


def run_ffn_grads(s, d, dgate, dup, hidden, n2, gb):
    tok, width = dgate.shape
    return call(
        ffn_grads_kernel,
        [shape_of(D, width)] * 2 + [shape_of(width // 2, D)] * 2,
        s, d, dgate, dup, hidden, n2, *gb,
        flops=6 * tok * width * D,
        scratch=[pltpu.VMEM((width, D), F32)],
    )


def attend_back_kernel(c_ref, *refs):
    parts, kv_refs = refs[:4], refs[4:8]
    h_ref, g_ref, q_ref, o_ref, lse_ref, gain, order, w0, w1, cosine, sine = refs[8:19]
    dh_ref, db_ref, gain_ref, dq_ref, d0, d1, d2, d3, dq_acc, dkv_acc = refs[19:]
    tok = q_ref.shape[0]
    dn = parts[0][...]
    for part in parts[1:]:
        dn = dn + part[...].astype(F32)
    h1 = h_ref[...]
    inverse = inverse_norm(h1)
    gain_ref[...] = jnp.sum(dn * h1 * inverse, axis=0, keepdims=True)
    scaled = dn * gain[1:2]
    dh = g_ref[...] + inverse * scaled - h1 * inverse**3 * jnp.mean(scaled * h1, axis=-1, keepdims=True)
    dh_ref[...] = dh
    db = dh.astype(BF)
    db_ref[...] = db
    dop = jnp.concatenate([dot_t(db, w0[:, :QW]), dot_t(db, w1[:, :QW])], axis=1).astype(BF)
    do = dot_t(dop, order[...]).astype(BF)
    kv = jnp.concatenate([r[...] for r in kv_refs], axis=0)
    q, o, lse_all = q_ref[...], o_ref[...], lse_ref[...]
    allowed = causal(c_ref[0], tok, 4)
    scale = HEAD_DIM**-0.5
    for j in range(KV_HEADS):
        k = kv[:, j * HEAD_DIM : (j + 1) * HEAD_DIM]
        v = kv[:, KVW + j * HEAD_DIM : KVW + (j + 1) * HEAD_DIM]
        qj, doj = heads_of(q, j), heads_of(do, j)
        delta = jnp.sum(doj.astype(F32) * heads_of(o, j).astype(F32), axis=-1, keepdims=True)
        lse = jnp.concatenate([lse_all[:, GROUP * j + g : GROUP * j + g + 1] for g in range(GROUP)], axis=0)
        probs = jnp.where(allowed, jnp.exp(dot_t(qj, k) * scale - lse), 0.0)
        dkv_acc[:, KVW + j * HEAD_DIM : KVW + (j + 1) * HEAD_DIM] = t_dot(probs.astype(BF), doj)
        ds = (probs * (dot_t(doj, v) - delta)).astype(BF)
        dkv_acc[:, j * HEAD_DIM : (j + 1) * HEAD_DIM] = t_dot(ds, qj) * scale
        dq = dot(ds, k) * scale
        for g in range(GROUP):
            h = GROUP * j + g
            dq_acc[:, h * HEAD_DIM : (h + 1) * HEAD_DIM] = dq[g * tok : (g + 1) * tok]
    dq_ref[...] = turn(dq_acc[...], cosine[...], sine[...], -1, 0, QW).astype(BF)
    d0[...] = dkv_acc[:tok]
    for k, d in enumerate((d1, d2, d3), 1):
        d[...] = dkv_acc[k * tok : (k + 1) * tok].astype(BF)


def run_attend_back(c, parts, kv, h1, g, q, o, lse, gain, order, wa, tables):
    tok = q.shape[0]
    return call(
        attend_back_kernel,
        [
            shape_of(tok, D, kind=F32),
            shape_of(tok, D),
            shape_of(1, D, kind=F32),
            shape_of(tok, QW),
            shape_of(tok, 2 * KVW, kind=F32),
        ]
        + [shape_of(tok, 2 * KVW)] * 3,
        c, *parts, *kv, h1, g, q, o, lse, gain, order, *wa, *tables,
        flops=2 * tok * (4 * tok * QW * 5 + order.shape[1] * D * 2),
        scratch=[pltpu.VMEM((tok, QW), F32), pltpu.VMEM((4 * tok, 2 * KVW), F32)],
    )


def project_back_kernel(*refs):
    parts, refs = refs[:4], refs[4:]
    dq_ref, x_ref, dh_ref, gain_f, gain, order, w0, w1, cosine, sine = refs[:10]
    in_ref, gb_ref, dqkv_ref, gains_ref = refs[10:]
    dkv = parts[0][...]
    for part in parts[1:]:
        dkv = dkv + part[...].astype(F32)
    dkv = turn(dkv, cosine[...], sine[...], -1, 0, KVW).astype(BF)
    dqkv_ref[:, : 2 * KVW] = dkv
    dqkv_ref[:, 2 * KVW :] = dq_ref[...]
    dqkv = dqkv_ref[...]
    ds = jnp.concatenate([dot_t(dqkv, w0[:, : GAINS - QKV]), dot_t(dqkv, w1[:, : GAINS - QKV])], axis=1)
    high = ds.astype(BF)
    low = (ds - high.astype(F32)).astype(BF)
    dn = dot_t(high, order[...]) + dot_t(low, order[...])
    x = x_ref[...]
    inverse = inverse_norm(x)
    gain_a = jnp.sum(dn * x * inverse, axis=0, keepdims=True)
    scaled = dn * gain[:1]
    out = dh_ref[...] + inverse * scaled - x * inverse**3 * jnp.mean(scaled * x, axis=-1, keepdims=True)
    in_ref[...] = out
    gb_ref[...] = out.astype(BF)
    row = lax.broadcasted_iota(jnp.int32, (16, D), 0)
    both = jnp.where(row == 0, gain_a, jnp.where(row == 1, gain_f[...], 0.0)).astype(BF)
    gains_ref[...] = dot(both, order[...]).astype(BF)


def run_project_back(parts, dq, x, dh1, gain_f, gain, order, wa, tables):
    tok = dq.shape[0]
    return call(
        project_back_kernel,
        [shape_of(tok, D, kind=F32), shape_of(tok, D), shape_of(tok, QW + 2 * KVW), shape_of(16, order.shape[1])],
        *parts, dq, x, dh1, gain_f, gain, order, *wa, *tables,
        flops=2 * tok * order.shape[1] * (2 * D + QW + 2 * KVW),
    )


def attention_grads_kernel(op0, op1, n0, n1, g0, g1, db_ref, dqkv_ref, keep_ref, send_ref):
    db, dqkv = db_ref[...], dqkv_ref[...]
    row = lax.broadcasted_iota(jnp.int32, (16, WIDTH - GAINS), 0)
    ones = (row == lax.broadcasted_iota(jnp.int32, (16, WIDTH - GAINS), 1)).astype(F32).astype(BF)
    for op, n, g, out in ((op0, n0, g0, keep_ref), (op1, n1, g1, send_ref)):
        out[:, WO:QW] = t_dot(op[...], db).astype(BF)
        out[:, QW:QKV] = jnp.zeros((out.shape[0], QKV - QW), BF)
        out[:, QKV:GAINS] = t_dot(n[...], dqkv).astype(BF)
        out[:, GAINS:] = t_dot(g[...], ones).astype(BF)


def run_attention_grads(op, db, n1, dqkv, gains):
    tok, rows = op.shape
    block = rows // 4

    def halves(height):
        return [pl.BlockSpec((height, block), lambda i: (0, i)), pl.BlockSpec((height, block), lambda i: (0, i + 2))]

    return call(
        attention_grads_kernel,
        [shape_of(rows // 2, WIDTH)] * 2,
        op, op, n1, n1, gains, gains, db, dqkv,
        flops=2 * tok * rows * WIDTH,
        grid=(2,),
        in_specs=halves(tok) + halves(tok) + halves(16)
        + [pl.BlockSpec((tok, QW), lambda i: (0, 0)), pl.BlockSpec((tok, QW + 2 * KVW), lambda i: (0, 0))],
        out_specs=[pl.BlockSpec((block, WIDTH), lambda i: (i, 0))] * 2,
    )


def add_kernel(a, b, out):
    out[...] = (a[...].astype(F32) + b[...].astype(F32)).astype(BF)


def run_add(a, b):
    return call(add_kernel, [shape_of(*a.shape)], a, b)[0]


def split_sum_kernel(axis, *refs):
    pairs = len(refs) // 4
    for i in range(pairs):
        a, b = refs[2 * i : 2 * i + 2]
        keep, send = refs[2 * pairs + 2 * i : 2 * pairs + 2 * i + 2]
        total = (a[...].astype(F32) + b[...].astype(F32)).astype(BF)
        keep[...], send[...] = total[0], total[1]


def pack(gu, down, out):
    rows, width = gu.shape
    unit = down.shape[0]
    out[:rows, :] = gu
    out[rows : rows + unit, :] = down[:, :width]
    out[rows + unit :, : width // 2] = down[: unit // 2, width:]
    out[rows + unit :, width // 2 :] = down[unit // 2 :, width:]


def unpack(packed, rows, unit):
    packed = packed.astype(F32)
    width = packed.shape[1]
    tail = packed[rows + unit :]
    tail = jnp.concatenate([tail[:, : width // 2], tail[:, width // 2 :]], axis=0)
    return packed[:rows], jnp.concatenate([packed[rows : rows + unit], tail], axis=1)


def ffn_split_kernel(c_ref, gu_a, gu_b, down_a, down_b, *outs):
    c = c_ref[0]
    for k, out in enumerate(outs):
        sums = []
        for a, b in ((gu_a, gu_b), (down_a, down_b)):
            rows = a.shape[0] // 4
            block = pl.ds(pl.multiple_of((c ^ k) * rows, rows), rows)
            sums.append((a[block, :].astype(F32) + b[block, :].astype(F32)).astype(BF))
        pack(*sums, out)


def run_ffn_split(c, gu_a, gu_b, down_a, down_b):
    width = gu_a.shape[1]
    rows = (gu_a.size + down_a.size) // (4 * width)
    return call(ffn_split_kernel, [shape_of(rows, width)] * 4, c, gu_a, gu_b, down_a, down_b)


def ffn_total_kernel(*refs):
    refs[4][...] = sum(r[...].astype(F32) for r in refs[:4]).astype(BF)


def run_ffn_total(blocks):
    return call(ffn_total_kernel, [shape_of(*blocks[0].shape)], *blocks)[0]


def ffn_pick_kernel(s_ref, *refs):
    first = s_ref[0] == 0
    rows = refs[0].shape[0]
    keep, send = refs[8:]
    for k in range(4):
        a, b = refs[k][...], refs[4 + k][...]
        keep[k * rows : (k + 1) * rows, :] = jnp.where(first, a, b)
        send[k * rows : (k + 1) * rows, :] = jnp.where(first, b, a)


def run_ffn_pick(s, layer0, layer1):
    rows, width = layer0[0].shape
    return call(ffn_pick_kernel, [shape_of(4 * rows, width)] * 2, s, *layer0, *layer1)


def ffn_out_kernel(s_ref, c_ref, keep, got, gate, up, whole):
    s, c = s_ref[0], c_ref[0]
    rows, unit = gate.shape[0] // 4, whole.shape[0] // 8
    size = keep.shape[0] // 4
    first = s == 0
    for k in range(4):
        (a, x), (b, y) = (unpack(r[k * size : (k + 1) * size, :], rows, unit) for r in (keep, got))
        block = pl.ds(pl.multiple_of((c ^ k) * rows, rows), rows)
        gate[block, :] = jnp.where(first, a, b)
        up[block, :] = jnp.where(first, b, a)
        for half, v in ((s, x), (1 - s, y)):
            whole[pl.ds(pl.multiple_of((half * 4 + (c ^ k)) * unit, unit), unit), :] = v


def run_ffn_out(s, c, keep, got):
    width = keep.shape[1]
    out = [shape_of(D, width, kind=F32)] * 2 + [shape_of(width, D, kind=F32)]
    return call(ffn_out_kernel, out, s, c, keep, got)


def first_split_kernel(keep_ref, got_ref, a_keep, a_send, b_keep, b_send):
    total = (keep_ref[...].astype(F32) + got_ref[...].astype(F32)).astype(BF)
    for i in range(2):
        a_keep[i], a_send[i] = total[2 * i, :2], total[2 * i + 1, :2]
        b_keep[i], b_send[i] = total[i, 2:], total[2 + i, 2:]


def run_first_split(keep, got):
    shape = (4, 4, keep.shape[0] // 16, keep.shape[1])
    return call(
        first_split_kernel,
        [shape_of(2, 2, *shape[2:])] * 4,
        keep.reshape(shape), got.reshape(shape),
    )


def run_split_sum(a, a1, b, b1):
    out = [shape_of(*a.shape[1:])] * 2 + [shape_of(*b.shape[1:])] * 2
    return call(functools.partial(split_sum_kernel, 0), out, a, a1, b, b1)


def dp_split_kernel(a, a1, b, b1, own, s1, s2, s3):
    x = a[...].astype(F32) + a1[...].astype(F32)
    y = b[...].astype(F32) + b1[...].astype(F32)
    own[...] = x[0]
    s1[...], s2[...], s3[...] = x[1].astype(BF), y[0].astype(BF), y[1].astype(BF)


def run_dp_split(a, a1, b, b1):
    shape = a.shape[1:]
    return call(dp_split_kernel, [shape_of(*shape, kind=F32)] + [shape_of(*shape)] * 3, a, a1, b, b1)


def owner_sum_kernel(s_ref, *refs):
    now, later = (sum(r[...].astype(F32) for r in refs[k : k + 4]).astype(BF) for k in (0, 4))
    keep, send = refs[8:]
    first = s_ref[0] == 0
    keep[...] = jnp.where(first, now, later)
    send[...] = jnp.where(first, later, now)


def run_owner_sum(s, now, later):
    return call(owner_sum_kernel, [shape_of(*now[0].shape)] * 2, s, *now, *later)


def attention_out_kernel(order, u0, u1, u2, u3, wo, gains, wk, wv, wq):
    rows = jnp.concatenate([u[h] for u in (u0, u1, u2, u3) for h in range(2)], axis=0)
    out = dot(order[...], rows)
    wo[...] = out[:, WO:QW]
    gains[...] = out[:, GAINS:]
    turned = lax.dot_general(
        rows[:, QKV : QKV + 2 * KVW], order[...], (((0,), (1,)), ((), ())), preferred_element_type=F32
    )
    wk[...], wv[...] = turned[:KVW], turned[KVW:]
    wq[...] = out[:, QKV + 2 * KVW : GAINS]


def run_attention_out(order, units):
    rows = order.shape[0]
    shapes = ((rows, QW), (rows, WIDTH - GAINS), (KVW, rows), (KVW, rows), (rows, QW))
    return call(
        attention_out_kernel,
        [shape_of(*shape, kind=F32) for shape in shapes],
        order, *units,
        flops=2 * rows * order.shape[1] * WIDTH,
    )


def swap(x, axis, bit):
    return lax.ppermute(x, axis, [(i, i ^ bit) for i in range(lax.axis_size(axis))])


def spread(x, axis):
    return [x] + [swap(x, axis, k) for k in range(1, 4)]


def deliver(blocks, axis):
    return [blocks[0]] + [swap(b, axis, k) for k, b in enumerate(blocks[1:], 1)]


def pick(x, index, axis=0):
    return lax.dynamic_index_in_dim(x, index, axis, keepdims=False)


def tie(*values):
    return lax.optimization_barrier(values)


def plane_gather(a, b):
    a1, b1 = swap(a, "ctx", 2), swap(b, "ctx", 1)
    a2, b2 = swap(jnp.stack([a, a1]), "ctx", 1), swap(jnp.stack([b, b1]), "ctx", 2)
    return jnp.stack([a, a2[0], a1, a2[1]]), jnp.stack([b, b1, b2[0], b2[1]])


WO, QKV = 0, QW + 64
GAINS = QKV + QW + 2 * KVW
WIDTH = GAINS + 64
PAD = 256


def row_orders(s, c, d):
    p = jnp.arange(4 * PAD, dtype=jnp.int32)
    row = (((p // 128) % 4) ^ c) * 64 + ((p // 512) ^ s) * 32 + p % 32
    feature = jnp.where(row < D // 4, (((p // 32) % 4) ^ d) * (D // 4) + row, -1)
    order = (jnp.arange(D, dtype=jnp.int32)[:, None] == feature[None, :]).astype(BF)
    p = jnp.arange(PAD, dtype=jnp.int32)
    out = ((p // 64) ^ c) * 64 + (((p // 32) % 2) ^ s) * 32 + p % 32
    return order, (jnp.arange(D // 4, dtype=jnp.int32)[:, None] == out[None, :]).astype(BF)


def body_fast(
    block_input, out_grad, w_query, w_key, w_value, w_out, norm_attn, w_gate, w_up, w_down, norm_ffn
):
    s, c, d = (lax.axis_index(n) for n in ("section", "ctx", "dp"))
    s1, c1, d1 = (i.astype(jnp.int32).reshape(1) for i in (s, c, d))
    tok = block_input.shape[2]
    cosine, sine = rope_tables(
        jnp.concatenate([(c ^ k) * tok + jnp.arange(tok, dtype=jnp.int32) for k in range(4)])
    )
    sign = jnp.where(jnp.arange(HEAD_DIM) < HEAD_DIM // 2, -1.0, 1.0)
    tables = cosine, sine * sign
    x = pick(block_input[:, 0], s)
    g = pick(out_grad[:, 0], s)

    def by_layer(own, got):
        return jnp.where(s == 0, own, got), jnp.where(s == 0, got, own)

    def own_rows(w):
        return pick(jnp.pad(w, ((0, PAD - w.shape[0]), (0, 0))).reshape(4, 2, 32, w.shape[1]), c)

    gains = own_rows(jnp.stack([norm_attn[0], norm_ffn[0]], axis=1))
    gains = jnp.pad(gains, ((0, 0), (0, 0), (0, WIDTH - GAINS - 2)))
    own = [own_rows(w[0]) for w in (w_out, w_key, w_value, w_query)]
    own = jnp.concatenate([own[0], jnp.zeros((2, 32, QKV - QW), BF), *own[1:], gains], axis=2)
    unit0, unit1 = by_layer(pick(own, s), swap(pick(own, 1 - s), "section", 1))
    ffn = [by_layer(w[0], swap(w[0], "section", 1)) for w in (w_gate, w_up, w_down)]
    unit0, s, c, d, w_gate, w_up, w_down, x = tie(unit0, s, c, d, w_gate, w_up, w_down, x)
    z = spread(unit0, "dp")
    others = (x * inverse_norm(x)).astype(BF)
    gb1 = g.astype(BF)
    z[2:], others, unit1, gb1 = tie(z[2:], spread(others, "ctx")[1:], unit1, gb1)
    order0, order_out = row_orders(s, c, d)

    def first_step(a, b):
        return a, swap(a, "ctx", 2), b, swap(b, "ctx", 1)

    def second_step(a, a1, b, b1):
        return a, a1, swap(jnp.stack([a, a1]), "ctx", 1), b, b1, swap(jnp.stack([b, b1]), "ctx", 2)

    def whole_half(a, a1, a2, b, b1, b2):
        a, b = jnp.stack([a, a2[0], a1, a2[1]]), jnp.stack([b, b1, b2[0], b2[1]])
        whole = jnp.concatenate([a, b], axis=1).reshape(512, WIDTH)
        return whole[:, :QKV], whole[:, QKV:]

    steps = second_step(*first_step(jnp.stack(z[:2]), jnp.stack(z[2:])))
    mine, gb1_2, gb1_1, z1, (ffn, order0, order_out, tables, x, g, gb1) = tie(
        whole_half(*steps), swap(gb1, "dp", 2), swap(gb1, "dp", 1), spread(unit1, "dp"), (ffn, order0, order_out, tables, x, g, gb1)
    )
    wa0 = [(w, swap(w, "section", 1)) for w in mine]

    def nothing(*values):
        return values

    def forward(parts, wa, order, w, beside, values, others=None):
        if others is None:
            x, n1, q, kv, gains = run_project(parts, order, wa[1], tables)
            kv, values = tie(spread(kv, "ctx"), beside[0](*values))
        else:
            x, n1, q, kv, gains = run_project_all(parts[0], others, order, wa[1], tables)
            values = beside[0](*values)
        o, op, lse, h1, n2 = run_attend(c1, x, q, kv, gains, order, wa[0])
        n2, values = tie(n2, values)
        n2, values = tie(lax.all_gather(n2, "dp"), beside[1](*values))
        gate, up, hidden, *parts = run_ffn(d1, h1, n2, *w)
        if beside[2] is not None:
            parts, values = tie(deliver(parts, "dp"), beside[2](*values))
        return parts, (x, n1, q, kv, o, op, lse, h1, n2, gate, up, hidden, gains), values

    def backward(g, gb, kept, wa, order, w, beside, values):
        x, n1, q, kv, o, op, lse, h1, n2, gate, up, hidden, gains = kept
        dgate, dup, *parts = run_ffn_back(d1, gb, gate, up, *w)
        parts = deliver(parts, "dp")
        values = beside[0](*values)
        gu_keep, gu_send, down_keep, down_send = run_ffn_grads(s1, d1, dgate, dup, hidden, n2, gb)
        sums = run_ffn_split(c1, gu_keep, swap(gu_send, "section", 1), down_keep, swap(down_send, "section", 1))
        parts, sums, values = tie(parts, sums, values)
        values = beside[1](*values)
        dh1, db, gain_f, dq, *dkv = run_attend_back(c1, parts, kv, h1, g, q, o, lse, gains, order, wa[0], tables)
        dkv, values = tie(dkv, values)
        sums = deliver(sums, "ctx")
        dkv, values, sums = tie(deliver(dkv, "ctx"), beside[2](*values), sums)
        g, gb, dqkv, gains = run_project_back(dkv, dq, x, dh1, gain_f, gains, order, wa[1], tables)
        return g, gb, (op, db, n1, dqkv, gains), sums, values

    w0, w1 = ([pair[l] for pair in ffn] for l in range(2))
    parts, kept0, wa1 = forward(
        [x], wa0, order0, w0,
        (
            lambda *z: first_step(jnp.stack(z[:2]), jnp.stack(z[2:])),
            second_step,
            lambda *steps: [(w, swap(w, "section", 1)) for w in whole_half(*steps)],
        ),
        z1, others,
    )
    out1, kept1, (gb1_3,) = forward(
        parts, wa1, order0, w1, (lambda v: (swap(v, "dp", 3),), nothing, None), (gb1,)
    )
    out0 = kept1[0]
    gb = [gb1, gb1_1, gb1_2, gb1_3]
    in1, gb, operands, ffn1, out1 = backward(
        g, gb, kept1, wa1, order0, w1,
        (
            nothing,
            nothing,
            lambda own, p1, p2, p3: (own, swap(p1, "dp", 1), p2, swap(p3, "dp", 3)),
        ),
        out1,
    )
    ffn1 = spread(run_ffn_total(ffn1), "ctx")
    gb, operands, ffn1 = tie(lax.all_gather(gb, "dp"), operands, ffn1)
    keep, send = run_attention_grads(*operands)
    gb, keep, send = tie(gb, keep, send)

    def scatter_first(a, a1, b, b1):
        return a, swap(a1, "ctx", 1), b, swap(b1, "ctx", 2)

    def scatter_second(a, a1, b, b1):
        return a, swap(a1, "ctx", 2), b, swap(b1, "ctx", 1)

    in0, _, operands, ffn0, later = backward(
        in1, [gb], kept0, wa0, order0, w0,
        (
            lambda keep, got: scatter_first(*run_first_split(keep, got)),
            lambda *steps: scatter_second(*run_split_sum(*steps)),
            lambda *steps: deliver(run_dp_split(*steps), "dp"),
        ),
        (keep, swap(send, "section", 1)),
    )
    keep, send = run_attention_grads(*operands)
    steps = scatter_first(*run_first_split(keep, swap(send, "section", 1)))
    steps, out1_2 = tie(steps, swap(out1[2], "dp", 2))
    out1 = out1[0] + sum(p.astype(F32) for p in (out1[1], out1_2, out1[3]))
    steps, ffn0 = tie(scatter_second(*run_split_sum(*steps)), ffn0)
    blocks = deliver(run_dp_split(*steps), "dp")
    ffn0 = spread(run_ffn_total(ffn0), "ctx")
    blocks, ffn0 = tie(blocks, ffn0)
    keep, send = run_owner_sum(s1, blocks, later)
    unit = jnp.stack([keep, swap(send, "section", 1)])
    unit, ffn0, ffn1 = tie(unit, ffn0, ffn1)
    keep, send = run_ffn_pick(s1, ffn0, ffn1)
    gate, up, down = run_ffn_out(s1, c1, keep, swap(send, "section", 1))
    def own_layer(p0, p1):
        keep, send = by_layer(p0, p1)
        got = swap(send, "section", 1)
        return jnp.stack(by_layer(keep, got))

    units, gate, up, down = tie(spread(unit, "ctx"), gate, up, down)
    wo, gains, wk, wv, wq = run_attention_out(order_out, units)
    return (
        own_layer(out0, out1)[None, :, None],
        own_layer(in0, in1)[None, :, None],
        wq[None],
        wk.T[None],
        wv.T[None],
        wo[None],
        gains[None, :, 0],
        gate[None],
        up[None],
        down[None],
        gains[None, :, 1],
    )


def body(*args):
    sizes = [lax.axis_size(name) for name in ("section", "ctx", "dp")]
    return (body_fast if sizes == [2, 4, 4] else body_plain)(*args)


def solution(mesh):
    return jax.shard_map(
        body,
        mesh=mesh,
        in_specs=(
            P(None, "dp", "ctx", None),
            P(None, "dp", "ctx", None),
            P("section", "dp", None),
            P("section", "dp", None),
            P("section", "dp", None),
            P("section", "dp", None),
            P("section", "dp"),
            P("section", None, "dp"),
            P("section", None, "dp"),
            P("section", "dp", None),
            P("section", "dp"),
        ),
        out_specs=(
            P("section", None, "dp", "ctx", None),
            P("section", None, "dp", "ctx", None),
            P("section", "dp", None),
            P("section", "dp", None),
            P("section", "dp", None),
            P("section", "dp", None),
            P("section", "dp"),
            P("section", None, "dp"),
            P("section", None, "dp"),
            P("section", "dp", None),
            P("section", "dp"),
        ),
        check_vma=False,
    )
```
